32 devices in a mesh: fsdp: 8 (over y, x, core), tp: 4 (over z).
Axes of the slice: x: 2, y: 2, z: 4, core: 2. Of those that a mesh axis runs over, the one named last changes fastest.
Arguments:
- tokens: bfloat16 [32, 1024, 768], P('fsdp', 'tp'), may hold values from -6 to 6
- segment_ids: int32 [32, 1024], P('fsdp'), may hold values from 0 to 17, as said below
- live_mask: int32 [32, 1024], P('fsdp'), may hold values from 0 to 1, as said below
- query_weight: bfloat16 [768, 768], P('fsdp', 'tp'), may hold values from -0.3125 to 0.3125
- query_bias: bfloat16 [768], P('tp'), may hold values from -3 to 3
- key_weight: bfloat16 [768, 768], P('fsdp', 'tp'), may hold values from -0.3125 to 0.3125
- value_weight: bfloat16 [768, 768], P('fsdp', 'tp'), may hold values from -0.21875 to 0.21875
- value_bias: bfloat16 [768], P('tp'), may hold values from -3 to 3
- output_weight: bfloat16 [768, 768], P('tp', 'fsdp'), may hold values from -0.875 to 0.875
- output_bias: bfloat16 [768], replicated, may hold values from -3 to 3
- first_gain: bfloat16 [768], replicated, may hold values from 0.5 to 1.5
- first_shift: bfloat16 [768], replicated, may hold values from -3 to 3
- inner_weight: bfloat16 [768, 3072], P('fsdp', 'tp'), may hold values from -0.21875 to 0.21875
- inner_bias: bfloat16 [3072], P('tp'), may hold values from -3 to 3
- outer_weight: bfloat16 [3072, 768], P('tp', 'fsdp'), may hold values from -0.15625 to 0.15625
- outer_bias: bfloat16 [768], replicated, may hold values from -3 to 3
- second_gain: bfloat16 [768], replicated, may hold values from 0.5 to 1.5
- second_shift: bfloat16 [768], replicated, may hold values from -3 to 3
- out_grad: bfloat16 [32, 1024, 768], P('fsdp', 'tp'), may hold values from -6 to 6
Outputs:
- layer_out: bfloat16 [32, 1024, 768], P('fsdp', 'tp')
- tokens_grad: float32 [32, 1024, 768], P('fsdp', 'tp')
- query_weight_grad: float32 [768, 768], P('fsdp', 'tp')
- query_bias_grad: float32 [768], P('tp')
- key_weight_grad: float32 [768, 768], P('fsdp', 'tp')
- value_weight_grad: float32 [768, 768], P('fsdp', 'tp')
- value_bias_grad: float32 [768], P('tp')
- output_weight_grad: float32 [768, 768], P('tp', 'fsdp')
- output_bias_grad: float32 [768], replicated
- first_gain_grad: float32 [768], replicated
- first_shift_grad: float32 [768], replicated
- inner_weight_grad: float32 [768, 3072], P('fsdp', 'tp')
- inner_bias_grad: float32 [3072], P('tp')
- outer_weight_grad: float32 [3072, 768], P('tp', 'fsdp')
- outer_bias_grad: float32 [768], replicated
- second_gain_grad: float32 [768], replicated
- second_shift_grad: float32 [768], replicated
The draws below stay inside these ranges and needn't reach their ends.
Inputs may be any that keep to these rules, and one draw needn't show every extreme that they name: `segment_ids`: in each sequence the ids start at 0 and rise by one from document to document; every document but the last one of a sequence spans 60 to 800 positions. `live_mask`: in each sequence the ones come first: documents that end within the sequence are live, the positions of a last document cut off by the sequence's end are 0.
All inputs are finite; a program needn't handle non-finite values.
Results may differ from the reference program's by a relative error of at most 0.018.
The reference program's roundings to bfloat16 on the way count: a program that leaves them out, or rounds other values in their place, can miss the bound.
Values may be sent and summed in bfloat16 or wider, within the bound.
No kernel may reach another device: no remote copies, remote signals or barrier semaphores. Data moves between devices by JAX's collectives and lax.ppermute only.
A program may use at most 192 MiB of HBM per device.

```python
import jax
import jax.numpy as jnp
from jax import lax

D = 768
HEADS = 12
HDIM = 64
FF = 3072
LEN = 1024
DOC_MIN = 60
DOC_MAX = 800
NSEQ = 32


def packing(key):
    count = LEN // DOC_MIN + 1
    lengths = jax.random.randint(jax.random.fold_in(key, 11), (NSEQ, count), DOC_MIN, DOC_MAX + 1)
    first_row = (jnp.arange(NSEQ, dtype=jnp.int32) == 0)[:, None]
    lengths = jnp.where(first_row, jnp.int32(DOC_MIN), lengths).astype(jnp.int32)
    ends = jnp.cumsum(lengths, axis=1).astype(jnp.int32)
    places = jnp.arange(LEN, dtype=jnp.int32)
    segment = jnp.sum((places[None, :, None] >= ends[:, None, :]).astype(jnp.int32), axis=2).astype(jnp.int32)
    finish = jnp.take_along_axis(ends, segment, axis=1)
    live = (finish <= LEN).astype(jnp.int32)
    return (segment, live)


def draw_segment_ids(key, part):
    return packing(key)[0]


def draw_live_mask(key, part):
    return packing(key)[1]


def strengthened(array, rng, source, target, shards_of, factor):
    owner, partner = [(jnp.arange(array.shape[position]) // (array.shape[position] // shards_of)).reshape([-1 if axis == position else 1 for axis in range(array.ndim)]) for position in (source, target)]
    chosen = jax.random.permutation(rng, shards_of)[partner]
    strong = (owner == chosen) | (owner == (partner + shards_of // 2) % shards_of)
    return jnp.where(strong, factor * array, array)


def level_of(stream_key, extent, shards, least, top_value):
    factor_of = 1.0
    for position, parts in shards:
        steps = jax.random.uniform(jax.random.fold_in(jax.random.fold_in(stream_key, 6), position), (parts,), jnp.float32, least / len(shards), top_value / len(shards))
        factor_of = factor_of * jnp.repeat(jnp.exp(steps), extent[position] // parts).reshape((-1,) + (1,) * (len(extent) - 1 - position))
    return factor_of


def bell_draw(rng, dims, width, most, pieces=(), kind=jnp.bfloat16):
    factor_of = level_of(rng, dims, pieces, -0.22, 0.18) if pieces else 1.0
    values = jax.random.normal(rng, dims, jnp.float32) * width * factor_of
    return jnp.minimum(jnp.maximum(values, -most), most).astype(kind)


def heavy_noise(stream_key, extent, width, most, shards, heavy, kind=jnp.bfloat16):
    values = width * jax.random.normal(stream_key, extent, jnp.float32)
    if shards:
        values = values * level_of(stream_key, extent, shards, -0.22, 0.18)
    return jnp.clip(strengthened(values, jax.random.fold_in(stream_key, 3), *heavy), -most, most).astype(kind)


def setup_inputs(seed: int = 0) -> dict:
    key_list = jax.random.split(jax.random.key(seed), 20)
    return {
        "tokens": heavy_noise(key_list[0], (NSEQ, LEN, D), 1.0, 6.0, ((0, 8), (1, 4)), (0, 2, 8, 2.0)),
        "segment_ids": draw_segment_ids(jax.random.fold_in(key_list[19], 71), 0),
        "live_mask": draw_live_mask(jax.random.fold_in(key_list[19], 71), 0),
        "query_weight": bell_draw(key_list[3], (D, D), (D // 2) ** -0.5, 0.3125, ((0, 8), (1, 4))),
        "query_bias": bell_draw(key_list[4], (D,), 0.5, 3.0, ((0, 4),)),
        "key_weight": bell_draw(key_list[5], (D, D), (D // 2) ** -0.5, 0.3125, ((0, 8), (1, 4))),
        "value_weight": bell_draw(key_list[6], (D, D), D ** -0.5, 0.21875, ((0, 8), (1, 4))),
        "value_bias": bell_draw(key_list[7], (D,), 0.5, 3.0, ((0, 4),)),
        "output_weight": bell_draw(key_list[8], (D, D), (D // 16) ** -0.5, 0.875, ((0, 4), (1, 8))),
        "output_bias": bell_draw(key_list[9], (D,), 0.5, 3.0),
        "first_gain": jnp.clip(1.0 + 0.1 * jax.random.normal(key_list[10], (D,), jnp.float32), 0.5, 1.5).astype(jnp.bfloat16),
        "first_shift": bell_draw(key_list[11], (D,), 0.5, 3.0),
        "inner_weight": bell_draw(key_list[12], (D, FF), D ** -0.5, 0.21875, ((0, 8), (1, 4))),
        "inner_bias": bell_draw(key_list[13], (FF,), 0.5, 3.0, ((0, 4),)),
        "outer_weight": bell_draw(key_list[14], (FF, D), (FF // 2) ** -0.5, 0.15625, ((0, 4), (1, 8))),
        "outer_bias": bell_draw(key_list[15], (D,), 0.5, 3.0),
        "second_gain": jnp.clip(1.0 + 0.1 * jax.random.normal(key_list[16], (D,), jnp.float32), 0.5, 1.5).astype(jnp.bfloat16),
        "second_shift": bell_draw(key_list[17], (D,), 0.5, 3.0),
        "out_grad": heavy_noise(key_list[18], (NSEQ, LEN, D), 1.0, 6.0, ((0, 8), (1, 4)), (0, 2, 8, 2.0)),
    }


TOP_PRECISION = lax.Precision.HIGHEST
EPSILON = 1e-12
MASKED = -1000000000.0

@jax.custom_vjp
def low(v):
    return lax.optimization_barrier(v.astype(jnp.bfloat16)).astype(jnp.float32)

@jax.custom_vjp
def low_back(v):
    return v

def low_keep(v):
    return (low(v), None)

def low_pass(kept, grad):
    return (grad,)

def back_keep(v):
    return (v, None)

def back_low(kept, grad):
    return (low(grad),)
low.defvjp(low_keep, low_pass)
low_back.defvjp(back_keep, back_low)

def normalize(token_rows, gain_row, shift_row):
    centred = token_rows - lax.optimization_barrier(jnp.mean(token_rows, axis=-1, keepdims=True))
    normed = centred * lax.rsqrt(lax.optimization_barrier(jnp.mean(centred * centred, axis=-1, keepdims=True)) + EPSILON)
    return normed * gain_row + shift_row

def visible(segment, live_row):
    length = segment.shape[0]
    places = lax.broadcasted_iota(jnp.int32, (length, length), 0)
    others = lax.broadcasted_iota(jnp.int32, (length, length), 1)
    same_doc = segment[:, None] == segment[None, :]
    return same_doc & ((live_row[None, :] == 1) | (places == others))

def attend(bundle):
    queries, keys_all, values, segment, live_row = bundle
    scores = jnp.einsum('qhe,khe->hqk', queries, keys_all, precision=TOP_PRECISION) * HDIM ** (-0.5)
    scores = low_back(jnp.where(visible(segment, live_row)[None], scores, MASKED))
    probs = low(jax.nn.softmax(scores, axis=-1))
    return jnp.einsum('hqk,khe->qhe', probs, values, precision=TOP_PRECISION)

def project(token_rows, weight_matrix):
    return jnp.einsum('mqp,pi->mqi', token_rows, weight_matrix, precision=TOP_PRECISION)

def layer(segment_ids, live_mask, tokens, query_weight, query_bias, key_weight, value_weight, value_bias, output_weight, output_bias, first_gain, first_shift, inner_weight, inner_bias, outer_weight, outer_bias, second_gain, second_shift):
    head_shape = (NSEQ, LEN, HEADS, HDIM)
    queries = low(low_back(project(tokens, query_weight) + query_bias)).reshape(head_shape)
    keys_all = low(low_back(project(tokens, key_weight))).reshape(head_shape)
    values = low(low_back(project(tokens, value_weight) + value_bias)).reshape(head_shape)
    context = lax.map(jax.checkpoint(attend), (queries, keys_all, values, segment_ids, live_mask))
    context = low(low_back(context.reshape(NSEQ, LEN, D)))
    mixed = low_back(project(context, output_weight)) + output_bias
    first_rows = normalize(tokens + mixed, first_gain, first_shift)
    first_low = low(first_rows)
    preactivation = low_back(project(first_low, inner_weight) + inner_bias)
    activation_rows = low(jax.nn.gelu(preactivation, approximate=False))
    branch = low_back(project(activation_rows, outer_weight)) + outer_bias
    return normalize(first_rows + branch, second_gain, second_shift)

def reference(tokens, segment_ids, live_mask, query_weight, query_bias, key_weight, value_weight, value_bias, output_weight, output_bias, first_gain, first_shift, inner_weight, inner_bias, outer_weight, outer_bias, second_gain, second_shift, out_grad):
    params = (tokens, query_weight, query_bias, key_weight, value_weight, value_bias, output_weight, output_bias, first_gain, first_shift, inner_weight, inner_bias, outer_weight, outer_bias, second_gain, second_shift)
    params = tuple((entry.astype(jnp.float32) for entry in params))

    def forward(*floats):
        return layer(segment_ids, live_mask, *floats)
    result, backward = jax.vjp(forward, *params)
    grads = backward(out_grad.astype(jnp.float32))
    return (result.astype(jnp.bfloat16), grads[0], grads[1], grads[2], grads[3], grads[4], grads[5], grads[6], grads[7], grads[8], grads[9], grads[10], grads[11], grads[12], grads[13], grads[14], grads[15])
```

```python
import functools

import jax
import jax.numpy as jnp
from jax import lax
from jax.experimental import pallas as pl
from jax.sharding import PartitionSpec as P

HDIM = 64
EPSILON = 1e-12
MASKED = -1000000000.0
PAIR = 2 * HDIM
BLOCK = 256
LOW = jnp.bfloat16
WIDE = jnp.float32
BY_LAST = (((1,), (1,)), ((), ()))
BY_ROWS = (((1,), (0,)), ((), ()))
BY_FIRST = (((0,), (0,)), ((), ()))


def dot(left, right, dims):
    return lax.dot_general(left, right, dims, preferred_element_type=WIDE)


def halves(pair):
    lane = lax.broadcasted_iota(jnp.int32, (1, PAIR), 1)
    zero = jnp.zeros((), pair.dtype)
    return jnp.where(lane < HDIM, pair, zero), jnp.where(lane < HDIM, zero, pair)


def attend_kernel(q_ref, k_ref, v_ref, row_ref, col_ref, context_ref, logsum_ref, *, scaling):
    keys_all = k_ref[0]
    turned = [half.T for half in halves(v_ref[0])]
    key_ids = col_ref[0]
    for start in range(0, q_ref.shape[1], BLOCK):
        part = slice(start, start + BLOCK)
        seen = key_ids == row_ref[0, :, part]
        total = None
        for head, queries in enumerate(halves(q_ref[0, part, :] * scaling)):
            scores = jnp.where(seen, dot(keys_all, queries, BY_LAST), MASKED)
            highest = jnp.max(scores, axis=0, keepdims=True)
            weights = jnp.exp(scores - highest)
            sums = jnp.sum(weights, axis=0, keepdims=True)
            probs = (weights * (1.0 / sums)).astype(LOW)
            logsum_ref[0, 0, head : head + 1, part] = highest + jnp.log(sums)
            piece = dot(turned[head], probs, BY_ROWS)
            total = piece if total is None else total + piece
        context_ref[0, part, :] = total.T.astype(LOW)


def attend_back_kernel(
    q_ref, k_ref, v_ref, g_ref, logsum_ref, row_ref, col_ref, dq_ref, dk_ref, dv_ref, *, scaling
):
    keys_all = k_ref[0]
    values = v_ref[0]
    turned = [half.T for half in halves(keys_all)]
    key_ids = col_ref[0]
    length = q_ref.shape[1]
    key_grad = jnp.zeros((length, PAIR), WIDE)
    value_grad = jnp.zeros((length, PAIR), WIDE)
    for start in range(0, length, BLOCK):
        part = slice(start, start + BLOCK)
        seen = key_ids == row_ref[0, :, part]
        total = None
        queries_of = halves(q_ref[0, part, :] * scaling)
        grads_of = halves(g_ref[0, part, :])
        for head in range(2):
            queries, grads = queries_of[head], grads_of[head]
            scores = jnp.where(seen, dot(keys_all, queries, BY_LAST), MASKED)
            probs = jnp.exp(scores - logsum_ref[0, 0, head : head + 1, part])
            grad_probs = dot(values, grads, BY_LAST)
            value_grad = value_grad + dot(probs.astype(LOW), grads, BY_ROWS)
            level = jnp.sum(probs * grad_probs, axis=0, keepdims=True)
            grad_scores = (probs * (grad_probs - level)).astype(LOW)
            key_grad = key_grad + dot(grad_scores, queries, BY_ROWS)
            piece = dot(turned[head], grad_scores, BY_ROWS)
            total = piece if total is None else total + piece
        dq_ref[0, part, :] = (total.T * HDIM ** (-0.5)).astype(LOW)
    dk_ref[0] = key_grad.astype(LOW)
    dv_ref[0] = value_grad.astype(LOW)


def attention_specs(length):
    return (
        pl.BlockSpec((1, length, PAIR), lambda s, p: (s, 0, p)),
        pl.BlockSpec((1, 1, length), lambda s, p: (s, 0, 0)),
        pl.BlockSpec((1, length, 1), lambda s, p: (s, 0, 0)),
        pl.BlockSpec((1, 1, 2, length), lambda s, p: (s, p, 0, 0)),
    )


def attend(queries, keys_all, values, ids):
    count, length, width = queries.shape
    rows, as_row, as_col, sums = attention_specs(length)
    scaling = HDIM ** (-0.5)
    return pl.pallas_call(
        functools.partial(attend_kernel, scaling=scaling),
        grid=(count, width // PAIR),
        in_specs=[rows, rows, rows, as_row, as_col],
        out_specs=[rows, sums],
        out_shape=[
            jax.ShapeDtypeStruct(queries.shape, LOW),
            jax.ShapeDtypeStruct((count, width // PAIR, 2, length), WIDE),
        ],
        name="attend",
    )(queries, keys_all, values, ids[:, None, :], ids[:, :, None])


def attend_back(queries, keys_all, values, grad_context, logsum, ids):
    count, length, width = queries.shape
    rows, as_row, as_col, sums = attention_specs(length)
    scaling = HDIM ** (-0.5)
    return pl.pallas_call(
        functools.partial(attend_back_kernel, scaling=scaling),
        grid=(count, width // PAIR),
        in_specs=[rows, rows, rows, rows, sums, as_row, as_col],
        out_specs=[rows, rows, rows],
        out_shape=[jax.ShapeDtypeStruct(queries.shape, LOW)] * 3,
        name="attend_back",
    )(queries, keys_all, values, grad_context, logsum, ids[:, None, :], ids[:, :, None])


def swap_over(axis, blocks):
    members = blocks.shape[0]
    rank = lax.axis_index(axis)
    result = lax.dynamic_update_slice_in_dim(
        jnp.zeros_like(blocks), lax.dynamic_slice_in_dim(blocks, rank, 1, 0), rank, 0
    )
    for step in range(1, members):
        moved = lax.ppermute(
            lax.dynamic_slice_in_dim(blocks, (rank + step) % members, 1, 0),
            axis,
            [(i, (i + step) % members) for i in range(members)],
        )
        result = lax.dynamic_update_slice_in_dim(result, moved, (rank - step) % members, 0)
    return result


def gather_over(axis, members, block):
    rank = lax.axis_index(axis)
    result = lax.dynamic_update_slice_in_dim(
        jnp.zeros((members,) + block.shape, block.dtype), block[None], rank, 0
    )
    for step in range(1, members):
        moved = lax.ppermute(block, axis, [(i, (i + step) % members) for i in range(members)])
        result = lax.dynamic_update_slice_in_dim(result, moved[None], (rank - step) % members, 0)
    return result


def flip(axis, members, bit, block):
    return lax.ppermute(block, axis, [(i, i ^ bit) for i in range(members)])


def paths(members):
    far = [1 << i for i in range(1, members.bit_length() - 1)]
    return (far + [1], far[::-1] + [1])


def gather_rows(axis, members, block):
    if members != 8:
        return lax.all_gather(block, axis, axis=0, tiled=True)
    rank = lax.axis_index(axis)
    rows, cols = block.shape
    half = cols // 2
    sides = []
    for order, piece in zip(paths(members), (block[:, :half], block[:, half:])):
        held = {0: piece}
        for bit in order:
            for mask in list(held):
                held[mask | bit] = flip(axis, members, bit, held[mask])
        side = jnp.zeros((members, rows, half), block.dtype)
        for mask in sorted(held):
            side = lax.dynamic_update_slice_in_dim(side, held[mask][None], rank ^ mask, 0)
        sides.append(side.reshape(members * rows, half))
    return jnp.concatenate(sides, axis=1)


def scatter_rows(axis, members, grad):
    if members != 8:
        return lax.psum_scatter(grad, axis, scatter_dimension=0, tiled=True)
    rank = lax.axis_index(axis)
    total_rows, cols = grad.shape
    rows = total_rows // members
    half = cols // 2
    sides = []
    for order, first in zip(paths(members), (0, half)):
        blocks = grad[:, first : first + half].reshape(members, rows, half)
        held = {mask: None for mask in range(members)}

        def own(mask):
            if held[mask] is None:
                return lax.dynamic_slice_in_dim(blocks, rank ^ mask, 1, 0)[0]
            return held[mask]

        for bit in order[::-1]:
            for mask in [m for m in held if not m & bit]:
                moved = flip(axis, members, bit, own(mask | bit))
                held[mask] = (own(mask).astype(WIDE) + moved.astype(WIDE)).astype(LOW)
            held = {m: v for m, v in held.items() if not m & bit}
        sides.append(held[0])
    return jnp.concatenate(sides, axis=1)


def total_over_all(vector, fsdp, tp):
    pieces = gather_over("tp", tp, vector)
    result = pieces[0]
    for i in range(1, tp):
        result = result + pieces[i]
    bit = 1
    if fsdp & (fsdp - 1):
        return lax.psum(result, "fsdp")
    while bit < fsdp:
        result = result + flip("fsdp", fsdp, bit, result)
        bit *= 2
    return result


def normalize(token_rows):
    centred = token_rows - jnp.mean(token_rows, axis=-1, keepdims=True)
    scaling = lax.rsqrt(jnp.mean(centred * centred, axis=-1, keepdims=True) + EPSILON)
    return centred * scaling, scaling


def normalize_back(grad_rows, normed, scaling, gain_row):
    grad_normed = grad_rows * gain_row
    adjusted = grad_normed - jnp.mean(grad_normed, axis=-1, keepdims=True)
    adjusted = adjusted - normed * jnp.mean(grad_normed * normed, axis=-1, keepdims=True)
    return scaling * adjusted, jnp.sum(grad_rows * normed, axis=0), jnp.sum(grad_rows, axis=0)


def on_device(
    fsdp,
    tp,
    tokens,
    segment_ids,
    live_mask,
    query_weight,
    query_bias,
    key_weight,
    value_weight,
    value_bias,
    output_weight,
    output_bias,
    first_gain,
    first_shift,
    inner_weight,
    inner_bias,
    outer_weight,
    outer_bias,
    second_gain,
    second_shift,
    out_grad,
):
    sequences, places, width = tokens.shape
    count = sequences // tp
    length = places * tp
    rank = lax.axis_index("tp")
    head_cols = query_weight.shape[1]
    unit_cols = inner_weight.shape[1]

    def whole_rows(array):
        blocks = swap_over("tp", array.reshape(tp, count, places, width))
        return blocks.transpose(1, 0, 2, 3).reshape(count * length, width)

    def own_places(array):
        blocks = array.reshape(count, tp, places, width).transpose(1, 0, 2, 3)
        return swap_over("tp", blocks).reshape(sequences, places, width)

    def whole_weight(block):
        return gather_rows("fsdp", fsdp, columns(gather_over("tp", tp, block)))

    def columns(blocks):
        members, rows, cols = blocks.shape
        return blocks.transpose(1, 0, 2).reshape(rows, members * cols)

    def own_share(grad):
        share = scatter_rows("fsdp", fsdp, grad.astype(LOW))
        rows, cols = share.shape
        blocks = share.reshape(rows, tp, cols // tp).transpose(1, 0, 2)
        return jnp.sum(swap_over("tp", blocks).astype(WIDE), axis=0)

    query_full = whole_weight(query_weight)
    key_full = whole_weight(key_weight)
    value_full = whole_weight(value_weight)
    rows = whole_rows(tokens)
    output_turned = whole_weight(output_weight.T)
    inner_full = whole_weight(inner_weight)
    outer_turned = whole_weight(outer_weight.T)
    biases = gather_over(
        "tp", tp, jnp.concatenate([query_bias, value_bias, inner_bias])
    ).astype(WIDE)
    query_bias_full = biases[:, :head_cols].reshape(-1)
    value_bias_full = biases[:, head_cols : 2 * head_cols].reshape(-1)
    inner_bias_full = biases[:, 2 * head_cols :].reshape(-1)

    first = rank * count
    segment = lax.dynamic_slice_in_dim(segment_ids, first, count, 0)
    live = lax.dynamic_slice_in_dim(live_mask, first, count, 0)
    spots = lax.broadcasted_iota(jnp.int32, segment.shape, 1)
    ids = jnp.where(live == 1, segment, length + spots)

    shape = (count, length, width)
    queries = (dot(rows, query_full, BY_ROWS) + query_bias_full).astype(LOW).reshape(shape)
    keys_all = dot(rows, key_full, BY_ROWS).astype(LOW).reshape(shape)
    values = (dot(rows, value_full, BY_ROWS) + value_bias_full).astype(LOW).reshape(shape)
    context, logsum = attend(queries, keys_all, values, ids)
    context = context.reshape(count * length, width)
    mixed = dot(context, output_turned, BY_LAST) + output_bias.astype(WIDE)
    first_normed, first_scaling = normalize(rows.astype(WIDE) + mixed)
    first_rows = first_normed * first_gain.astype(WIDE) + first_shift.astype(WIDE)
    first_low = first_rows.astype(LOW)
    preactivation = dot(first_low, inner_full, BY_ROWS) + inner_bias_full
    cumulative = 0.5 * (1.0 + lax.erf(preactivation * 0.7071067811865476))
    activation_rows = (preactivation * cumulative).astype(LOW)
    density = jnp.exp(-0.5 * preactivation * preactivation) * 0.3989422804014327
    slope = cumulative + preactivation * density
    branch = dot(activation_rows, outer_turned, BY_LAST)
    second_normed, second_scaling = normalize(first_rows + branch + outer_bias.astype(WIDE))
    second_rows = second_normed * second_gain.astype(WIDE) + second_shift.astype(WIDE)
    layer_out = own_places(second_rows.astype(LOW))

    grad_out = whole_rows(out_grad).astype(WIDE)
    grad_second, second_gain_grad, second_shift_grad = normalize_back(
        grad_out, second_normed, second_scaling, second_gain.astype(WIDE)
    )
    outer_bias_grad = jnp.sum(grad_second, axis=0)
    grad_branch = grad_second.astype(LOW)
    outer_share = own_share(dot(grad_branch, activation_rows, BY_FIRST))
    grad_activ = dot(grad_branch, outer_turned, BY_ROWS)
    grad_pre = (grad_activ * slope).astype(LOW)
    inner_bias_grad = jnp.sum(grad_pre.astype(WIDE), axis=0)
    inner_share = own_share(dot(first_low, grad_pre, BY_FIRST))
    grad_first = grad_second + dot(grad_pre, inner_full, BY_LAST)
    grad_mixed, first_gain_grad, first_shift_grad = normalize_back(
        grad_first, first_normed, first_scaling, first_gain.astype(WIDE)
    )
    output_bias_grad = jnp.sum(grad_mixed, axis=0)
    grad_mixed_low = grad_mixed.astype(LOW)
    output_share = own_share(dot(grad_mixed_low, context, BY_FIRST))
    grad_context = dot(grad_mixed_low, output_turned, BY_ROWS).astype(LOW).reshape(shape)
    query_rows_grad, key_rows_grad, value_rows_grad = (
        array.reshape(count * length, width)
        for array in attend_back(queries, keys_all, values, grad_context, logsum, ids)
    )
    query_bias_grad = jnp.sum(query_rows_grad.astype(WIDE), axis=0)
    value_bias_grad = jnp.sum(value_rows_grad.astype(WIDE), axis=0)
    tokens_grad = (
        grad_mixed
        + dot(query_rows_grad, query_full, BY_LAST)
        + dot(key_rows_grad, key_full, BY_LAST)
        + dot(value_rows_grad, value_full, BY_LAST)
    )
    tokens_grad = own_places(tokens_grad.astype(LOW)).astype(WIDE)
    query_share = own_share(dot(rows, query_rows_grad, BY_FIRST))
    key_share = own_share(dot(rows, key_rows_grad, BY_FIRST))
    value_share = own_share(dot(rows, value_rows_grad, BY_FIRST))

    early = total_over_all(
        jnp.concatenate(
            [
                output_bias_grad,
                first_gain_grad,
                first_shift_grad,
                outer_bias_grad,
                second_gain_grad,
                second_shift_grad,
                inner_bias_grad,
            ]
        ),
        fsdp,
        tp,
    )
    late = total_over_all(jnp.concatenate([query_bias_grad, value_bias_grad]), fsdp, tp)
    rowwise = [early[i * width : (i + 1) * width] for i in range(6)]
    inner_bias_total = lax.dynamic_slice_in_dim(early, 6 * width + rank * unit_cols, unit_cols)
    query_bias_total = lax.dynamic_slice_in_dim(late, rank * head_cols, head_cols)
    value_bias_total = lax.dynamic_slice_in_dim(late, width + rank * head_cols, head_cols)
    return (
        layer_out,
        tokens_grad,
        query_share,
        query_bias_total,
        key_share,
        value_share,
        value_bias_total,
        output_share.T,
        rowwise[0],
        rowwise[1],
        rowwise[2],
        inner_share,
        inner_bias_total,
        outer_share.T,
        rowwise[3],
        rowwise[4],
        rowwise[5],
    )


def solution(mesh):
    split = P("fsdp", "tp", None)
    across, turned = P("fsdp", "tp"), P("tp", "fsdp")
    seqs, units, copied = P("fsdp", None), P("tp"), P()
    return jax.shard_map(
        functools.partial(on_device, mesh.shape["fsdp"], mesh.shape["tp"]),
        mesh=mesh,
        in_specs=(
            split,
            seqs,
            seqs,
            across,
            units,
            across,
            across,
            units,
            turned,
            copied,
            copied,
            copied,
            across,
            units,
            turned,
            copied,
            copied,
            copied,
            split,
        ),
        out_specs=(
            split,
            split,
            across,
            units,
            across,
            across,
            units,
            turned,
            copied,
            copied,
            copied,
            across,
            units,
            turned,
            copied,
            copied,
            copied,
        ),
        check_vma=False,
    )
```

```python
import functools

import jax
import jax.numpy as jnp
from jax import lax
from jax.experimental import pallas as pl
from jax.sharding import PartitionSpec as P

HDIM = 64
EPSILON = 1e-12
MASKED = -1000000000.0
PAIR = 2 * HDIM
BLOCK = 256
LOW = jnp.bfloat16
WIDE = jnp.float32
BY_LAST = (((1,), (1,)), ((), ()))
BY_ROWS = (((1,), (0,)), ((), ()))
BY_FIRST = (((0,), (0,)), ((), ()))


def dot(left, right, dims):
    return lax.dot_general(left, right, dims, preferred_element_type=WIDE)


def halves(pair):
    lane = lax.broadcasted_iota(jnp.int32, (1, PAIR), 1)
    zero = jnp.zeros((), pair.dtype)
    return jnp.where(lane < HDIM, pair, zero), jnp.where(lane < HDIM, zero, pair)


def attend_kernel(q_ref, k_ref, v_ref, row_ref, col_ref, context_ref, logsum_ref, *, scaling):
    keys_all = k_ref[0]
    turned = [half.T for half in halves(v_ref[0])]
    key_ids = col_ref[0]
    for start in range(0, q_ref.shape[1], BLOCK):
        part = slice(start, start + BLOCK)
        seen = key_ids == row_ref[0, :, part]
        total = None
        for head, queries in enumerate(halves(q_ref[0, part, :] * scaling)):
            scores = jnp.where(seen, dot(keys_all, queries, BY_LAST), MASKED)
            highest = jnp.max(scores, axis=0, keepdims=True)
            weights = jnp.exp(scores - highest)
            sums = jnp.sum(weights, axis=0, keepdims=True)
            probs = (weights * (1.0 / sums)).astype(LOW)
            logsum_ref[0, 0, head : head + 1, part] = highest + jnp.log(sums)
            piece = dot(turned[head], probs, BY_ROWS)
            total = piece if total is None else total + piece
        context_ref[0, part, :] = total.T.astype(LOW)


def attend_back_kernel(
    q_ref, k_ref, v_ref, g_ref, logsum_ref, row_ref, col_ref, dq_ref, dk_ref, dv_ref, *, scaling
):
    keys_all = k_ref[0]
    values = v_ref[0]
    turned = [half.T for half in halves(keys_all)]
    key_ids = col_ref[0]
    length = q_ref.shape[1]
    key_grad = jnp.zeros((length, PAIR), WIDE)
    value_grad = jnp.zeros((length, PAIR), WIDE)
    for start in range(0, length, BLOCK):
        part = slice(start, start + BLOCK)
        seen = key_ids == row_ref[0, :, part]
        total = None
        queries_of = halves(q_ref[0, part, :] * scaling)
        grads_of = halves(g_ref[0, part, :])
        for head in range(2):
            queries, grads = queries_of[head], grads_of[head]
            scores = jnp.where(seen, dot(keys_all, queries, BY_LAST), MASKED)
            probs = jnp.exp(scores - logsum_ref[0, 0, head : head + 1, part])
            grad_probs = dot(values, grads, BY_LAST)
            value_grad = value_grad + dot(probs.astype(LOW), grads, BY_ROWS)
            level = jnp.sum(probs * grad_probs, axis=0, keepdims=True)
            grad_scores = (probs * (grad_probs - level)).astype(LOW)
            key_grad = key_grad + dot(grad_scores, queries, BY_ROWS)
            piece = dot(turned[head], grad_scores, BY_ROWS)
            total = piece if total is None else total + piece
        dq_ref[0, part, :] = (total.T * HDIM ** (-0.5)).astype(LOW)
    dk_ref[0] = key_grad.astype(LOW)
    dv_ref[0] = value_grad.astype(LOW)


def attention_specs(length):
    return (
        pl.BlockSpec((1, length, PAIR), lambda s, p: (s, 0, p)),
        pl.BlockSpec((1, 1, length), lambda s, p: (s, 0, 0)),
        pl.BlockSpec((1, length, 1), lambda s, p: (s, 0, 0)),
        pl.BlockSpec((1, 1, 2, length), lambda s, p: (s, p, 0, 0)),
    )


def attend(queries, keys_all, values, ids):
    count, length, width = queries.shape
    rows, as_row, as_col, sums = attention_specs(length)
    scaling = HDIM ** (-0.5)
    return pl.pallas_call(
        functools.partial(attend_kernel, scaling=scaling),
        grid=(count, width // PAIR),
        in_specs=[rows, rows, rows, as_row, as_col],
        out_specs=[rows, sums],
        out_shape=[
            jax.ShapeDtypeStruct(queries.shape, LOW),
            jax.ShapeDtypeStruct((count, width // PAIR, 2, length), WIDE),
        ],
        name="attend",
    )(queries, keys_all, values, ids[:, None, :], ids[:, :, None])


def attend_back(queries, keys_all, values, grad_context, logsum, ids):
    count, length, width = queries.shape
    rows, as_row, as_col, sums = attention_specs(length)
    scaling = HDIM ** (-0.5)
    return pl.pallas_call(
        functools.partial(attend_back_kernel, scaling=scaling),
        grid=(count, width // PAIR),
        in_specs=[rows, rows, rows, rows, sums, as_row, as_col],
        out_specs=[rows, rows, rows],
        out_shape=[jax.ShapeDtypeStruct(queries.shape, LOW)] * 3,
        name="attend_back",
    )(queries, keys_all, values, grad_context, logsum, ids[:, None, :], ids[:, :, None])


def dealt(axis, members, blocks):
    rank = lax.axis_index(axis)
    parts = []
    for step in range(members):
        block = lax.dynamic_slice_in_dim(blocks, (rank + step) % members, 1, 0)[0]
        pairs = [(i, (i + step) % members) for i in range(members)]
        parts.append(lax.ppermute(block, axis, pairs) if step else block)
    return parts


def returned(axis, members, parts):
    rank = lax.axis_index(axis)
    result = None
    for step in range(members):
        pairs = [(i, (i - step) % members) for i in range(members)]
        block = (lax.ppermute(parts[step], axis, pairs) if step else parts[step])[None]
        if result is None:
            result = jnp.broadcast_to(block, (members,) + block.shape[1:])
        else:
            result = lax.dynamic_update_slice_in_dim(result, block, (rank + step) % members, 0)
    return result


def flip(axis, members, bit, block):
    return lax.ppermute(block, axis, [(i, i ^ bit) for i in range(members)])


def joined(axis, members, bit, block, place):
    mine = lax.axis_index(axis) // bit % 2
    other = flip(axis, members, bit, block)
    shape = block.shape[:place] + (2,) + block.shape[place:]
    spot = lax.broadcasted_iota(jnp.int32, shape, place)
    return jnp.where(spot == mine, jnp.expand_dims(block, place), jnp.expand_dims(other, place))


def halved(axis, members, bit, array, place):
    mine = lax.axis_index(axis) // bit % 2
    theirs = lax.squeeze(lax.dynamic_slice_in_dim(array, 1 - mine, 1, place), (place,))
    kept = lax.squeeze(lax.dynamic_slice_in_dim(array, mine, 1, place), (place,))
    return kept.astype(WIDE) + flip(axis, members, bit, theirs).astype(WIDE)


def gather_tp(members, block):
    if members != 4:
        return lax.all_gather(block, "tp", axis=0)
    shape = block.shape
    block = joined("tp", members, 1, block, 0)
    block = joined("tp", members, 2, block, 0)
    return block.reshape((members,) + shape)


def gather_rows(members, block):
    if members != 8:
        return lax.all_gather(block, "fsdp", axis=0, tiled=True)
    rows, cols = block.shape
    first = joined("fsdp", members, 2, block[:, : cols // 2], 0)
    second = joined("fsdp", members, 4, block[:, cols // 2 :], 0)
    first = joined("fsdp", members, 4, first, 0)
    second = joined("fsdp", members, 2, second, 1)
    both = jnp.concatenate([first, second], axis=3)
    return joined("fsdp", members, 1, both, 2).reshape(members * rows, cols)


def scatter_rows(members, grad):
    if members != 8:
        return lax.psum_scatter(grad, "fsdp", scatter_dimension=0, tiled=True).astype(WIDE)
    total_rows, cols = grad.shape
    rows = total_rows // members
    grad = halved("fsdp", members, 1, grad.reshape(2, 2, 2, rows, cols), 2).astype(LOW)
    first = halved("fsdp", members, 4, grad[..., : cols // 2], 0).astype(LOW)
    second = halved("fsdp", members, 2, grad[..., cols // 2 :], 1).astype(LOW)
    first = halved("fsdp", members, 2, first, 0)
    second = halved("fsdp", members, 4, second, 0)
    return jnp.concatenate([first, second], axis=1)


def scatter_tp(members, blocks):
    if members != 4:
        return lax.psum_scatter(blocks.astype(LOW), "tp", scatter_dimension=0).astype(WIDE)
    blocks = blocks.astype(LOW).reshape((2, 2) + blocks.shape[1:])
    return halved("tp", members, 1, halved("tp", members, 2, blocks, 0).astype(LOW), 0)


def total_over_all(fsdp, tp, vector):
    for axis, members in (("fsdp", fsdp), ("tp", tp)):
        bit = 1
        while bit < members:
            vector = vector + flip(axis, members, bit, vector)
            bit *= 2
    return vector


def normalize(token_rows):
    centred = token_rows - jnp.mean(token_rows, axis=-1, keepdims=True)
    scaling = lax.rsqrt(jnp.mean(centred * centred, axis=-1, keepdims=True) + EPSILON)
    return centred * scaling, scaling


def normalize_back(grad_rows, normed, scaling, gain_row):
    grad_normed = grad_rows * gain_row
    adjusted = grad_normed - jnp.mean(grad_normed, axis=-1, keepdims=True)
    adjusted = adjusted - normed * jnp.mean(grad_normed * normed, axis=-1, keepdims=True)
    return scaling * adjusted, jnp.sum(grad_rows * normed, axis=0), jnp.sum(grad_rows, axis=0)


def on_device(
    fsdp,
    tp,
    tokens,
    segment_ids,
    live_mask,
    query_weight,
    query_bias,
    key_weight,
    value_weight,
    value_bias,
    output_weight,
    output_bias,
    first_gain,
    first_shift,
    inner_weight,
    inner_bias,
    outer_weight,
    outer_bias,
    second_gain,
    second_shift,
    out_grad,
):
    sequences, places, width = tokens.shape
    count = sequences // tp
    length = places * tp
    rank = lax.axis_index("tp")
    head_cols = query_weight.shape[1]
    unit_cols = inner_weight.shape[1]
    shard_rows = query_weight.shape[0]

    def whole_rows(array):
        parts = dealt("tp", tp, array.reshape(tp, count, places, width))
        return jnp.concatenate(parts, axis=1).reshape(count * length, width)

    def own_places(array):
        parts = array.reshape(count, tp, places, width)
        parts = returned("tp", tp, [parts[:, step] for step in range(tp)])
        return parts.reshape(sequences, places, width)

    def columns(blocks):
        members, rows, cols = blocks.shape
        return blocks.transpose(1, 0, 2).reshape(rows, members * cols)

    def own_share(grad, widths):
        share = scatter_rows(fsdp, grad)
        rows, first, blocks = share.shape[0], 0, []
        for cols in widths:
            piece = share[:, first : first + cols].reshape(rows, tp, cols // tp)
            blocks.append(piece.transpose(1, 0, 2))
            first += cols
        share, first, pieces = scatter_tp(tp, jnp.concatenate(blocks, axis=2)), 0, []
        for cols in widths:
            pieces.append(share[:, first : first + cols // tp])
            first += cols // tp
        return pieces

    biases = jnp.concatenate([query_bias, value_bias, inner_bias]).reshape(-1, 3 * head_cols)
    heads = jnp.concatenate(
        [jnp.concatenate([query_weight, key_weight, value_weight], axis=1), biases], axis=0
    )
    heads = gather_tp(tp, heads)
    biases = heads[:, shard_rows:].reshape(tp, -1).astype(WIDE)
    query_bias_full = biases[:, :head_cols].reshape(-1)
    value_bias_full = biases[:, head_cols : 2 * head_cols].reshape(-1)
    inner_bias_full = biases[:, 2 * head_cols :].reshape(-1)
    heads = heads[:, :shard_rows].reshape(tp, shard_rows, 3, head_cols).transpose(1, 2, 0, 3)
    heads = gather_rows(fsdp, heads.reshape(shard_rows, 3 * width))
    query_full, key_full, value_full = (heads[:, i * width : (i + 1) * width] for i in range(3))
    rows = whole_rows(tokens)
    rest = jnp.concatenate([inner_weight, outer_weight.T, output_weight.T], axis=1)
    rest = lax.all_gather(rest, ("tp", "fsdp"), axis=0, tiled=True).reshape(tp, width, -1)
    inner_full = columns(rest[:, :, :unit_cols])
    outer_turned = columns(rest[:, :, unit_cols : 2 * unit_cols])
    output_turned = columns(rest[:, :, 2 * unit_cols :])

    first = rank * count
    segment = lax.dynamic_slice_in_dim(segment_ids, first, count, 0)
    live = lax.dynamic_slice_in_dim(live_mask, first, count, 0)
    spots = lax.broadcasted_iota(jnp.int32, segment.shape, 1)
    ids = jnp.where(live == 1, segment, length + spots).reshape(count, tp, places)
    ids = [lax.dynamic_slice_in_dim(ids, (rank - step) % tp, 1, 1) for step in range(tp)]
    ids = jnp.concatenate(ids, axis=1).reshape(count, length)

    shape = (count, length, width)
    queries = (dot(rows, query_full, BY_ROWS) + query_bias_full).astype(LOW).reshape(shape)
    keys_all = dot(rows, key_full, BY_ROWS).astype(LOW).reshape(shape)
    values = (dot(rows, value_full, BY_ROWS) + value_bias_full).astype(LOW).reshape(shape)
    context, logsum = attend(queries, keys_all, values, ids)
    context = context.reshape(count * length, width)
    mixed = dot(context, output_turned, BY_LAST) + output_bias.astype(WIDE)
    first_normed, first_scaling = normalize(rows.astype(WIDE) + mixed)
    first_rows = first_normed * first_gain.astype(WIDE) + first_shift.astype(WIDE)
    first_low = first_rows.astype(LOW)
    preactivation = dot(first_low, inner_full, BY_ROWS) + inner_bias_full
    cumulative = 0.5 * (1.0 + lax.erf(preactivation * 0.7071067811865476))
    activation_rows = (preactivation * cumulative).astype(LOW)
    density = jnp.exp(-0.5 * preactivation * preactivation) * 0.3989422804014327
    slope = cumulative + preactivation * density
    branch = dot(activation_rows, outer_turned, BY_LAST)
    second_normed, second_scaling = normalize(first_rows + branch + outer_bias.astype(WIDE))
    second_rows = second_normed * second_gain.astype(WIDE) + second_shift.astype(WIDE)
    layer_out = own_places(second_rows.astype(LOW))

    grad_out = whole_rows(out_grad).astype(WIDE)
    grad_second, second_gain_grad, second_shift_grad = normalize_back(
        grad_out, second_normed, second_scaling, second_gain.astype(WIDE)
    )
    outer_bias_grad = jnp.sum(grad_second, axis=0)
    grad_branch = grad_second.astype(LOW)
    (outer_share,) = own_share(dot(grad_branch, activation_rows, BY_FIRST).astype(LOW), (outer_turned.shape[1],))
    grad_activ = dot(grad_branch, outer_turned, BY_ROWS)
    grad_pre = (grad_activ * slope).astype(LOW)
    inner_bias_grad = jnp.sum(grad_pre.astype(WIDE), axis=0)
    inner_grad = dot(first_low, grad_pre, BY_FIRST).astype(LOW)
    grad_first = grad_second + dot(grad_pre, inner_full, BY_LAST)
    grad_mixed, first_gain_grad, first_shift_grad = normalize_back(
        grad_first, first_normed, first_scaling, first_gain.astype(WIDE)
    )
    output_bias_grad = jnp.sum(grad_mixed, axis=0)
    grad_mixed_low = grad_mixed.astype(LOW)
    output_grad = dot(grad_mixed_low, context, BY_FIRST).astype(LOW)
    inner_share, output_share = own_share(
        jnp.concatenate([inner_grad, output_grad], axis=1), (inner_grad.shape[1], width)
    )
    grad_context = dot(grad_mixed_low, output_turned, BY_ROWS).astype(LOW).reshape(shape)
    query_rows_grad, key_rows_grad, value_rows_grad = (
        array.reshape(count * length, width)
        for array in attend_back(queries, keys_all, values, grad_context, logsum, ids)
    )
    query_bias_grad = jnp.sum(query_rows_grad.astype(WIDE), axis=0)
    value_bias_grad = jnp.sum(value_rows_grad.astype(WIDE), axis=0)
    tokens_grad = (
        grad_mixed
        + dot(query_rows_grad, query_full, BY_LAST)
        + dot(key_rows_grad, key_full, BY_LAST)
        + dot(value_rows_grad, value_full, BY_LAST)
    )
    tokens_grad = own_places(tokens_grad.astype(LOW)).astype(WIDE)
    head_grads = [
        dot(rows, grad, BY_FIRST).astype(LOW)
        for grad in (query_rows_grad, key_rows_grad, value_rows_grad)
    ]
    query_share, key_share, value_share = own_share(
        jnp.concatenate(head_grads, axis=1), (width, width, width)
    )
    totals = total_over_all(
        fsdp,
        tp,
        jnp.concatenate(
            [
                output_bias_grad,
                first_gain_grad,
                first_shift_grad,
                outer_bias_grad,
                second_gain_grad,
                second_shift_grad,
                query_bias_grad,
                value_bias_grad,
                inner_bias_grad,
            ]
        ),
    )
    rowwise = [totals[i * width : (i + 1) * width] for i in range(6)]
    query_bias_total = lax.dynamic_slice_in_dim(totals, 6 * width + rank * head_cols, head_cols)
    value_bias_total = lax.dynamic_slice_in_dim(totals, 7 * width + rank * head_cols, head_cols)
    inner_bias_total = lax.dynamic_slice_in_dim(totals, 8 * width + rank * unit_cols, unit_cols)
    return (
        layer_out,
        tokens_grad,
        query_share,
        query_bias_total,
        key_share,
        value_share,
        value_bias_total,
        output_share.T,
        rowwise[0],
        rowwise[1],
        rowwise[2],
        inner_share,
        inner_bias_total,
        outer_share.T,
        rowwise[3],
        rowwise[4],
        rowwise[5],
    )


def solution(mesh):
    split = P("fsdp", "tp", None)
    across, turned = P("fsdp", "tp"), P("tp", "fsdp")
    seqs, units, copied = P("fsdp", None), P("tp"), P()
    return jax.shard_map(
        functools.partial(on_device, mesh.shape["fsdp"], mesh.shape["tp"]),
        mesh=mesh,
        in_specs=(
            split,
            seqs,
            seqs,
            across,
            units,
            across,
            across,
            units,
            turned,
            copied,
            copied,
            copied,
            across,
            units,
            turned,
            copied,
            copied,
            copied,
            split,
        ),
        out_specs=(
            split,
            split,
            across,
            units,
            across,
            across,
            units,
            turned,
            copied,
            copied,
            copied,
            across,
            units,
            turned,
            copied,
            copied,
            copied,
        ),
        check_vma=False,
    )
```

```python
import functools

import jax
import jax.numpy as jnp
from jax import lax
from jax.experimental import pallas as pl
from jax.sharding import PartitionSpec as P

HDIM = 64
EPSILON = 1e-12
MASKED = -1000000000.0
PAIR = 2 * HDIM
BLOCK = 256
LOW = jnp.bfloat16
WIDE = jnp.float32
BY_LAST = (((1,), (1,)), ((), ()))
BY_ROWS = (((1,), (0,)), ((), ()))
BY_FIRST = (((0,), (0,)), ((), ()))


def dot(left, right, dims):
    return lax.dot_general(left, right, dims, preferred_element_type=WIDE)


def halves(pair):
    lane = lax.broadcasted_iota(jnp.int32, (1, PAIR), 1)
    zero = jnp.zeros((), pair.dtype)
    return jnp.where(lane < HDIM, pair, zero), jnp.where(lane < HDIM, zero, pair)


def attend_kernel(q_ref, k_ref, v_ref, row_ref, col_ref, context_ref, logsum_ref, *, scaling):
    keys_all = k_ref[0]
    turned = [half.T for half in halves(v_ref[0])]
    key_ids = col_ref[0]
    for start in range(0, q_ref.shape[1], BLOCK):
        part = slice(start, start + BLOCK)
        seen = key_ids == row_ref[0, :, part]
        total = None
        for head, queries in enumerate(halves(q_ref[0, part, :] * scaling)):
            scores = jnp.where(seen, dot(keys_all, queries, BY_LAST), MASKED)
            highest = jnp.max(scores, axis=0, keepdims=True)
            weights = jnp.exp(scores - highest)
            sums = jnp.sum(weights, axis=0, keepdims=True)
            probs = (weights * (1.0 / sums)).astype(LOW)
            logsum_ref[0, 0, head : head + 1, part] = highest + jnp.log(sums)
            piece = dot(turned[head], probs, BY_ROWS)
            total = piece if total is None else total + piece
        context_ref[0, part, :] = total.T.astype(LOW)


def attend_back_kernel(
    q_ref, k_ref, v_ref, g_ref, logsum_ref, row_ref, col_ref, dq_ref, dk_ref, dv_ref, *, scaling
):
    keys_all = k_ref[0]
    values = v_ref[0]
    turned = [half.T for half in halves(keys_all)]
    key_ids = col_ref[0]
    length = q_ref.shape[1]
    key_grad = jnp.zeros((length, PAIR), WIDE)
    value_grad = jnp.zeros((length, PAIR), WIDE)
    for start in range(0, length, BLOCK):
        part = slice(start, start + BLOCK)
        seen = key_ids == row_ref[0, :, part]
        total = None
        queries_of = halves(q_ref[0, part, :] * scaling)
        grads_of = halves(g_ref[0, part, :])
        for head in range(2):
            queries, grads = queries_of[head], grads_of[head]
            scores = jnp.where(seen, dot(keys_all, queries, BY_LAST), MASKED)
            probs = jnp.exp(scores - logsum_ref[0, 0, head : head + 1, part])
            grad_probs = dot(values, grads, BY_LAST)
            value_grad = value_grad + dot(probs.astype(LOW), grads, BY_ROWS)
            level = jnp.sum(probs * grad_probs, axis=0, keepdims=True)
            grad_scores = (probs * (grad_probs - level)).astype(LOW)
            key_grad = key_grad + dot(grad_scores, queries, BY_ROWS)
            piece = dot(turned[head], grad_scores, BY_ROWS)
            total = piece if total is None else total + piece
        dq_ref[0, part, :] = (total.T * HDIM ** (-0.5)).astype(LOW)
    dk_ref[0] = key_grad.astype(LOW)
    dv_ref[0] = value_grad.astype(LOW)


def attention_specs(length):
    return (
        pl.BlockSpec((1, length, PAIR), lambda s, p: (s, 0, p)),
        pl.BlockSpec((1, 1, length), lambda s, p: (s, 0, 0)),
        pl.BlockSpec((1, length, 1), lambda s, p: (s, 0, 0)),
        pl.BlockSpec((1, 1, 2, length), lambda s, p: (s, p, 0, 0)),
    )


def attend(queries, keys_all, values, ids):
    count, length, width = queries.shape
    rows, as_row, as_col, sums = attention_specs(length)
    scaling = HDIM ** (-0.5)
    return pl.pallas_call(
        functools.partial(attend_kernel, scaling=scaling),
        grid=(count, width // PAIR),
        in_specs=[rows, rows, rows, as_row, as_col],
        out_specs=[rows, sums],
        out_shape=[
            jax.ShapeDtypeStruct(queries.shape, LOW),
            jax.ShapeDtypeStruct((count, width // PAIR, 2, length), WIDE),
        ],
        cost_estimate=pl.CostEstimate(
            flops=28 * count * width * length * length,
            transcendentals=count * width * length * length // HDIM,
            bytes_accessed=8 * count * width * length,
        ),
        name="attend",
    )(queries, keys_all, values, ids[:, None, :], ids[:, :, None])


def attend_back(queries, keys_all, values, grad_context, logsum, ids):
    count, length, width = queries.shape
    rows, as_row, as_col, sums = attention_specs(length)
    scaling = HDIM ** (-0.5)
    return pl.pallas_call(
        functools.partial(attend_back_kernel, scaling=scaling),
        grid=(count, width // PAIR),
        in_specs=[rows, rows, rows, rows, sums, as_row, as_col],
        out_specs=[rows, rows, rows],
        out_shape=[jax.ShapeDtypeStruct(queries.shape, LOW)] * 3,
        cost_estimate=pl.CostEstimate(
            flops=48 * count * width * length * length,
            transcendentals=count * width * length * length // HDIM,
            bytes_accessed=14 * count * width * length,
        ),
        name="attend_back",
    )(queries, keys_all, values, grad_context, logsum, ids[:, None, :], ids[:, :, None])


def dealt(axis, members, blocks):
    rank = lax.axis_index(axis)
    parts = []
    for step in range(members):
        block = lax.dynamic_slice_in_dim(blocks, (rank + step) % members, 1, 0)[0]
        pairs = [(i, (i + step) % members) for i in range(members)]
        parts.append(lax.ppermute(block, axis, pairs) if step else block)
    return parts


def sent_back(axis, members, parts):
    moved = [parts[0]]
    for step in range(1, members):
        pairs = [(i, (i - step) % members) for i in range(members)]
        moved.append(lax.ppermute(parts[step], axis, pairs))
    return moved


def by_source(axis, members, moved):
    rank = lax.axis_index(axis)
    result = jnp.broadcast_to(moved[0][None], (members,) + moved[0].shape)
    for step in range(1, members):
        result = lax.dynamic_update_slice_in_dim(
            result, moved[step][None], (rank + step) % members, 0
        )
    return result


def flip(axis, members, bit, block):
    return lax.ppermute(block, axis, [(i, i ^ bit) for i in range(members)])


def joined(axis, members, bit, block, place):
    mine = lax.axis_index(axis) // bit % 2
    other = flip(axis, members, bit, block)
    shape = block.shape[:place] + (2,) + block.shape[place:]
    spot = lax.broadcasted_iota(jnp.int32, shape, place)
    return jnp.where(spot == mine, jnp.expand_dims(block, place), jnp.expand_dims(other, place))


def halved(axis, members, bit, array, place):
    mine = lax.axis_index(axis) // bit % 2
    theirs = lax.squeeze(lax.dynamic_slice_in_dim(array, 1 - mine, 1, place), (place,))
    kept = lax.squeeze(lax.dynamic_slice_in_dim(array, mine, 1, place), (place,))
    return kept.astype(WIDE) + flip(axis, members, bit, theirs).astype(WIDE)


def gather_tp(members, block):
    if members != 4:
        return lax.all_gather(block, "tp", axis=0)
    shape = block.shape
    block = joined("tp", members, 1, block, 0)
    block = joined("tp", members, 2, block, 0)
    return block.reshape((members,) + shape)


def gather_rows(members, block, before):
    if members != 8:
        return lax.all_gather(block, "fsdp", axis=0, tiled=True), before
    rows, cols = block.shape
    first = joined("fsdp", members, 2, block[:, : cols // 2], 0)
    second = joined("fsdp", members, 4, block[:, cols // 2 :], 0)
    first = joined("fsdp", members, 4, first, 0)
    second = joined("fsdp", members, 2, second, 1)
    both, before = lax.optimization_barrier((jnp.concatenate([first, second], axis=3), before))
    return joined("fsdp", members, 1, both, 2).reshape(members * rows, cols), before


def scatter_rows(members, grad):
    if members != 8:
        return lax.psum_scatter(grad, "fsdp", scatter_dimension=0, tiled=True).astype(WIDE)
    total_rows, cols = grad.shape
    rows = total_rows // members
    grad = halved("fsdp", members, 1, grad.reshape(2, 2, 2, rows, cols), 2).astype(LOW)
    first = halved("fsdp", members, 4, grad[..., : cols // 2], 0).astype(LOW)
    second = halved("fsdp", members, 2, grad[..., cols // 2 :], 1).astype(LOW)
    first = halved("fsdp", members, 2, first, 0)
    second = halved("fsdp", members, 4, second, 0)
    return jnp.concatenate([first, second], axis=1)


def scatter_long(members, grad):
    return lax.psum_scatter(grad, "fsdp", scatter_dimension=0, tiled=True).astype(WIDE)


def scatter_tp_first(members, blocks):
    blocks = blocks.astype(LOW)
    if members != 4:
        return lax.psum_scatter(blocks, "tp", scatter_dimension=0)
    return halved("tp", members, 2, blocks.reshape((2, 2) + blocks.shape[1:]), 0).astype(LOW)


def scatter_tp_last(members, blocks):
    return halved("tp", members, 1, blocks, 0) if members == 4 else blocks.astype(WIDE)


def total_over_all(fsdp, tp, vector):
    for axis, members in (("fsdp", fsdp), ("tp", tp)):
        bit = 1
        while bit < members:
            vector = vector + flip(axis, members, bit, vector)
            bit *= 2
    return vector


def normalize(token_rows):
    centred = token_rows - jnp.mean(token_rows, axis=-1, keepdims=True)
    scaling = lax.rsqrt(jnp.mean(centred * centred, axis=-1, keepdims=True) + EPSILON)
    return centred * scaling, scaling


def normalize_back(grad_rows, normed, scaling, gain_row):
    grad_normed = grad_rows * gain_row
    adjusted = grad_normed - jnp.mean(grad_normed, axis=-1, keepdims=True)
    adjusted = adjusted - normed * jnp.mean(grad_normed * normed, axis=-1, keepdims=True)
    return scaling * adjusted, jnp.sum(grad_rows * normed, axis=0), jnp.sum(grad_rows, axis=0)


def on_device(
    fsdp,
    tp,
    tokens,
    segment_ids,
    live_mask,
    query_weight,
    query_bias,
    key_weight,
    value_weight,
    value_bias,
    output_weight,
    output_bias,
    first_gain,
    first_shift,
    inner_weight,
    inner_bias,
    outer_weight,
    outer_bias,
    second_gain,
    second_shift,
    out_grad,
):
    sequences, places, width = tokens.shape
    count = sequences // tp
    length = places * tp
    rank = lax.axis_index("tp")
    head_cols = query_weight.shape[1]
    unit_cols = inner_weight.shape[1]
    shard_rows = query_weight.shape[0]

    def whole_rows(array):
        parts = dealt("tp", tp, array.reshape(tp, count, places, width))
        return jnp.concatenate(parts, axis=1).reshape(count * length, width)

    def to_owners(array):
        parts = array.reshape(count, tp, places, width)
        return sent_back("tp", tp, [parts[:, step] for step in range(tp)])

    def own_places(parts):
        return by_source("tp", tp, parts).reshape(sequences, places, width)

    def columns(blocks):
        members, rows, cols = blocks.shape
        return blocks.transpose(1, 0, 2).reshape(rows, members * cols)

    def blocks_of(share, widths):
        rows, first, blocks = share.shape[0], 0, []
        for cols in widths:
            piece = share[:, first : first + cols].reshape(rows, tp, cols // tp)
            blocks.append(piece.transpose(1, 0, 2))
            first += cols
        return jnp.concatenate(blocks, axis=2)

    def own_share(share, widths):
        share = scatter_tp_last(tp, scatter_tp_first(tp, blocks_of(share, widths)))
        first, pieces = 0, []
        for cols in widths:
            pieces.append(share[:, first : first + cols // tp])
            first += cols // tp
        return pieces

    biases = jnp.concatenate([query_bias, value_bias, inner_bias]).reshape(-1, 3 * head_cols)
    heads = jnp.concatenate(
        [jnp.concatenate([query_weight, key_weight, value_weight], axis=1), biases], axis=0
    )
    heads = gather_tp(tp, heads)
    biases = heads[:, shard_rows:].reshape(tp, -1).astype(WIDE)
    query_bias_full = biases[:, :head_cols].reshape(-1)
    value_bias_full = biases[:, head_cols : 2 * head_cols].reshape(-1)
    inner_bias_full = biases[:, 2 * head_cols :].reshape(-1)
    heads = heads[:, :shard_rows].reshape(tp, shard_rows, 3, head_cols).transpose(1, 2, 0, 3)
    rows = whole_rows(tokens)
    heads, rows = gather_rows(fsdp, heads.reshape(shard_rows, 3 * width), rows)
    query_full, key_full, value_full = (heads[:, i * width : (i + 1) * width] for i in range(3))
    wide = jnp.concatenate([inner_weight, output_weight.T], axis=1)
    wide = gather_tp(tp, wide)
    wide = jnp.concatenate([columns(wide[:, :, :unit_cols]), columns(wide[:, :, unit_cols:])], axis=1)
    wide = lax.all_gather(wide, "fsdp", axis=0, tiled=True)
    inner_full, output_turned = wide[:, : tp * unit_cols], wide[:, tp * unit_cols :]
    outer_turned = columns(gather_tp(tp, outer_weight.T))
    outer_turned = lax.all_gather(outer_turned, "fsdp", axis=0, tiled=True)

    first = rank * count
    segment = lax.dynamic_slice_in_dim(segment_ids, first, count, 0)
    live = lax.dynamic_slice_in_dim(live_mask, first, count, 0)
    spots = lax.broadcasted_iota(jnp.int32, segment.shape, 1)
    ids = jnp.where(live == 1, segment, length + spots).reshape(count, tp, places)
    ids = [lax.dynamic_slice_in_dim(ids, (rank - step) % tp, 1, 1) for step in range(tp)]
    ids = jnp.concatenate(ids, axis=1).reshape(count, length)

    shape = (count, length, width)
    queries = (dot(rows, query_full, BY_ROWS) + query_bias_full).astype(LOW).reshape(shape)
    keys_all = dot(rows, key_full, BY_ROWS).astype(LOW).reshape(shape)
    values = (dot(rows, value_full, BY_ROWS) + value_bias_full).astype(LOW).reshape(shape)
    context, logsum = attend(queries, keys_all, values, ids)
    context = context.reshape(count * length, width)
    mixed = dot(context, output_turned, BY_LAST) + output_bias.astype(WIDE)
    first_normed, first_scaling = normalize(rows.astype(WIDE) + mixed)
    first_rows = first_normed * first_gain.astype(WIDE) + first_shift.astype(WIDE)
    first_low = first_rows.astype(LOW)
    preactivation = dot(first_low, inner_full, BY_ROWS) + inner_bias_full
    cumulative = 0.5 * (1.0 + lax.erf(preactivation * 0.7071067811865476))
    activation_rows = (preactivation * cumulative).astype(LOW)
    density = jnp.exp(-0.5 * preactivation * preactivation) * 0.3989422804014327
    slope = cumulative + preactivation * density
    branch = dot(activation_rows, outer_turned, BY_LAST)
    second_normed, second_scaling = normalize(first_rows + branch + outer_bias.astype(WIDE))
    second_rows = second_normed * second_gain.astype(WIDE) + second_shift.astype(WIDE)
    layer_out = to_owners(second_rows.astype(LOW))

    grad_out = whole_rows(out_grad).astype(WIDE)
    grad_second, second_gain_grad, second_shift_grad = normalize_back(
        grad_out, second_normed, second_scaling, second_gain.astype(WIDE)
    )
    outer_bias_grad = jnp.sum(grad_second, axis=0)
    grad_branch = grad_second.astype(LOW)
    outer_share = scatter_rows(fsdp, dot(grad_branch, activation_rows, BY_FIRST).astype(LOW))
    grad_activ = dot(grad_branch, outer_turned, BY_ROWS)
    grad_pre = (grad_activ * slope).astype(LOW)
    inner_bias_grad = jnp.sum(grad_pre.astype(WIDE), axis=0)
    inner_grad = dot(first_low, grad_pre, BY_FIRST).astype(LOW)
    grad_first = grad_second + dot(grad_pre, inner_full, BY_LAST)
    grad_mixed, first_gain_grad, first_shift_grad = normalize_back(
        grad_first, first_normed, first_scaling, first_gain.astype(WIDE)
    )
    output_bias_grad = jnp.sum(grad_mixed, axis=0)
    grad_mixed_low = grad_mixed.astype(LOW)
    output_grad = dot(grad_mixed_low, context, BY_FIRST).astype(LOW)
    grad_context = dot(grad_mixed_low, output_turned, BY_ROWS).astype(LOW).reshape(shape)
    grad_context, inner_grad, output_grad, outer_share = lax.optimization_barrier(
        (grad_context, inner_grad, output_grad, outer_share)
    )
    inner_share = scatter_long(fsdp, inner_grad)
    outer_share = blocks_of(outer_share, (outer_turned.shape[1],))
    outer_share = scatter_tp_first(tp, outer_share)
    query_rows_grad, key_rows_grad, value_rows_grad = (
        array.reshape(count * length, width)
        for array in attend_back(queries, keys_all, values, grad_context, logsum, ids)
    )
    query_rows_grad, layer_out, outer_share, inner_share = lax.optimization_barrier(
        (query_rows_grad, layer_out, outer_share, inner_share)
    )
    layer_out = own_places(layer_out)
    outer_share = scatter_tp_last(tp, outer_share)
    (inner_share,) = own_share(inner_share, (inner_full.shape[1],))
    query_bias_grad = jnp.sum(query_rows_grad.astype(WIDE), axis=0)
    value_bias_grad = jnp.sum(value_rows_grad.astype(WIDE), axis=0)
    tokens_grad = (
        grad_mixed
        + dot(query_rows_grad, query_full, BY_LAST)
        + dot(key_rows_grad, key_full, BY_LAST)
        + dot(value_rows_grad, value_full, BY_LAST)
    )
    tokens_grad = to_owners(tokens_grad.astype(LOW))
    head_grads = [
        dot(rows, grad, BY_FIRST).astype(LOW)
        for grad in (query_rows_grad, key_rows_grad, value_rows_grad)
    ]
    heads_share = scatter_rows(fsdp, jnp.concatenate(head_grads + [output_grad], axis=1))
    heads_share, tokens_grad = lax.optimization_barrier((heads_share, tokens_grad))
    query_share, key_share, value_share, output_share = own_share(heads_share, (width,) * 4)
    tokens_grad = own_places(tokens_grad).astype(WIDE)
    totals = total_over_all(
        fsdp,
        tp,
        jnp.concatenate(
            [
                output_bias_grad,
                first_gain_grad,
                first_shift_grad,
                outer_bias_grad,
                second_gain_grad,
                second_shift_grad,
                query_bias_grad,
                value_bias_grad,
                inner_bias_grad,
            ]
        ),
    )
    rowwise = [totals[i * width : (i + 1) * width] for i in range(6)]
    query_bias_total = lax.dynamic_slice_in_dim(totals, 6 * width + rank * head_cols, head_cols)
    value_bias_total = lax.dynamic_slice_in_dim(totals, 7 * width + rank * head_cols, head_cols)
    inner_bias_total = lax.dynamic_slice_in_dim(totals, 8 * width + rank * unit_cols, unit_cols)
    return (
        layer_out,
        tokens_grad,
        query_share,
        query_bias_total,
        key_share,
        value_share,
        value_bias_total,
        output_share.T,
        rowwise[0],
        rowwise[1],
        rowwise[2],
        inner_share,
        inner_bias_total,
        outer_share.T,
        rowwise[3],
        rowwise[4],
        rowwise[5],
    )


def solution(mesh):
    split = P("fsdp", "tp", None)
    across, turned = P("fsdp", "tp"), P("tp", "fsdp")
    seqs, units, copied = P("fsdp", None), P("tp"), P()
    return jax.shard_map(
        functools.partial(on_device, mesh.shape["fsdp"], mesh.shape["tp"]),
        mesh=mesh,
        in_specs=(
            split,
            seqs,
            seqs,
            across,
            units,
            across,
            across,
            units,
            turned,
            copied,
            copied,
            copied,
            across,
            units,
            turned,
            copied,
            copied,
            copied,
            split,
        ),
        out_specs=(
            split,
            split,
            across,
            units,
            across,
            across,
            units,
            turned,
            copied,
            copied,
            copied,
            across,
            units,
            turned,
            copied,
            copied,
            copied,
        ),
        check_vma=False,
    )
```

```python
import functools

import jax
import jax.numpy as jnp
from jax import lax
from jax.experimental import pallas as pl
from jax.sharding import PartitionSpec as P

HDIM = 64
EPSILON = 1e-12
MASKED = -1000000000.0
PAIR = 2 * HDIM
BLOCK = 256
LOW = jnp.bfloat16
WIDE = jnp.float32
BY_LAST = (((1,), (1,)), ((), ()))
BY_ROWS = (((1,), (0,)), ((), ()))
BY_FIRST = (((0,), (0,)), ((), ()))


def dot(left, right, dims):
    return lax.dot_general(left, right, dims, preferred_element_type=WIDE)


def halves(pair):
    lane = lax.broadcasted_iota(jnp.int32, (1, PAIR), 1)
    zero = jnp.zeros((), pair.dtype)
    return jnp.where(lane < HDIM, pair, zero), jnp.where(lane < HDIM, zero, pair)


def attend_kernel(q_ref, k_ref, v_ref, row_ref, col_ref, context_ref, logsum_ref, *, scaling):
    keys_all = k_ref[0]
    turned = [half.T for half in halves(v_ref[0])]
    key_ids = col_ref[0]
    for start in range(0, q_ref.shape[1], BLOCK):
        part = slice(start, start + BLOCK)
        seen = key_ids == row_ref[0, :, part]
        total = None
        for head, queries in enumerate(halves(q_ref[0, part, :] * scaling)):
            scores = jnp.where(seen, dot(keys_all, queries, BY_LAST), MASKED)
            highest = jnp.max(scores, axis=0, keepdims=True)
            weights = jnp.exp(scores - highest)
            sums = jnp.sum(weights, axis=0, keepdims=True)
            probs = (weights * (1.0 / sums)).astype(LOW)
            logsum_ref[0, 0, head : head + 1, part] = highest + jnp.log(sums)
            piece = dot(turned[head], probs, BY_ROWS)
            total = piece if total is None else total + piece
        context_ref[0, part, :] = total.T.astype(LOW)


def attend_back_kernel(
    q_ref, k_ref, v_ref, g_ref, logsum_ref, row_ref, col_ref, dq_ref, dk_ref, dv_ref, *, scaling
):
    keys_all = k_ref[0]
    values = v_ref[0]
    turned = [half.T for half in halves(keys_all)]
    key_ids = col_ref[0]
    length = q_ref.shape[1]
    key_grad = jnp.zeros((length, PAIR), WIDE)
    value_grad = jnp.zeros((length, PAIR), WIDE)
    for start in range(0, length, BLOCK):
        part = slice(start, start + BLOCK)
        seen = key_ids == row_ref[0, :, part]
        total = None
        queries_of = halves(q_ref[0, part, :] * scaling)
        grads_of = halves(g_ref[0, part, :])
        for head in range(2):
            queries, grads = queries_of[head], grads_of[head]
            scores = jnp.where(seen, dot(keys_all, queries, BY_LAST), MASKED)
            probs = jnp.exp(scores - logsum_ref[0, 0, head : head + 1, part])
            grad_probs = dot(values, grads, BY_LAST)
            value_grad = value_grad + dot(probs.astype(LOW), grads, BY_ROWS)
            level = jnp.sum(probs * grad_probs, axis=0, keepdims=True)
            grad_scores = (probs * (grad_probs - level)).astype(LOW)
            key_grad = key_grad + dot(grad_scores, queries, BY_ROWS)
            piece = dot(turned[head], grad_scores, BY_ROWS)
            total = piece if total is None else total + piece
        dq_ref[0, part, :] = (total.T * HDIM ** (-0.5)).astype(LOW)
    dk_ref[0] = key_grad.astype(LOW)
    dv_ref[0] = value_grad.astype(LOW)


def attention_specs(length, first=0):
    return (
        pl.BlockSpec((1, length, PAIR), lambda s, p: (s, 0, p + first)),
        pl.BlockSpec((1, 1, length), lambda s, p: (s, 0, 0)),
        pl.BlockSpec((1, length, 1), lambda s, p: (s, 0, 0)),
        pl.BlockSpec((1, 1, 2, length), lambda s, p: (s, p + first, 0, 0)),
    )


def attend(queries, keys_all, values, ids):
    count, length, width = queries.shape
    rows, as_row, as_col, sums = attention_specs(length)
    scaling = HDIM ** (-0.5)
    return pl.pallas_call(
        functools.partial(attend_kernel, scaling=scaling),
        grid=(count, width // PAIR),
        in_specs=[rows, rows, rows, as_row, as_col],
        out_specs=[rows, sums],
        out_shape=[
            jax.ShapeDtypeStruct(queries.shape, LOW),
            jax.ShapeDtypeStruct((count, width // PAIR, 2, length), WIDE),
        ],
        cost_estimate=pl.CostEstimate(
            flops=28 * count * width * length * length,
            transcendentals=count * width * length * length // HDIM,
            bytes_accessed=8 * count * width * length,
        ),
        name="attend",
    )(queries, keys_all, values, ids[:, None, :], ids[:, :, None])


def attend_back(queries, keys_all, values, grad_context, logsum, ids, earlier, part):
    count, length, width = queries.shape
    pairs = width // PAIR
    first = pairs // 2 * part
    rows, as_row, as_col, sums = attention_specs(length, first)
    body = functools.partial(attend_back_kernel, scaling=HDIM ** (-0.5))
    operands = [queries, keys_all, values, grad_context, logsum, ids[:, None, :], ids[:, :, None]]
    in_specs = [rows, rows, rows, rows, sums, as_row, as_col]
    aliases = {}
    if earlier is not None:

        def body(*refs):
            attend_back_kernel(*refs[:7], *refs[10:], scaling=HDIM ** (-0.5))

        aliases = {7 + i: i for i in range(3)}
        operands += list(earlier)
        in_specs += [pl.BlockSpec(memory_space=pl.ANY)] * 3
    return pl.pallas_call(
        body,
        grid=(count, (pairs - first) if part else pairs // 2),
        in_specs=in_specs,
        out_specs=[rows, rows, rows],
        out_shape=[jax.ShapeDtypeStruct(queries.shape, LOW)] * 3,
        input_output_aliases=aliases,
        cost_estimate=pl.CostEstimate(
            flops=24 * count * width * length * length,
            transcendentals=count * width * length * length // HDIM // 2,
            bytes_accessed=7 * count * width * length,
        ),
        name="attend_back",
    )(*operands)


def meet(value, parts, picks):
    picked = [step for step in picks if step < len(parts)]
    value, held = lax.optimization_barrier((value, [parts[step] for step in picked]))
    parts = list(parts)
    for step, part in zip(picked, held):
        parts[step] = part
    return value, parts


def spread(block):
    members = lax.axis_size("tp")
    rank_pairs = [[(i, (i + step) % members) for i in range(members)] for step in range(1, members)]
    return [block] + [lax.ppermute(block, "tp", pairs) for pairs in rank_pairs]


def dealt(blocks):
    members, rank = lax.axis_size("tp"), lax.axis_index("tp")
    parts = []
    for step in range(members):
        block = lax.dynamic_slice_in_dim(blocks, (rank + step) % members, 1, 0)[0]
        pairs = [(i, (i + step) % members) for i in range(members)]
        parts.append(lax.ppermute(block, "tp", pairs) if step else block)
    return parts


def sent_back(parts):
    members = lax.axis_size("tp")
    moved = [parts[0]]
    for step in range(1, members):
        pairs = [(i, (i - step) % members) for i in range(members)]
        moved.append(lax.ppermute(parts[step], "tp", pairs))
    return moved


def by_source(moved):
    members, rank = len(moved), lax.axis_index("tp")
    shape = (members,) + moved[0].shape
    above = (lax.broadcasted_iota(jnp.int32, shape, 0) - rank) % members
    result = jnp.broadcast_to(moved[0][None], shape)
    for step in range(1, members):
        result = jnp.where(above == step, moved[step][None], result)
    return result


def flip(axis, members, bit, block):
    return lax.ppermute(block, axis, [(i, i ^ bit) for i in range(members)])


def beside(bit, block, other, place):
    mine = lax.axis_index("fsdp") // bit % 2
    shape = block.shape[:place] + (2,) + block.shape[place:]
    spot = lax.broadcasted_iota(jnp.int32, shape, place)
    return jnp.where(spot == mine, jnp.expand_dims(block, place), jnp.expand_dims(other, place))


def entries(bit, array, place):
    mine = lax.axis_index("fsdp") // bit % 2
    return [
        lax.squeeze(lax.dynamic_slice_in_dim(array, spot, 1, place), (place,)) for spot in (mine, 1 - mine)
    ]


def gather_rows(members, block, before, beyond):
    if members != 8:
        return lax.all_gather(block, "fsdp", axis=0, tiled=True), before, beyond
    rows, cols = block.shape
    first, second = block[:, : cols // 2], block[:, cols // 2 :]
    (over_x, over_y), beyond = meet(
        (flip("fsdp", members, 2, first), flip("fsdp", members, 4, second)), beyond, (2, 3)
    )
    first, second = beside(2, first, over_x, 0), beside(4, second, over_y, 0)
    (over_y, over_x), before = meet(
        (flip("fsdp", members, 4, first), flip("fsdp", members, 2, second)), before, (1, 2)
    )
    both = jnp.concatenate([beside(4, first, over_y, 0), beside(2, second, over_x, 1)], axis=3)
    other, before = meet(flip("fsdp", members, 1, both), before, (3,))
    return beside(1, both, other, 2).reshape(members * rows, cols), before, beyond


def add_low(kept, moved):
    return (kept.astype(WIDE) + moved.astype(WIDE)).astype(LOW)


def scatter_core(grad):
    if lax.axis_size("fsdp") != 8:
        return lax.psum_scatter(grad, "fsdp", scatter_dimension=0, tiled=True)
    total_rows, cols = grad.shape
    kept, theirs = entries(1, grad.reshape(2, 2, 2, total_rows // 8, cols), 2)
    return add_low(kept, flip("fsdp", 8, 1, theirs))


def scatter_near(grad):
    if lax.axis_size("fsdp") != 8:
        return grad
    half = grad.shape[-1] // 2
    first, first_out = entries(4, grad[..., :half], 0)
    second, second_out = entries(2, grad[..., half:], 1)
    over_y, over_x = lax.optimization_barrier(
        (flip("fsdp", 8, 4, first_out), flip("fsdp", 8, 2, second_out))
    )
    return add_low(first, over_y), add_low(second, over_x)


def scatter_far(grad):
    if lax.axis_size("fsdp") != 8:
        return grad
    first, first_out = entries(2, grad[0], 0)
    second, second_out = entries(4, grad[1], 0)
    over_x, over_y = lax.optimization_barrier(
        (flip("fsdp", 8, 2, first_out), flip("fsdp", 8, 4, second_out))
    )
    return jnp.concatenate([add_low(first, over_x), add_low(second, over_y)], axis=1)


def total_over_tp(vector):
    bit = 1
    while bit < lax.axis_size("tp"):
        vector = vector + flip("tp", lax.axis_size("tp"), bit, vector)
        bit *= 2
    return vector


def total_over_fsdp(vector):
    bit = 1
    while bit < lax.axis_size("fsdp"):
        vector = vector + flip("fsdp", lax.axis_size("fsdp"), bit, vector)
        bit *= 2
    return vector


def normalize(token_rows):
    centred = token_rows - jnp.mean(token_rows, axis=-1, keepdims=True)
    scaling = lax.rsqrt(jnp.mean(centred * centred, axis=-1, keepdims=True) + EPSILON)
    return centred * scaling, scaling


def normalize_back(grad_rows, normed, scaling, gain_row):
    grad_normed = grad_rows * gain_row
    adjusted = grad_normed - jnp.mean(grad_normed, axis=-1, keepdims=True)
    adjusted = adjusted - normed * jnp.mean(grad_normed * normed, axis=-1, keepdims=True)
    return scaling * adjusted, jnp.sum(grad_rows * normed, axis=0), jnp.sum(grad_rows, axis=0)


def on_device(
    fsdp,
    tp,
    tokens,
    segment_ids,
    live_mask,
    query_weight,
    query_bias,
    key_weight,
    value_weight,
    value_bias,
    output_weight,
    output_bias,
    first_gain,
    first_shift,
    inner_weight,
    inner_bias,
    outer_weight,
    outer_bias,
    second_gain,
    second_shift,
    out_grad,
):
    sequences, places, width = tokens.shape
    count = sequences // tp
    length = places * tp
    rank = lax.axis_index("tp")
    head_cols = query_weight.shape[1]
    unit_cols = inner_weight.shape[1]
    shard_rows = query_weight.shape[0]

    def whole_rows(parts):
        return jnp.concatenate(parts, axis=1).reshape(count * length, width)

    def by_member(array):
        return array.reshape(tp, count, places, width)

    def to_owners(array):
        parts = array.reshape(count, tp, places, width)
        return sent_back([parts[:, step] for step in range(tp)])

    def own_places(parts):
        return by_source(parts).reshape(sequences, places, width)

    def columns(parts, widths):
        pieces, first = [], 0
        for cols in widths:
            pieces += [part[:shard_rows, first : first + cols] for part in parts]
            first += cols
        return jnp.concatenate(pieces, axis=1)

    def own_columns(share, widths):
        parts = []
        for step in range(tp):
            pieces, first = [], 0
            for cols in widths:
                pieces.append(share[:, first + step * cols : first + (step + 1) * cols])
                first += tp * cols
            parts.append(jnp.concatenate(pieces, axis=1))
        return sent_back(parts)

    def summed(parts, widths):
        total, first, pieces = sum(part.astype(WIDE) for part in parts), 0, []
        for cols in widths:
            pieces.append(total[:, first : first + cols])
            first += cols
        return pieces

    def by_rank(vector):
        parts = vector.reshape(tp, -1)
        parts = [lax.dynamic_slice_in_dim(parts, (rank - spot) % tp, 1, 0) for spot in range(tp)]
        return jnp.concatenate(parts, axis=0).reshape(-1)

    biases = jnp.concatenate([query_bias, value_bias, inner_bias]).reshape(-1, 4 * head_cols // 2)
    biases = jnp.pad(biases, ((0, 0), (0, 4 * head_cols - biases.shape[1])))
    heads = jnp.concatenate([query_weight, key_weight, value_weight, output_weight.T], axis=1)
    heads = spread(jnp.concatenate([heads, biases], axis=0))
    rest = jnp.concatenate([inner_weight, outer_weight.T], axis=1)
    rest, heads = meet(rest, heads, (1, 2, 3))
    rest = spread(rest)
    tokens, rest = meet(tokens, rest, (1,))
    rows = dealt(by_member(tokens))
    biases = [part[shard_rows:, : 2 * head_cols].reshape(-1).astype(WIDE) for part in heads]
    query_bias_full = jnp.concatenate([part[:head_cols] for part in biases])
    value_bias_full = jnp.concatenate([part[head_cols : 2 * head_cols] for part in biases])
    inner_bias_full = jnp.concatenate([part[2 * head_cols :] for part in biases])
    heads, rows, rest = gather_rows(fsdp, columns(heads, (head_cols,) * 4), rows, rest)
    query_full, key_full, value_full, output_turned = (
        heads[:, i * width : (i + 1) * width] for i in range(4)
    )
    rows = whole_rows(rows)
    rows, out_grad = lax.optimization_barrier((rows, out_grad))
    rest = lax.all_gather(columns(rest, (unit_cols, unit_cols)), "fsdp", axis=0, tiled=True)
    inner_full, outer_turned = rest[:, : tp * unit_cols], rest[:, tp * unit_cols :]

    first = rank * count
    segment = lax.dynamic_slice_in_dim(segment_ids, first, count, 0)
    live = lax.dynamic_slice_in_dim(live_mask, first, count, 0)
    spots = lax.broadcasted_iota(jnp.int32, segment.shape, 1)
    ids = jnp.where(live == 1, segment, length + spots).reshape(count, tp, places)
    ids = [lax.dynamic_slice_in_dim(ids, (rank - step) % tp, 1, 1) for step in range(tp)]
    ids = jnp.concatenate(ids, axis=1).reshape(count, length)

    shape = (count, length, width)
    queries = (dot(rows, query_full, BY_ROWS) + query_bias_full).astype(LOW).reshape(shape)
    keys_all = dot(rows, key_full, BY_ROWS).astype(LOW).reshape(shape)
    values = (dot(rows, value_full, BY_ROWS) + value_bias_full).astype(LOW).reshape(shape)
    context, logsum = attend(queries, keys_all, values, ids)
    context, grad_out = meet(context, dealt(by_member(out_grad)), (2,))
    context = context.reshape(count * length, width)
    mixed = dot(context, output_turned, BY_LAST) + output_bias.astype(WIDE)
    first_normed, first_scaling = normalize(rows.astype(WIDE) + mixed)
    first_rows = first_normed * first_gain.astype(WIDE) + first_shift.astype(WIDE)
    first_low = first_rows.astype(LOW)
    preactivation = dot(first_low, inner_full, BY_ROWS) + inner_bias_full
    cumulative = 0.5 * (1.0 + lax.erf(preactivation * 0.7071067811865476))
    activation_rows = (preactivation * cumulative).astype(LOW)
    density = jnp.exp(-0.5 * preactivation * preactivation) * 0.3989422804014327
    slope = cumulative + preactivation * density
    activation_rows, grad_out = meet(activation_rows, grad_out, (1, 3))
    branch = dot(activation_rows, outer_turned, BY_LAST)
    second_normed, second_scaling = normalize(first_rows + branch + outer_bias.astype(WIDE))
    second_rows = second_normed * second_gain.astype(WIDE) + second_shift.astype(WIDE)
    layer_out = to_owners(second_rows.astype(LOW))

    grad_out = whole_rows(grad_out).astype(WIDE)
    grad_second, second_gain_grad, second_shift_grad = normalize_back(
        grad_out, second_normed, second_scaling, second_gain.astype(WIDE)
    )
    outer_bias_grad = jnp.sum(grad_second, axis=0)
    grad_branch = grad_second.astype(LOW)
    outer_grad = dot(grad_branch, activation_rows, BY_FIRST).astype(LOW)
    outer_share = lax.psum_scatter(outer_grad, "fsdp", scatter_dimension=0, tiled=True)
    grad_activ = dot(grad_branch, outer_turned, BY_ROWS)
    grad_pre = (grad_activ * slope).astype(LOW)
    grad_pre, layer_out = meet(grad_pre, layer_out, (2,))
    inner_bias_grad = jnp.sum(grad_pre.astype(WIDE), axis=0)
    inner_share = scatter_core(dot(first_low, grad_pre, BY_FIRST).astype(LOW))
    grad_first = grad_second + dot(grad_pre, inner_full, BY_LAST)
    grad_mixed, first_gain_grad, first_shift_grad = normalize_back(
        grad_first, first_normed, first_scaling, first_gain.astype(WIDE)
    )
    output_bias_grad = jnp.sum(grad_mixed, axis=0)
    grad_mixed_low = grad_mixed.astype(LOW)
    output_grad = dot(grad_mixed_low, context, BY_FIRST).astype(LOW)
    grad_context = dot(grad_mixed_low, output_turned, BY_ROWS).astype(LOW).reshape(shape)
    early = total_over_tp(
        jnp.concatenate(
            [
                output_bias_grad,
                first_gain_grad,
                first_shift_grad,
                outer_bias_grad,
                second_gain_grad,
                second_shift_grad,
                by_rank(inner_bias_grad),
            ]
        )
    )
    grad_context, inner_share, output_grad, layer_out, early = lax.optimization_barrier(
        (grad_context, scatter_near(inner_share), output_grad, layer_out, early)
    )
    early = total_over_fsdp(early)
    inner_share = scatter_far(inner_share)
    back = functools.partial(attend_back, queries, keys_all, values, grad_context, logsum, ids)
    halfway = back(None, 0)
    halfway, inner_share, outer_share, early = lax.optimization_barrier(
        (halfway, inner_share, outer_share, early)
    )
    layer_out = own_places(layer_out)
    inner_parts = own_columns(inner_share, (unit_cols,))
    outer_parts = own_columns(outer_share, (unit_cols,))
    rows_grads = back(halfway, 1)
    rows_grads, inner_parts, outer_parts = lax.optimization_barrier(
        (rows_grads, inner_parts, outer_parts)
    )
    (inner_share,) = summed(inner_parts, (unit_cols,))
    (outer_share,) = summed(outer_parts, (unit_cols,))
    query_rows_grad, key_rows_grad, value_rows_grad = (
        array.reshape(count * length, width) for array in rows_grads
    )
    query_bias_grad = jnp.sum(query_rows_grad.astype(WIDE), axis=0)
    value_bias_grad = jnp.sum(value_rows_grad.astype(WIDE), axis=0)
    late = total_over_tp(
        jnp.concatenate([by_rank(query_bias_grad), by_rank(value_bias_grad)])
    )
    head_grads = [
        dot(rows, grad, BY_FIRST).astype(LOW)
        for grad in (query_rows_grad, key_rows_grad, value_rows_grad)
    ]
    heads_share = scatter_core(jnp.concatenate(head_grads + [output_grad], axis=1))
    tokens_grad = (
        grad_mixed
        + dot(query_rows_grad, query_full, BY_LAST)
        + dot(key_rows_grad, key_full, BY_LAST)
        + dot(value_rows_grad, value_full, BY_LAST)
    ).astype(LOW)
    tokens_grad, late = lax.optimization_barrier((tokens_grad, late))
    tokens_grad = to_owners(tokens_grad)
    late = total_over_fsdp(late)
    heads_share, tokens_grad = meet(scatter_near(heads_share), tokens_grad, (2,))
    heads_share, tokens_grad = meet(scatter_far(heads_share), tokens_grad, (1, 3))
    heads_share, late = lax.optimization_barrier((heads_share, late))
    query_share, key_share, value_share, output_share = summed(
        own_columns(heads_share, (head_cols,) * 4), (head_cols,) * 4
    )
    tokens_grad = own_places(tokens_grad).astype(WIDE)
    totals = jnp.concatenate([early[: 6 * width], late, early[6 * width :]])
    rowwise = [totals[i * width : (i + 1) * width] for i in range(6)]
    query_bias_total = lax.dynamic_slice_in_dim(totals, 6 * width + rank * head_cols, head_cols)
    value_bias_total = lax.dynamic_slice_in_dim(totals, 7 * width + rank * head_cols, head_cols)
    inner_bias_total = lax.dynamic_slice_in_dim(totals, 8 * width + rank * unit_cols, unit_cols)
    return (
        layer_out,
        tokens_grad,
        query_share,
        query_bias_total,
        key_share,
        value_share,
        value_bias_total,
        output_share.T,
        rowwise[0],
        rowwise[1],
        rowwise[2],
        inner_share,
        inner_bias_total,
        outer_share.T,
        rowwise[3],
        rowwise[4],
        rowwise[5],
    )


def solution(mesh):
    split = P("fsdp", "tp", None)
    across, turned = P("fsdp", "tp"), P("tp", "fsdp")
    seqs, units, copied = P("fsdp", None), P("tp"), P()
    return jax.shard_map(
        functools.partial(on_device, mesh.shape["fsdp"], mesh.shape["tp"]),
        mesh=mesh,
        in_specs=(
            split,
            seqs,
            seqs,
            across,
            units,
            across,
            across,
            units,
            turned,
            copied,
            copied,
            copied,
            across,
            units,
            turned,
            copied,
            copied,
            copied,
            split,
        ),
        out_specs=(
            split,
            split,
            across,
            units,
            across,
            across,
            units,
            turned,
            copied,
            copied,
            copied,
            across,
            units,
            turned,
            copied,
            copied,
            copied,
        ),
        check_vma=False,
    )
```

```python
import functools

import jax
import jax.numpy as jnp
from jax import lax
from jax.experimental import pallas as pl
from jax.sharding import PartitionSpec as P

HDIM = 64
EPSILON = 1e-12
MASKED = -1000000000.0
PAIR = 2 * HDIM
BLOCK = 256
LOW = jnp.bfloat16
WIDE = jnp.float32
BY_LAST = (((1,), (1,)), ((), ()))
BY_ROWS = (((1,), (0,)), ((), ()))
BY_FIRST = (((0,), (0,)), ((), ()))


def dot(left, right, dims):
    return lax.dot_general(left, right, dims, preferred_element_type=WIDE)


def halves(pair):
    lane = lax.broadcasted_iota(jnp.int32, (1, PAIR), 1)
    zero = jnp.zeros((), pair.dtype)
    return jnp.where(lane < HDIM, pair, zero), jnp.where(lane < HDIM, zero, pair)


def attend_kernel(q_ref, k_ref, v_ref, row_ref, col_ref, context_ref, logsum_ref, *, scaling):
    keys_all = k_ref[0]
    turned = [half.T for half in halves(v_ref[0])]
    key_ids = col_ref[0]
    for start in range(0, q_ref.shape[1], BLOCK):
        part = slice(start, start + BLOCK)
        seen = key_ids == row_ref[0, :, part]
        total = None
        for head, queries in enumerate(halves(q_ref[0, part, :] * scaling)):
            scores = jnp.where(seen, dot(keys_all, queries, BY_LAST), MASKED)
            highest = jnp.max(scores, axis=0, keepdims=True)
            weights = jnp.exp(scores - highest)
            sums = jnp.sum(weights, axis=0, keepdims=True)
            probs = (weights * (1.0 / sums)).astype(LOW)
            logsum_ref[0, 0, head : head + 1, part] = highest + jnp.log(sums)
            piece = dot(turned[head], probs, BY_ROWS)
            total = piece if total is None else total + piece
        context_ref[0, part, :] = total.T.astype(LOW)


def attend_back_kernel(
    q_ref, k_ref, v_ref, g_ref, logsum_ref, row_ref, col_ref, dq_ref, dk_ref, dv_ref, *, scaling
):
    keys_all = k_ref[0]
    values = v_ref[0]
    turned = [half.T for half in halves(keys_all)]
    key_ids = col_ref[0]
    length = q_ref.shape[1]
    key_grad = jnp.zeros((length, PAIR), WIDE)
    value_grad = jnp.zeros((length, PAIR), WIDE)
    for start in range(0, length, BLOCK):
        part = slice(start, start + BLOCK)
        seen = key_ids == row_ref[0, :, part]
        total = None
        queries_of = halves(q_ref[0, part, :] * scaling)
        grads_of = halves(g_ref[0, part, :])
        for head in range(2):
            queries, grads = queries_of[head], grads_of[head]
            scores = jnp.where(seen, dot(keys_all, queries, BY_LAST), MASKED)
            probs = jnp.exp(scores - logsum_ref[0, 0, head : head + 1, part])
            grad_probs = dot(values, grads, BY_LAST)
            value_grad = value_grad + dot(probs.astype(LOW), grads, BY_ROWS)
            level = jnp.sum(probs * grad_probs, axis=0, keepdims=True)
            grad_scores = (probs * (grad_probs - level)).astype(LOW)
            key_grad = key_grad + dot(grad_scores, queries, BY_ROWS)
            piece = dot(turned[head], grad_scores, BY_ROWS)
            total = piece if total is None else total + piece
        dq_ref[0, part, :] = (total.T * HDIM ** (-0.5)).astype(LOW)
    dk_ref[0] = key_grad.astype(LOW)
    dv_ref[0] = value_grad.astype(LOW)


def attention_specs(length, first=0):
    return (
        pl.BlockSpec((1, length, PAIR), lambda s, p: (s, 0, p + first)),
        pl.BlockSpec((1, 1, length), lambda s, p: (s, 0, 0)),
        pl.BlockSpec((1, length, 1), lambda s, p: (s, 0, 0)),
        pl.BlockSpec((1, 1, 2, length), lambda s, p: (s, p + first, 0, 0)),
    )


def attend(queries, keys_all, values, ids):
    count, length, width = queries.shape
    rows, as_row, as_col, sums = attention_specs(length)
    scaling = HDIM ** (-0.5)
    return pl.pallas_call(
        functools.partial(attend_kernel, scaling=scaling),
        grid=(count, width // PAIR),
        in_specs=[rows, rows, rows, as_row, as_col],
        out_specs=[rows, sums],
        out_shape=[
            jax.ShapeDtypeStruct(queries.shape, LOW),
            jax.ShapeDtypeStruct((count, width // PAIR, 2, length), WIDE),
        ],
        cost_estimate=pl.CostEstimate(
            flops=28 * count * width * length * length,
            transcendentals=count * width * length * length // HDIM,
            bytes_accessed=8 * count * width * length,
        ),
        name="attend",
    )(queries, keys_all, values, *ids)


def attend_back(queries, keys_all, values, grad_context, logsum, ids, earlier, part):
    count, length, width = queries.shape
    pairs = width // PAIR
    first = pairs // 2 * part
    rows, as_row, as_col, sums = attention_specs(length, first)
    body = functools.partial(attend_back_kernel, scaling=HDIM ** (-0.5))
    operands = [queries, keys_all, values, grad_context, logsum, *ids]
    in_specs = [rows, rows, rows, rows, sums, as_row, as_col]
    aliases = {}
    if earlier is not None:

        def body(*refs):
            attend_back_kernel(*refs[:7], *refs[10:], scaling=HDIM ** (-0.5))

        aliases = {7 + i: i for i in range(3)}
        operands += list(earlier)
        in_specs += [pl.BlockSpec(memory_space=pl.ANY)] * 3
    return pl.pallas_call(
        body,
        grid=(count, (pairs - first) if part else pairs // 2),
        in_specs=in_specs,
        out_specs=[rows, rows, rows],
        out_shape=[jax.ShapeDtypeStruct(queries.shape, LOW)] * 3,
        input_output_aliases=aliases,
        cost_estimate=pl.CostEstimate(
            flops=24 * count * width * length * length,
            transcendentals=count * width * length * length // HDIM // 2,
            bytes_accessed=7 * count * width * length,
        ),
        name="attend_back",
    )(*operands)


def meet(value, parts, picks):
    picked = [step for step in picks if step < len(parts)]
    value, held = lax.optimization_barrier((value, [parts[step] for step in picked]))
    parts = list(parts)
    for step, part in zip(picked, held):
        parts[step] = part
    return value, parts


def spread(block):
    members = lax.axis_size("tp")
    rank_pairs = [[(i, (i + step) % members) for i in range(members)] for step in range(1, members)]
    return [block] + [lax.ppermute(block, "tp", pairs) for pairs in rank_pairs]


def dealt(blocks):
    members, rank = lax.axis_size("tp"), lax.axis_index("tp")
    parts = []
    for step in range(members):
        block = lax.dynamic_slice_in_dim(blocks, (rank + step) % members, 1, 0)[0]
        pairs = [(i, (i + step) % members) for i in range(members)]
        parts.append(lax.ppermute(block, "tp", pairs) if step else block)
    return parts


def sent_back(parts):
    members = lax.axis_size("tp")
    moved = [parts[0]]
    for step in range(1, members):
        pairs = [(i, (i - step) % members) for i in range(members)]
        moved.append(lax.ppermute(parts[step], "tp", pairs))
    return moved


def by_source(moved):
    members, rank = len(moved), lax.axis_index("tp")
    shape = (members,) + moved[0].shape
    above = (lax.broadcasted_iota(jnp.int32, shape, 0) - rank) % members
    result = jnp.broadcast_to(moved[0][None], shape)
    for step in range(1, members):
        result = jnp.where(above == step, moved[step][None], result)
    return result


def flip(axis, members, bit, block):
    return lax.ppermute(block, axis, [(i, i ^ bit) for i in range(members)])


def beside(bit, block, other, place):
    mine = lax.axis_index("fsdp") // bit % 2
    shape = block.shape[:place] + (2,) + block.shape[place:]
    spot = lax.broadcasted_iota(jnp.int32, shape, place)
    return jnp.where(spot == mine, jnp.expand_dims(block, place), jnp.expand_dims(other, place))


def entries(bit, array, place):
    mine = lax.axis_index("fsdp") // bit % 2
    return [
        lax.squeeze(lax.dynamic_slice_in_dim(array, spot, 1, place), (place,)) for spot in (mine, 1 - mine)
    ]


def together(*groups):
    return lax.optimization_barrier(tuple(list(group) for group in groups))


def gather_rows(members, block, before, beyond, fillers):
    if members != 8:
        return lax.all_gather(block, "fsdp", axis=0, tiled=True), before, beyond, fillers
    rows, cols = block.shape
    first, second = block[:, : cols // 2], block[:, cols // 2 :]
    near = (flip("fsdp", members, 2, first), flip("fsdp", members, 4, second))
    near, beyond, fillers = together(near, beyond, fillers)
    first, second = beside(2, first, near[0], 0), beside(4, second, near[1], 0)
    far = (flip("fsdp", members, 4, first), flip("fsdp", members, 2, second))
    far, before[:3] = together(far, before[:3])
    both = jnp.concatenate([beside(4, first, far[0], 0), beside(2, second, far[1], 1)], axis=3)
    (other,), before[3:] = together((flip("fsdp", members, 1, both),), before[3:])
    return beside(1, both, other, 2).reshape(members * rows, cols), before, beyond, fillers


def add_low(kept, moved):
    return (kept.astype(WIDE) + moved.astype(WIDE)).astype(LOW)


def scatter_core(grad, others=()):
    if lax.axis_size("fsdp") != 8:
        return lax.psum_scatter(grad, "fsdp", scatter_dimension=0, tiled=True), others
    total_rows, cols = grad.shape
    kept, theirs = entries(1, grad.reshape(2, 2, 2, total_rows // 8, cols), 2)
    (moved,), others = together((flip("fsdp", 8, 1, theirs),), others)
    return add_low(kept, moved), others


def scatter_near(grad, others=()):
    if lax.axis_size("fsdp") != 8:
        return grad, others
    half = grad.shape[-1] // 2
    first, first_out = entries(4, grad[..., :half], 0)
    second, second_out = entries(2, grad[..., half:], 1)
    moved = (flip("fsdp", 8, 4, first_out), flip("fsdp", 8, 2, second_out))
    moved, others = together(moved, others)
    return (add_low(first, moved[0]), add_low(second, moved[1])), others


def scatter_far(grad, others=()):
    if lax.axis_size("fsdp") != 8:
        return grad, others
    first, first_out = entries(2, grad[0], 0)
    second, second_out = entries(4, grad[1], 0)
    moved = (flip("fsdp", 8, 2, first_out), flip("fsdp", 8, 4, second_out))
    moved, others = together(moved, others)
    return jnp.concatenate([add_low(first, moved[0]), add_low(second, moved[1])], axis=1), others


def total_over_tp(vector):
    bit = 1
    while bit < lax.axis_size("tp"):
        vector = vector + flip("tp", lax.axis_size("tp"), bit, vector)
        bit *= 2
    return vector


def total_over_fsdp(vector):
    bit = 1
    while bit < lax.axis_size("fsdp"):
        vector = vector + flip("fsdp", lax.axis_size("fsdp"), bit, vector)
        bit *= 2
    return vector


def normalize(token_rows):
    centred = token_rows - jnp.mean(token_rows, axis=-1, keepdims=True)
    scaling = lax.rsqrt(jnp.mean(centred * centred, axis=-1, keepdims=True) + EPSILON)
    return centred * scaling, scaling


def normalize_back(grad_rows, normed, scaling, gain_row):
    grad_normed = grad_rows * gain_row
    adjusted = grad_normed - jnp.mean(grad_normed, axis=-1, keepdims=True)
    adjusted = adjusted - normed * jnp.mean(grad_normed * normed, axis=-1, keepdims=True)
    return scaling * adjusted, jnp.sum(grad_rows * normed, axis=0), jnp.sum(grad_rows, axis=0)


def on_device(
    fsdp,
    tp,
    tokens,
    segment_ids,
    live_mask,
    query_weight,
    query_bias,
    key_weight,
    value_weight,
    value_bias,
    output_weight,
    output_bias,
    first_gain,
    first_shift,
    inner_weight,
    inner_bias,
    outer_weight,
    outer_bias,
    second_gain,
    second_shift,
    out_grad,
):
    sequences, places, width = tokens.shape
    count = sequences // tp
    length = places * tp
    rank = lax.axis_index("tp")
    head_cols = query_weight.shape[1]
    unit_cols = inner_weight.shape[1]
    shard_rows = query_weight.shape[0]

    def whole_rows(parts):
        return jnp.concatenate(parts, axis=1).reshape(count * length, width)

    def by_member(array):
        return array.reshape(tp, count, places, width)

    def to_owners(array):
        parts = array.reshape(count, tp, places, width)
        return sent_back([parts[:, step] for step in range(tp)])

    def own_places(parts):
        return by_source(parts).reshape(sequences, places, width)

    def columns(parts, widths):
        pieces, first = [], 0
        for cols in widths:
            pieces += [part[:shard_rows, first : first + cols] for part in parts]
            first += cols
        return jnp.concatenate(pieces, axis=1)

    def own_columns(share, widths):
        parts = []
        for step in range(tp):
            pieces, first = [], 0
            for cols in widths:
                pieces.append(share[:, first + step * cols : first + (step + 1) * cols])
                first += tp * cols
            parts.append(jnp.concatenate(pieces, axis=1))
        return sent_back(parts)

    def summed(parts, widths):
        total, first, pieces = sum(part.astype(WIDE) for part in parts), 0, []
        for cols in widths:
            pieces.append(total[:, first : first + cols])
            first += cols
        return pieces

    def by_rank(vector):
        parts = vector.reshape(tp, -1)
        parts = [lax.dynamic_slice_in_dim(parts, (rank - spot) % tp, 1, 0) for spot in range(tp)]
        return jnp.concatenate(parts, axis=0).reshape(-1)

    biases = jnp.concatenate([query_bias, value_bias, inner_bias]).reshape(-1, 4 * head_cols // 2)
    biases = jnp.pad(biases, ((0, 0), (0, 4 * head_cols - biases.shape[1])))
    heads = jnp.concatenate([query_weight, key_weight, value_weight, output_weight.T], axis=1)
    heads = spread(jnp.concatenate([heads, biases], axis=0))
    rest = jnp.concatenate([inner_weight, outer_weight.T], axis=1)
    rest, heads = meet(rest, heads, (1, 2, 3))
    rest = spread(rest)
    tokens, rest = meet(tokens, rest, (1,))
    rows = dealt(by_member(tokens))
    biases = [part[shard_rows:, : 2 * head_cols].reshape(-1).astype(WIDE) for part in heads]
    query_bias_full = jnp.concatenate([part[:head_cols] for part in biases])
    value_bias_full = jnp.concatenate([part[head_cols : 2 * head_cols] for part in biases])
    inner_bias_full = jnp.concatenate([part[2 * head_cols :] for part in biases])
    first = rank * count
    segment = lax.dynamic_slice_in_dim(segment_ids, first, count, 0)
    live = lax.dynamic_slice_in_dim(live_mask, first, count, 0)
    spots = lax.broadcasted_iota(jnp.int32, segment.shape, 1)
    ids = jnp.where(live == 1, segment, length + spots).reshape(count, tp, places)
    ids = [lax.dynamic_slice_in_dim(ids, (rank - step) % tp, 1, 1) for step in range(tp)]
    ids = jnp.concatenate(ids, axis=1).reshape(count, length)
    ids = (ids[:, None, :], ids[:, :, None])
    fillers = (*ids, query_bias_full, value_bias_full, inner_bias_full)
    heads, rows, rest, fillers = gather_rows(
        fsdp, columns(heads, (head_cols,) * 4), rows, rest, fillers
    )
    *ids, query_bias_full, value_bias_full, inner_bias_full = fillers
    query_full, key_full, value_full, output_turned = (
        heads[:, i * width : (i + 1) * width] for i in range(4)
    )
    rows = whole_rows(rows)
    rows, out_grad = lax.optimization_barrier((rows, out_grad))
    rest = lax.all_gather(columns(rest, (unit_cols, unit_cols)), "fsdp", axis=0, tiled=True)
    inner_full, outer_turned = rest[:, : tp * unit_cols], rest[:, tp * unit_cols :]

    shape = (count, length, width)
    queries = (dot(rows, query_full, BY_ROWS) + query_bias_full).astype(LOW).reshape(shape)
    keys_all = dot(rows, key_full, BY_ROWS).astype(LOW).reshape(shape)
    values = (dot(rows, value_full, BY_ROWS) + value_bias_full).astype(LOW).reshape(shape)
    context, logsum = attend(queries, keys_all, values, ids)
    context, grad_out = meet(context, dealt(by_member(out_grad)), (2,))
    context = context.reshape(count * length, width)
    mixed = dot(context, output_turned, BY_LAST) + output_bias.astype(WIDE)
    first_normed, first_scaling = normalize(rows.astype(WIDE) + mixed)
    first_rows = first_normed * first_gain.astype(WIDE) + first_shift.astype(WIDE)
    first_low = first_rows.astype(LOW)
    preactivation = dot(first_low, inner_full, BY_ROWS) + inner_bias_full
    cumulative = 0.5 * (1.0 + lax.erf(preactivation * 0.7071067811865476))
    activation_rows = (preactivation * cumulative).astype(LOW)
    density = jnp.exp(-0.5 * preactivation * preactivation) * 0.3989422804014327
    slope = cumulative + preactivation * density
    activation_rows, grad_out = meet(activation_rows, grad_out, (1, 3))
    branch = dot(activation_rows, outer_turned, BY_LAST)
    second_normed, second_scaling = normalize(first_rows + branch + outer_bias.astype(WIDE))
    second_rows = second_normed * second_gain.astype(WIDE) + second_shift.astype(WIDE)
    layer_out = to_owners(second_rows.astype(LOW))

    grad_out = whole_rows(grad_out).astype(WIDE)
    grad_second, second_gain_grad, second_shift_grad = normalize_back(
        grad_out, second_normed, second_scaling, second_gain.astype(WIDE)
    )
    outer_bias_grad = jnp.sum(grad_second, axis=0)
    grad_branch = grad_second.astype(LOW)
    outer_grad = dot(grad_branch, activation_rows, BY_FIRST).astype(LOW)
    outer_share = lax.psum_scatter(outer_grad, "fsdp", scatter_dimension=0, tiled=True)
    grad_activ = dot(grad_branch, outer_turned, BY_ROWS)
    grad_pre = (grad_activ * slope).astype(LOW)
    inner_bias_grad = jnp.sum(grad_pre.astype(WIDE), axis=0)
    inner_share, layer_out[:3] = scatter_core(
        dot(first_low, grad_pre, BY_FIRST).astype(LOW), layer_out[:3]
    )
    grad_first = grad_second + dot(grad_pre, inner_full, BY_LAST)
    grad_mixed, first_gain_grad, first_shift_grad = normalize_back(
        grad_first, first_normed, first_scaling, first_gain.astype(WIDE)
    )
    output_bias_grad = jnp.sum(grad_mixed, axis=0)
    grad_mixed_low = grad_mixed.astype(LOW)
    output_grad = dot(grad_mixed_low, context, BY_FIRST).astype(LOW)
    grad_context = dot(grad_mixed_low, output_turned, BY_ROWS).astype(LOW).reshape(shape)
    early = total_over_tp(
        jnp.concatenate(
            [
                output_bias_grad,
                first_gain_grad,
                first_shift_grad,
                outer_bias_grad,
                second_gain_grad,
                second_shift_grad,
                by_rank(inner_bias_grad),
            ]
        )
    )
    grad_context, inner_share, output_grad, layer_out, early = lax.optimization_barrier(
        (grad_context, scatter_near(inner_share)[0], output_grad, layer_out, early)
    )
    early = total_over_fsdp(early)
    inner_share, _ = scatter_far(inner_share)
    back = functools.partial(attend_back, queries, keys_all, values, grad_context, logsum, ids)
    halfway = back(None, 0)
    halfway, inner_share, outer_share, early = lax.optimization_barrier(
        (halfway, inner_share, outer_share, early)
    )
    layer_out = own_places(layer_out)
    inner_parts = own_columns(inner_share, (unit_cols,))
    outer_parts = own_columns(outer_share, (unit_cols,))
    rows_grads = back(halfway, 1)
    rows_grads, inner_parts, outer_parts = lax.optimization_barrier(
        (rows_grads, inner_parts, outer_parts)
    )
    (inner_share,) = summed(inner_parts, (unit_cols,))
    (outer_share,) = summed(outer_parts, (unit_cols,))
    query_rows_grad, key_rows_grad, value_rows_grad = (
        array.reshape(count * length, width) for array in rows_grads
    )
    head_grads = [
        dot(rows, grad, BY_FIRST).astype(LOW)
        for grad in (query_rows_grad, key_rows_grad, value_rows_grad)
    ]
    tokens_grad = (
        grad_mixed
        + dot(query_rows_grad, query_full, BY_LAST)
        + dot(key_rows_grad, key_full, BY_LAST)
        + dot(value_rows_grad, value_full, BY_LAST)
    ).astype(LOW)
    late = [by_rank(jnp.sum(grad.astype(WIDE), axis=0)) for grad in (query_rows_grad, value_rows_grad)]
    heads_share, (tokens_grad, late) = scatter_core(
        jnp.concatenate(head_grads + [output_grad], axis=1), (tokens_grad, jnp.concatenate(late))
    )
    tokens_grad = to_owners(tokens_grad)
    late = late + flip("fsdp", fsdp, 1, late) if fsdp == 8 else lax.psum(late, "fsdp")
    heads_share, tokens_grad[:3] = scatter_near(heads_share, tokens_grad[:3])
    late = late + flip("fsdp", fsdp, 2, late) if fsdp == 8 else late
    heads_share, tokens_grad[3:] = scatter_far(heads_share, tokens_grad[3:])
    late = late + flip("fsdp", fsdp, 4, late) if fsdp == 8 else late
    late = spread(late)
    late = jnp.sum(by_source(late[:1] + late[:0:-1]), axis=0)
    query_share, key_share, value_share, output_share = summed(
        own_columns(heads_share, (head_cols,) * 4), (head_cols,) * 4
    )
    tokens_grad = own_places(tokens_grad).astype(WIDE)
    totals = jnp.concatenate([early[: 6 * width], late, early[6 * width :]])
    rowwise = [totals[i * width : (i + 1) * width] for i in range(6)]
    query_bias_total = lax.dynamic_slice_in_dim(totals, 6 * width + rank * head_cols, head_cols)
    value_bias_total = lax.dynamic_slice_in_dim(totals, 7 * width + rank * head_cols, head_cols)
    inner_bias_total = lax.dynamic_slice_in_dim(totals, 8 * width + rank * unit_cols, unit_cols)
    return (
        layer_out,
        tokens_grad,
        query_share,
        query_bias_total,
        key_share,
        value_share,
        value_bias_total,
        output_share.T,
        rowwise[0],
        rowwise[1],
        rowwise[2],
        inner_share,
        inner_bias_total,
        outer_share.T,
        rowwise[3],
        rowwise[4],
        rowwise[5],
    )


def solution(mesh):
    split = P("fsdp", "tp", None)
    across, turned = P("fsdp", "tp"), P("tp", "fsdp")
    seqs, units, copied = P("fsdp", None), P("tp"), P()
    return jax.shard_map(
        functools.partial(on_device, mesh.shape["fsdp"], mesh.shape["tp"]),
        mesh=mesh,
        in_specs=(
            split,
            seqs,
            seqs,
            across,
            units,
            across,
            across,
            units,
            turned,
            copied,
            copied,
            copied,
            across,
            units,
            turned,
            copied,
            copied,
            copied,
            split,
        ),
        out_specs=(
            split,
            split,
            across,
            units,
            across,
            across,
            units,
            turned,
            copied,
            copied,
            copied,
            across,
            units,
            turned,
            copied,
            copied,
            copied,
        ),
        check_vma=False,
    )
```

```python
import functools

import jax
import jax.numpy as jnp
from jax import lax
from jax.experimental import pallas as pl
from jax.sharding import PartitionSpec as P

HDIM = 64
EPSILON = 1e-12
MASKED = -1000000000.0
PAIR = 2 * HDIM
BLOCK = 256
LOW = jnp.bfloat16
WIDE = jnp.float32
BY_LAST = (((1,), (1,)), ((), ()))
BY_ROWS = (((1,), (0,)), ((), ()))
BY_FIRST = (((0,), (0,)), ((), ()))


def dot(left, right, dims):
    return lax.dot_general(left, right, dims, preferred_element_type=WIDE)


def halves(pair, fill=0):
    lane = lax.broadcasted_iota(jnp.int32, (1, PAIR), 1)
    other = jnp.full((), fill, pair.dtype)
    return jnp.where(lane < HDIM, pair, other), jnp.where(lane < HDIM, other, pair)


def attend_kernel(q_ref, k_ref, v_ref, row_ref, col_ref, context_ref, logsum_ref, *, scaling):
    keys_all = k_ref[0]
    turned = [half.T for half in halves(v_ref[0], 1)]
    seen = col_ref[0] == row_ref[0]
    pieces = []
    for head, queries in enumerate(halves(q_ref[0] * scaling)):
        scores = jnp.where(seen, dot(keys_all, queries, BY_LAST), MASKED)
        highest = jnp.max(scores, axis=0, keepdims=True)
        piece = dot(turned[head], jnp.exp(scores - highest).astype(LOW), BY_ROWS)
        mine, ones = (piece[:HDIM], piece[HDIM:]) if head == 0 else (piece[HDIM:], piece[:HDIM])
        sums = ones[:1]
        logsum_ref[0, 0, head : head + 1, :] = highest + jnp.log(sums)
        pieces.append(mine * (1.0 / sums))
    context_ref[0] = jnp.concatenate(pieces, axis=0).T.astype(LOW)


def attend_back_kernel(
    q_ref, k_ref, v_ref, g_ref, c_ref, logsum_ref, row_ref, col_ref, dq_ref, dk_ref, dv_ref, *, scaling
):
    keys_all = k_ref[0]
    values = v_ref[0]
    turned = [half.T for half in halves(keys_all)]
    key_ids = col_ref[0]
    length = q_ref.shape[1]
    key_grad = jnp.zeros((length, PAIR), WIDE)
    value_grad = jnp.zeros((length, PAIR), WIDE)
    for start in range(0, length, BLOCK):
        part = slice(start, start + BLOCK)
        seen = key_ids == row_ref[0, :, part]
        total = None
        queries_of = halves(q_ref[0, part, :] * scaling)
        grads_of = halves(g_ref[0, part, :])
        products = g_ref[0, part, :].astype(WIDE).T * c_ref[0, part, :].astype(WIDE).T
        for head in range(2):
            queries, grads = queries_of[head], grads_of[head]
            level = jnp.sum(products[head * HDIM : (head + 1) * HDIM], axis=0, keepdims=True)
            scores = jnp.where(seen, dot(keys_all, queries, BY_LAST), MASKED)
            probs = jnp.exp(scores - logsum_ref[0, 0, head : head + 1, part])
            grad_probs = dot(values, grads, BY_LAST)
            value_grad = value_grad + dot(probs.astype(LOW), grads, BY_ROWS)
            grad_scores = (probs * (grad_probs - level)).astype(LOW)
            key_grad = key_grad + dot(grad_scores, queries, BY_ROWS)
            piece = dot(turned[head], grad_scores, BY_ROWS)
            total = piece if total is None else total + piece
        dq_ref[0, part, :] = (total.T * HDIM ** (-0.5)).astype(LOW)
    dk_ref[0] = key_grad.astype(LOW)
    dv_ref[0] = value_grad.astype(LOW)


def attention_specs(length, first=0):
    return (
        pl.BlockSpec((1, length, PAIR), lambda s, p: (s, 0, p + first)),
        pl.BlockSpec((1, 1, length), lambda s, p: (s, 0, 0)),
        pl.BlockSpec((1, length, 1), lambda s, p: (s, 0, 0)),
        pl.BlockSpec((1, 1, 2, length), lambda s, p: (s, p + first, 0, 0)),
    )


def attend(queries, keys_all, values, ids):
    count, length, width = queries.shape
    rows, as_row, as_col, sums = attention_specs(length)
    scaling = HDIM ** (-0.5)
    return pl.pallas_call(
        functools.partial(attend_kernel, scaling=scaling),
        grid=(count, width // PAIR),
        in_specs=[rows, rows, rows, as_row, as_col],
        out_specs=[rows, sums],
        out_shape=[
            jax.ShapeDtypeStruct(queries.shape, LOW),
            jax.ShapeDtypeStruct((count, width // PAIR, 2, length), WIDE),
        ],
        cost_estimate=pl.CostEstimate(
            flops=28 * count * width * length * length,
            transcendentals=count * width * length * length // HDIM,
            bytes_accessed=8 * count * width * length,
        ),
        name="attend",
    )(queries, keys_all, values, *ids)


def attend_back(queries, keys_all, values, grad_context, context, logsum, ids, earlier, part):
    count, length, width = queries.shape
    pairs = width // PAIR
    first = pairs // 2 * part
    rows, as_row, as_col, sums = attention_specs(length, first)
    body = functools.partial(attend_back_kernel, scaling=HDIM ** (-0.5))
    operands = [queries, keys_all, values, grad_context, context, logsum, *ids]
    in_specs = [rows] * 5 + [sums, as_row, as_col]
    aliases = {}
    if earlier is not None:

        def body(*refs):
            attend_back_kernel(*refs[:8], *refs[11:], scaling=HDIM ** (-0.5))

        aliases = {8 + i: i for i in range(3)}
        operands += list(earlier)
        in_specs += [pl.BlockSpec(memory_space=pl.ANY)] * 3
    return pl.pallas_call(
        body,
        grid=(count, (pairs - first) if part else pairs // 2),
        in_specs=in_specs,
        out_specs=[rows, rows, rows],
        out_shape=[jax.ShapeDtypeStruct(queries.shape, LOW)] * 3,
        input_output_aliases=aliases,
        cost_estimate=pl.CostEstimate(
            flops=24 * count * width * length * length,
            transcendentals=count * width * length * length // HDIM // 2,
            bytes_accessed=7 * count * width * length,
        ),
        name="attend_back",
    )(*operands)


def meet(value, parts, picks):
    picked = [step for step in picks if step < len(parts)]
    value, held = lax.optimization_barrier((value, [parts[step] for step in picked]))
    parts = list(parts)
    for step, part in zip(picked, held):
        parts[step] = part
    return value, parts


def spread(block):
    members = lax.axis_size("tp")
    rank_pairs = [[(i, (i + step) % members) for i in range(members)] for step in range(1, members)]
    return [block] + [lax.ppermute(block, "tp", pairs) for pairs in rank_pairs]


def dealt(blocks):
    members, rank = lax.axis_size("tp"), lax.axis_index("tp")
    parts = []
    for step in range(members):
        block = lax.dynamic_slice_in_dim(blocks, (rank + step) % members, 1, 0)[0]
        pairs = [(i, (i + step) % members) for i in range(members)]
        parts.append(lax.ppermute(block, "tp", pairs) if step else block)
    return parts


def sent_back(parts):
    members = lax.axis_size("tp")
    moved = [parts[0]]
    for step in range(1, members):
        pairs = [(i, (i - step) % members) for i in range(members)]
        moved.append(lax.ppermute(parts[step], "tp", pairs))
    return moved


def by_source(moved):
    members, rank = len(moved), lax.axis_index("tp")
    shape = (members,) + moved[0].shape
    above = (lax.broadcasted_iota(jnp.int32, shape, 0) - rank) % members
    result = jnp.broadcast_to(moved[0][None], shape)
    for step in range(1, members):
        result = jnp.where(above == step, moved[step][None], result)
    return result


def flip(axis, members, bit, block):
    return lax.ppermute(block, axis, [(i, i ^ bit) for i in range(members)])


def beside(bit, block, other, place):
    mine = lax.axis_index("fsdp") // bit % 2
    shape = block.shape[:place] + (2,) + block.shape[place:]
    spot = lax.broadcasted_iota(jnp.int32, shape, place)
    return jnp.where(spot == mine, jnp.expand_dims(block, place), jnp.expand_dims(other, place))


def entries(bit, array, place):
    mine = lax.axis_index("fsdp") // bit % 2
    return [
        lax.squeeze(lax.dynamic_slice_in_dim(array, spot, 1, place), (place,)) for spot in (mine, 1 - mine)
    ]


def together(*groups):
    return lax.optimization_barrier(tuple(list(group) for group in groups))


def gather_rows(members, block, before, beyond, fillers):
    if members != 8:
        return lax.all_gather(block, "fsdp", axis=0, tiled=True), before, beyond, fillers
    rows, cols = block.shape
    first, second = block[:, : cols // 2], block[:, cols // 2 :]
    near = (flip("fsdp", members, 2, first), flip("fsdp", members, 4, second))
    near, beyond, fillers = together(near, beyond, fillers)
    first, second = beside(2, first, near[0], 0), beside(4, second, near[1], 0)
    far = (flip("fsdp", members, 4, first), flip("fsdp", members, 2, second))
    far, before[:3] = together(far, before[:3])
    both = jnp.concatenate([beside(4, first, far[0], 0), beside(2, second, far[1], 1)], axis=3)
    (other,), before[3:] = together((flip("fsdp", members, 1, both),), before[3:])
    return beside(1, both, other, 2).reshape(members * rows, cols), before, beyond, fillers


def add_low(kept, moved):
    return (kept.astype(WIDE) + moved.astype(WIDE)).astype(LOW)


def scatter_core(grad, others=()):
    if lax.axis_size("fsdp") != 8:
        return lax.psum_scatter(grad, "fsdp", scatter_dimension=0, tiled=True), others
    total_rows, cols = grad.shape
    kept, theirs = entries(1, grad.reshape(2, 2, 2, total_rows // 8, cols), 2)
    (moved,), others = together((flip("fsdp", 8, 1, theirs),), others)
    return add_low(kept, moved), others


def scatter_near(grad, others=()):
    if lax.axis_size("fsdp") != 8:
        return grad, others
    half = grad.shape[-1] // 2
    first, first_out = entries(4, grad[..., :half], 0)
    second, second_out = entries(2, grad[..., half:], 1)
    moved = (flip("fsdp", 8, 4, first_out), flip("fsdp", 8, 2, second_out))
    moved, others = together(moved, others)
    return (add_low(first, moved[0]), add_low(second, moved[1])), others


def scatter_far(grad, others=()):
    if lax.axis_size("fsdp") != 8:
        return grad, others
    first, first_out = entries(2, grad[0], 0)
    second, second_out = entries(4, grad[1], 0)
    moved = (flip("fsdp", 8, 2, first_out), flip("fsdp", 8, 4, second_out))
    moved, others = together(moved, others)
    return jnp.concatenate([add_low(first, moved[0]), add_low(second, moved[1])], axis=1), others


def normalize(token_rows):
    centred = token_rows - jnp.mean(token_rows, axis=-1, keepdims=True)
    scaling = lax.rsqrt(jnp.mean(centred * centred, axis=-1, keepdims=True) + EPSILON)
    return centred * scaling, scaling


def normalize_back(grad_rows, normed, scaling, gain_row):
    grad_normed = grad_rows * gain_row
    adjusted = grad_normed - jnp.mean(grad_normed, axis=-1, keepdims=True)
    adjusted = adjusted - normed * jnp.mean(grad_normed * normed, axis=-1, keepdims=True)
    return scaling * adjusted, jnp.sum(grad_rows * normed, axis=0), jnp.sum(grad_rows, axis=0)


def on_device(
    fsdp,
    tp,
    tokens,
    segment_ids,
    live_mask,
    query_weight,
    query_bias,
    key_weight,
    value_weight,
    value_bias,
    output_weight,
    output_bias,
    first_gain,
    first_shift,
    inner_weight,
    inner_bias,
    outer_weight,
    outer_bias,
    second_gain,
    second_shift,
    out_grad,
):
    sequences, places, width = tokens.shape
    count = sequences // tp
    length = places * tp
    rank = lax.axis_index("tp")
    head_cols = query_weight.shape[1]
    unit_cols = inner_weight.shape[1]
    shard_rows = query_weight.shape[0]

    def whole_rows(parts):
        return jnp.concatenate(parts, axis=1).reshape(count * length, width)

    def by_member(array):
        return array.reshape(tp, count, places, width)

    def to_owners(array):
        parts = array.reshape(count, tp, places, width)
        return sent_back([parts[:, step] for step in range(tp)])

    def own_places(parts):
        return by_source(parts).reshape(sequences, places, width)

    def columns(parts, widths):
        pieces, first = [], 0
        for cols in widths:
            pieces += [part[:shard_rows, first : first + cols] for part in parts]
            first += cols
        return jnp.concatenate(pieces, axis=1)

    def own_columns(share, widths):
        parts = []
        for step in range(tp):
            pieces, first = [], 0
            for cols in widths:
                pieces.append(share[:, first + step * cols : first + (step + 1) * cols])
                first += tp * cols
            parts.append(jnp.concatenate(pieces, axis=1))
        return sent_back(parts)

    def summed(parts, widths):
        total, first, pieces = sum(part.astype(WIDE) for part in parts), 0, []
        for cols in widths:
            pieces.append(total[:, first : first + cols])
            first += cols
        return pieces

    def by_rank(vector):
        parts = vector.reshape(tp, -1)
        parts = [lax.dynamic_slice_in_dim(parts, (rank - spot) % tp, 1, 0) for spot in range(tp)]
        return jnp.concatenate(parts, axis=0).reshape(-1)

    biases = jnp.concatenate([query_bias, value_bias, inner_bias]).reshape(-1, 4 * head_cols // 2)
    biases = jnp.pad(biases, ((0, 0), (0, 4 * head_cols - biases.shape[1])))
    heads = jnp.concatenate([query_weight, key_weight, value_weight, output_weight.T], axis=1)
    heads = spread(jnp.concatenate([heads, biases], axis=0))
    rest = jnp.concatenate([inner_weight, outer_weight.T], axis=1)
    rest, heads = meet(rest, heads, (1, 2, 3))
    rest = spread(rest)
    tokens, rest = meet(tokens, rest, (1,))
    rows = dealt(by_member(tokens))
    biases = [part[shard_rows:, : 2 * head_cols].reshape(-1).astype(WIDE) for part in heads]
    query_bias_full = jnp.concatenate([part[:head_cols] for part in biases])
    value_bias_full = jnp.concatenate([part[head_cols : 2 * head_cols] for part in biases])
    inner_bias_full = jnp.concatenate([part[2 * head_cols :] for part in biases])
    first = rank * count
    segment = lax.dynamic_slice_in_dim(segment_ids, first, count, 0)
    live = lax.dynamic_slice_in_dim(live_mask, first, count, 0)
    spots = lax.broadcasted_iota(jnp.int32, segment.shape, 1)
    ids = jnp.where(live == 1, segment, length + spots).reshape(count, tp, places)
    ids = [lax.dynamic_slice_in_dim(ids, (rank - step) % tp, 1, 1) for step in range(tp)]
    ids = jnp.concatenate(ids, axis=1).reshape(count, length)
    ids = (ids[:, None, :], ids[:, :, None])
    fillers = (*ids, query_bias_full, value_bias_full, inner_bias_full)
    heads, rows, rest, fillers = gather_rows(
        fsdp, columns(heads, (head_cols,) * 4), rows, rest, fillers
    )
    *ids, query_bias_full, value_bias_full, inner_bias_full = fillers
    query_full, key_full, value_full, output_turned = (
        heads[:, i * width : (i + 1) * width] for i in range(4)
    )
    rows = whole_rows(rows)
    rows, out_grad = lax.optimization_barrier((rows, out_grad))
    rest = lax.all_gather(columns(rest, (unit_cols, unit_cols)), "fsdp", axis=0, tiled=True)
    inner_full, outer_turned = rest[:, : tp * unit_cols], rest[:, tp * unit_cols :]

    shape = (count, length, width)
    queries = (dot(rows, query_full, BY_ROWS) + query_bias_full).astype(LOW).reshape(shape)
    keys_all = dot(rows, key_full, BY_ROWS).astype(LOW).reshape(shape)
    values = (dot(rows, value_full, BY_ROWS) + value_bias_full).astype(LOW).reshape(shape)
    context, logsum = attend(queries, keys_all, values, ids)
    context, grad_out = meet(context, dealt(by_member(out_grad)), (2,))
    context = context.reshape(count * length, width)
    mixed = dot(context, output_turned, BY_LAST) + output_bias.astype(WIDE)
    first_normed, first_scaling = normalize(rows.astype(WIDE) + mixed)
    first_rows = first_normed * first_gain.astype(WIDE) + first_shift.astype(WIDE)
    first_low = first_rows.astype(LOW)
    preactivation = dot(first_low, inner_full, BY_ROWS) + inner_bias_full
    cumulative = 0.5 * (1.0 + lax.erf(preactivation * 0.7071067811865476))
    activation_rows = (preactivation * cumulative).astype(LOW)
    density = jnp.exp(-0.5 * preactivation * preactivation) * 0.3989422804014327
    slope = cumulative + preactivation * density
    activation_rows, grad_out = meet(activation_rows, grad_out, (1, 3))
    branch = dot(activation_rows, outer_turned, BY_LAST)
    second_normed, second_scaling = normalize(first_rows + branch + outer_bias.astype(WIDE))
    second_rows = second_normed * second_gain.astype(WIDE) + second_shift.astype(WIDE)
    layer_out = to_owners(second_rows.astype(LOW))

    grad_out = whole_rows(grad_out).astype(WIDE)
    grad_second, second_gain_grad, second_shift_grad = normalize_back(
        grad_out, second_normed, second_scaling, second_gain.astype(WIDE)
    )
    outer_bias_grad = jnp.sum(grad_second, axis=0)
    grad_branch = grad_second.astype(LOW)
    outer_grad = dot(grad_branch, activation_rows, BY_FIRST).astype(LOW)
    outer_share = lax.psum_scatter(outer_grad, "fsdp", scatter_dimension=0, tiled=True)
    grad_activ = dot(grad_branch, outer_turned, BY_ROWS)
    grad_pre = (grad_activ * slope).astype(LOW)
    inner_bias_grad = jnp.sum(grad_pre.astype(WIDE), axis=0)
    inner_share, layer_out[:3] = scatter_core(
        dot(first_low, grad_pre, BY_FIRST).astype(LOW), layer_out[:3]
    )
    grad_first = grad_second + dot(grad_pre, inner_full, BY_LAST)
    grad_mixed, first_gain_grad, first_shift_grad = normalize_back(
        grad_first, first_normed, first_scaling, first_gain.astype(WIDE)
    )
    output_bias_grad = jnp.sum(grad_mixed, axis=0)
    grad_mixed_low = grad_mixed.astype(LOW)
    output_grad = dot(grad_mixed_low, context, BY_FIRST).astype(LOW)
    grad_context = dot(grad_mixed_low, output_turned, BY_ROWS).astype(LOW).reshape(shape)
    grad_context, inner_share, output_grad, layer_out = lax.optimization_barrier(
        (grad_context, scatter_near(inner_share)[0], output_grad, layer_out)
    )
    inner_share, _ = scatter_far(inner_share)
    back = functools.partial(
        attend_back, queries, keys_all, values, grad_context, context.reshape(shape), logsum, ids
    )
    halfway = back(None, 0)
    halfway, inner_share, outer_share = lax.optimization_barrier(
        (halfway, inner_share, outer_share)
    )
    layer_out = own_places(layer_out)
    units = (unit_cols, unit_cols)
    unit_parts = own_columns(jnp.concatenate([inner_share, outer_share], axis=1), units)
    rows_grads, unit_parts = lax.optimization_barrier((back(halfway, 1), unit_parts))
    inner_share, outer_share = summed(unit_parts, units)
    query_rows_grad, key_rows_grad, value_rows_grad = (
        array.reshape(count * length, width) for array in rows_grads
    )
    head_grads = [
        dot(rows, grad, BY_FIRST).astype(LOW)
        for grad in (query_rows_grad, key_rows_grad, value_rows_grad)
    ]
    tokens_grad = (
        grad_mixed
        + dot(query_rows_grad, query_full, BY_LAST)
        + dot(key_rows_grad, key_full, BY_LAST)
        + dot(value_rows_grad, value_full, BY_LAST)
    ).astype(LOW)
    vectors = [
        output_bias_grad,
        first_gain_grad,
        first_shift_grad,
        outer_bias_grad,
        second_gain_grad,
        second_shift_grad,
        by_rank(jnp.sum(query_rows_grad.astype(WIDE), axis=0)),
        by_rank(jnp.sum(value_rows_grad.astype(WIDE), axis=0)),
        by_rank(inner_bias_grad),
    ]
    vectors = jnp.concatenate(vectors).reshape(-1, 128)
    vectors = lax.all_gather(vectors, ("tp", "fsdp"), axis=0)
    heads_share, (tokens_grad,) = scatter_core(
        jnp.concatenate(head_grads + [output_grad], axis=1), (tokens_grad,)
    )
    tokens_grad = to_owners(tokens_grad)
    heads_share, tokens_grad[:3] = scatter_near(heads_share, tokens_grad[:3])
    heads_share, tokens_grad[3:] = scatter_far(heads_share, tokens_grad[3:])
    heads_share, vectors = lax.optimization_barrier((heads_share, vectors))
    totals = jnp.sum(vectors, axis=0).reshape(-1)
    query_share, key_share, value_share, output_share = summed(
        own_columns(heads_share, (head_cols,) * 4), (head_cols,) * 4
    )
    tokens_grad = own_places(tokens_grad).astype(WIDE)
    rowwise = [totals[i * width : (i + 1) * width] for i in range(6)]
    query_bias_total = lax.dynamic_slice_in_dim(totals, 6 * width + rank * head_cols, head_cols)
    value_bias_total = lax.dynamic_slice_in_dim(totals, 7 * width + rank * head_cols, head_cols)
    inner_bias_total = lax.dynamic_slice_in_dim(totals, 8 * width + rank * unit_cols, unit_cols)
    return (
        layer_out,
        tokens_grad,
        query_share,
        query_bias_total,
        key_share,
        value_share,
        value_bias_total,
        output_share.T,
        rowwise[0],
        rowwise[1],
        rowwise[2],
        inner_share,
        inner_bias_total,
        outer_share.T,
        rowwise[3],
        rowwise[4],
        rowwise[5],
    )


def solution(mesh):
    split = P("fsdp", "tp", None)
    across, turned = P("fsdp", "tp"), P("tp", "fsdp")
    seqs, units, copied = P("fsdp", None), P("tp"), P()
    return jax.shard_map(
        functools.partial(on_device, mesh.shape["fsdp"], mesh.shape["tp"]),
        mesh=mesh,
        in_specs=(
            split,
            seqs,
            seqs,
            across,
            units,
            across,
            across,
            units,
            turned,
            copied,
            copied,
            copied,
            across,
            units,
            turned,
            copied,
            copied,
            copied,
            split,
        ),
        out_specs=(
            split,
            split,
            across,
            units,
            across,
            across,
            units,
            turned,
            copied,
            copied,
            copied,
            across,
            units,
            turned,
            copied,
            copied,
            copied,
        ),
        check_vma=False,
    )
```

```python
import functools

import jax
import jax.numpy as jnp
from jax import lax
from jax.experimental import pallas as pl
from jax.sharding import PartitionSpec as P

HDIM = 64
EPSILON = 1e-12
MASKED = -1000000000.0
PAIR = 2 * HDIM
BLOCK = 256
LOW = jnp.bfloat16
WIDE = jnp.float32
BY_LAST = (((1,), (1,)), ((), ()))
BY_ROWS = (((1,), (0,)), ((), ()))
BY_FIRST = (((0,), (0,)), ((), ()))


def dot(left, right, dims):
    return lax.dot_general(left, right, dims, preferred_element_type=WIDE)


def halves(pair, fill=0):
    lane = lax.broadcasted_iota(jnp.int32, (1, PAIR), 1)
    other = jnp.full((), fill, pair.dtype)
    return jnp.where(lane < HDIM, pair, other), jnp.where(lane < HDIM, other, pair)


def attend_kernel(q_ref, k_ref, v_ref, row_ref, col_ref, context_ref, logsum_ref, *, scaling):
    keys_all = k_ref[0]
    turned = [half.T for half in halves(v_ref[0], 1)]
    seen = col_ref[0] == row_ref[0]
    pieces = []
    for head, queries in enumerate(halves(q_ref[0] * scaling)):
        scores = jnp.where(seen, dot(keys_all, queries, BY_LAST), MASKED)
        highest = jnp.max(scores, axis=0, keepdims=True)
        piece = dot(turned[head], jnp.exp(scores - highest).astype(LOW), BY_ROWS)
        mine, ones = (piece[:HDIM], piece[HDIM:]) if head == 0 else (piece[HDIM:], piece[:HDIM])
        sums = ones[:1]
        logsum_ref[0, 0, head : head + 1, :] = highest + jnp.log(sums)
        pieces.append(mine * (1.0 / sums))
    context_ref[0] = jnp.concatenate(pieces, axis=0).T.astype(LOW)


def attend_back_kernel(
    q_ref, k_ref, v_ref, g_ref, c_ref, logsum_ref, row_ref, col_ref, dq_ref, dk_ref, dv_ref, *, scaling
):
    keys_all = k_ref[0]
    values = v_ref[0]
    turned = [half.T for half in halves(keys_all)]
    key_ids = col_ref[0]
    length = q_ref.shape[1]
    key_grad = jnp.zeros((length, PAIR), WIDE)
    value_grad = jnp.zeros((length, PAIR), WIDE)
    for start in range(0, length, BLOCK):
        part = slice(start, start + BLOCK)
        seen = key_ids == row_ref[0, :, part]
        total = None
        queries_of = halves(q_ref[0, part, :] * scaling)
        grads_of = halves(g_ref[0, part, :])
        products = g_ref[0, part, :].astype(WIDE).T * c_ref[0, part, :].astype(WIDE).T
        for head in range(2):
            queries, grads = queries_of[head], grads_of[head]
            level = jnp.sum(products[head * HDIM : (head + 1) * HDIM], axis=0, keepdims=True)
            scores = jnp.where(seen, dot(keys_all, queries, BY_LAST), MASKED)
            probs = jnp.exp(scores - logsum_ref[0, 0, head : head + 1, part])
            grad_probs = dot(values, grads, BY_LAST)
            value_grad = value_grad + dot(probs.astype(LOW), grads, BY_ROWS)
            grad_scores = (probs * (grad_probs - level)).astype(LOW)
            key_grad = key_grad + dot(grad_scores, queries, BY_ROWS)
            piece = dot(turned[head], grad_scores, BY_ROWS)
            total = piece if total is None else total + piece
        dq_ref[0, part, :] = (total.T * HDIM ** (-0.5)).astype(LOW)
    dk_ref[0] = key_grad.astype(LOW)
    dv_ref[0] = value_grad.astype(LOW)


def attention_specs(length, first=0):
    return (
        pl.BlockSpec((1, length, PAIR), lambda s, p: (s, 0, p + first)),
        pl.BlockSpec((1, 1, length), lambda s, p: (s, 0, 0)),
        pl.BlockSpec((1, length, 1), lambda s, p: (s, 0, 0)),
        pl.BlockSpec((1, 1, 2, length), lambda s, p: (s, p + first, 0, 0)),
    )


def attend(queries, keys_all, values, ids):
    count, length, width = queries.shape
    rows, as_row, as_col, sums = attention_specs(length)
    scaling = HDIM ** (-0.5)
    return pl.pallas_call(
        functools.partial(attend_kernel, scaling=scaling),
        grid=(count, width // PAIR),
        in_specs=[rows, rows, rows, as_row, as_col],
        out_specs=[rows, sums],
        out_shape=[
            jax.ShapeDtypeStruct(queries.shape, LOW),
            jax.ShapeDtypeStruct((count, width // PAIR, 2, length), WIDE),
        ],
        cost_estimate=pl.CostEstimate(
            flops=28 * count * width * length * length,
            transcendentals=count * width * length * length // HDIM,
            bytes_accessed=8 * count * width * length,
        ),
        name="attend",
    )(queries, keys_all, values, *ids)


def attend_back(queries, keys_all, values, grad_context, context, logsum, ids, earlier, part):
    count, length, width = queries.shape
    pairs = width // PAIR
    first = pairs // 2 * part
    rows, as_row, as_col, sums = attention_specs(length, first)
    body = functools.partial(attend_back_kernel, scaling=HDIM ** (-0.5))
    operands = [queries, keys_all, values, grad_context, context, logsum, *ids]
    in_specs = [rows] * 5 + [sums, as_row, as_col]
    aliases = {}
    if earlier is not None:

        def body(*refs):
            attend_back_kernel(*refs[:8], *refs[11:], scaling=HDIM ** (-0.5))

        aliases = {8 + i: i for i in range(3)}
        operands += list(earlier)
        in_specs += [pl.BlockSpec(memory_space=pl.ANY)] * 3
    return pl.pallas_call(
        body,
        grid=(count, (pairs - first) if part else pairs // 2),
        in_specs=in_specs,
        out_specs=[rows, rows, rows],
        out_shape=[jax.ShapeDtypeStruct(queries.shape, LOW)] * 3,
        input_output_aliases=aliases,
        cost_estimate=pl.CostEstimate(
            flops=24 * count * width * length * length,
            transcendentals=count * width * length * length // HDIM // 2,
            bytes_accessed=7 * count * width * length,
        ),
        name="attend_back",
    )(*operands)


def meet(value, parts, picks):
    picked = [step for step in picks if step < len(parts)]
    value, held = lax.optimization_barrier((value, [parts[step] for step in picked]))
    parts = list(parts)
    for step, part in zip(picked, held):
        parts[step] = part
    return value, parts


def spread(block):
    members = lax.axis_size("tp")
    rank_pairs = [[(i, (i + step) % members) for i in range(members)] for step in range(1, members)]
    return [block] + [lax.ppermute(block, "tp", pairs) for pairs in rank_pairs]


def dealt(blocks):
    members, rank = lax.axis_size("tp"), lax.axis_index("tp")
    parts = []
    for step in range(members):
        block = lax.dynamic_slice_in_dim(blocks, (rank + step) % members, 1, 0)[0]
        pairs = [(i, (i + step) % members) for i in range(members)]
        parts.append(lax.ppermute(block, "tp", pairs) if step else block)
    return parts


def sent_back(parts, steps=None):
    members = lax.axis_size("tp")
    moved = list(parts)
    for step in range(1, members) if steps is None else steps:
        pairs = [(i, (i - step) % members) for i in range(members)]
        moved[step] = lax.ppermute(parts[step], "tp", pairs)
    return moved


def by_source(moved):
    members, rank = len(moved), lax.axis_index("tp")
    shape = (members,) + moved[0].shape
    above = (lax.broadcasted_iota(jnp.int32, shape, 0) - rank) % members
    result = jnp.broadcast_to(moved[0][None], shape)
    for step in range(1, members):
        result = jnp.where(above == step, moved[step][None], result)
    return result


def flip(axis, members, bit, block):
    return lax.ppermute(block, axis, [(i, i ^ bit) for i in range(members)])


def beside(bit, block, other, place):
    mine = lax.axis_index("fsdp") // bit % 2
    shape = block.shape[:place] + (2,) + block.shape[place:]
    spot = lax.broadcasted_iota(jnp.int32, shape, place)
    return jnp.where(spot == mine, jnp.expand_dims(block, place), jnp.expand_dims(other, place))


def entries(bit, array, place):
    mine = lax.axis_index("fsdp") // bit % 2
    return [
        lax.squeeze(lax.dynamic_slice_in_dim(array, spot, 1, place), (place,)) for spot in (mine, 1 - mine)
    ]


def together(*groups):
    return lax.optimization_barrier(tuple(list(group) for group in groups))


def gather_rows(members, block, before, beyond, fillers):
    if members != 8:
        return lax.all_gather(block, "fsdp", axis=0, tiled=True), before, beyond, fillers
    rows, cols = block.shape
    first, second = block[:, : cols // 2], block[:, cols // 2 :]
    near = (flip("fsdp", members, 2, first), flip("fsdp", members, 4, second))
    near, beyond, fillers = together(near, beyond, fillers)
    first, second = beside(2, first, near[0], 0), beside(4, second, near[1], 0)
    far = (flip("fsdp", members, 4, first), flip("fsdp", members, 2, second))
    far, before[:3] = together(far, before[:3])
    both = jnp.concatenate([beside(4, first, far[0], 0), beside(2, second, far[1], 1)], axis=3)
    (other,), before[3:] = together((flip("fsdp", members, 1, both),), before[3:])
    return beside(1, both, other, 2).reshape(members * rows, cols), before, beyond, fillers


def add_low(kept, moved):
    return (kept.astype(WIDE) + moved.astype(WIDE)).astype(LOW)


def scatter_core(grad, others=()):
    if lax.axis_size("fsdp") != 8:
        return lax.psum_scatter(grad, "fsdp", scatter_dimension=0, tiled=True), others
    total_rows, cols = grad.shape
    kept, theirs = entries(1, grad.reshape(2, 2, 2, total_rows // 8, cols), 2)
    (moved,), others = together((flip("fsdp", 8, 1, theirs),), others)
    return add_low(kept, moved), others


def scatter_near(grad, others=()):
    if lax.axis_size("fsdp") != 8:
        return grad, others
    half = grad.shape[-1] // 2
    first, first_out = entries(4, grad[..., :half], 0)
    second, second_out = entries(2, grad[..., half:], 1)
    moved = (flip("fsdp", 8, 4, first_out), flip("fsdp", 8, 2, second_out))
    moved, others = together(moved, others)
    return (add_low(first, moved[0]), add_low(second, moved[1])), others


def scatter_far(grad, others=()):
    if lax.axis_size("fsdp") != 8:
        return grad, others
    first, first_out = entries(2, grad[0], 0)
    second, second_out = entries(4, grad[1], 0)
    moved = (flip("fsdp", 8, 2, first_out), flip("fsdp", 8, 4, second_out))
    moved, others = together(moved, others)
    return jnp.concatenate([add_low(first, moved[0]), add_low(second, moved[1])], axis=1), others


def total_over_fsdp(vector):
    members, bit = lax.axis_size("fsdp"), 1
    while bit < members:
        vector = vector + flip("fsdp", members, bit, vector)
        bit *= 2
    return vector


def normalize(token_rows):
    centred = token_rows - jnp.mean(token_rows, axis=-1, keepdims=True)
    scaling = lax.rsqrt(jnp.mean(centred * centred, axis=-1, keepdims=True) + EPSILON)
    return centred * scaling, scaling


def normalize_back(grad_rows, normed, scaling, gain_row):
    grad_normed = grad_rows * gain_row
    adjusted = grad_normed - jnp.mean(grad_normed, axis=-1, keepdims=True)
    adjusted = adjusted - normed * jnp.mean(grad_normed * normed, axis=-1, keepdims=True)
    return scaling * adjusted, jnp.sum(grad_rows * normed, axis=0), jnp.sum(grad_rows, axis=0)


def on_device(
    fsdp,
    tp,
    tokens,
    segment_ids,
    live_mask,
    query_weight,
    query_bias,
    key_weight,
    value_weight,
    value_bias,
    output_weight,
    output_bias,
    first_gain,
    first_shift,
    inner_weight,
    inner_bias,
    outer_weight,
    outer_bias,
    second_gain,
    second_shift,
    out_grad,
):
    sequences, places, width = tokens.shape
    count = sequences // tp
    length = places * tp
    rank = lax.axis_index("tp")
    head_cols = query_weight.shape[1]
    unit_cols = inner_weight.shape[1]
    shard_rows = query_weight.shape[0]

    def whole_rows(parts):
        return jnp.concatenate(parts, axis=1).reshape(count * length, width)

    def by_member(array):
        return array.reshape(tp, count, places, width)

    def by_arrival(array):
        parts = array.reshape(count, tp, places, width)
        return [parts[:, step] for step in range(tp)]

    def own_places(parts):
        return by_source(parts).reshape(sequences, places, width)

    def columns(parts, widths):
        pieces, first = [], 0
        for cols in widths:
            pieces += [part[:shard_rows, first : first + cols] for part in parts]
            first += cols
        return jnp.concatenate(pieces, axis=1)

    def own_columns(share, widths):
        parts = []
        for step in range(tp):
            pieces, first = [], 0
            for cols in widths:
                pieces.append(share[:, first + step * cols : first + (step + 1) * cols])
                first += tp * cols
            parts.append(jnp.concatenate(pieces, axis=1))
        return sent_back(parts)

    def summed(parts, widths):
        total, first, pieces = sum(part.astype(WIDE) for part in parts), 0, []
        for cols in widths:
            pieces.append(total[:, first : first + cols])
            first += cols
        return pieces

    def by_rank(vector):
        parts = vector.reshape(tp, -1)
        parts = [lax.dynamic_slice_in_dim(parts, (rank - spot) % tp, 1, 0) for spot in range(tp)]
        return jnp.concatenate(parts, axis=0).reshape(-1)

    biases = jnp.concatenate([query_bias, value_bias, inner_bias]).reshape(-1, 4 * head_cols // 2)
    biases = jnp.pad(biases, ((0, 0), (0, 4 * head_cols - biases.shape[1])))
    heads = jnp.concatenate([query_weight, key_weight, value_weight, output_weight.T], axis=1)
    heads = spread(jnp.concatenate([heads, biases], axis=0))
    rest = jnp.concatenate([inner_weight, outer_weight.T], axis=1)
    rest, heads = meet(rest, heads, (1, 2, 3))
    rest = spread(rest)
    tokens, rest = meet(tokens, rest, (1,))
    rows = dealt(by_member(tokens))
    biases = [part[shard_rows:, : 2 * head_cols].reshape(-1).astype(WIDE) for part in heads]
    query_bias_full = jnp.concatenate([part[:head_cols] for part in biases])
    value_bias_full = jnp.concatenate([part[head_cols : 2 * head_cols] for part in biases])
    inner_bias_full = jnp.concatenate([part[2 * head_cols :] for part in biases])
    first = rank * count
    segment = lax.dynamic_slice_in_dim(segment_ids, first, count, 0)
    live = lax.dynamic_slice_in_dim(live_mask, first, count, 0)
    spots = lax.broadcasted_iota(jnp.int32, segment.shape, 1)
    ids = jnp.where(live == 1, segment, length + spots).reshape(count, tp, places)
    ids = [lax.dynamic_slice_in_dim(ids, (rank - step) % tp, 1, 1) for step in range(tp)]
    ids = jnp.concatenate(ids, axis=1).reshape(count, length)
    ids = (ids[:, None, :], ids[:, :, None])
    fillers = (
        *ids,
        *(vector.astype(WIDE) for vector in (output_bias, first_gain, first_shift)),
        *(vector.astype(WIDE) for vector in (outer_bias, second_gain, second_shift)),
        *(query_bias_full, value_bias_full, inner_bias_full),
    )
    heads, rows, rest, fillers = gather_rows(
        fsdp, columns(heads, (head_cols,) * 4), rows, rest, fillers
    )
    ids = fillers[:2]
    output_bias, first_gain, first_shift, outer_bias, second_gain, second_shift = fillers[2:8]
    query_bias_full, value_bias_full, inner_bias_full = fillers[8:]
    query_full, key_full, value_full, output_turned = (
        heads[:, i * width : (i + 1) * width] for i in range(4)
    )
    rows = whole_rows(rows)
    rows, out_grad = lax.optimization_barrier((rows, out_grad))
    rest = lax.all_gather(columns(rest, (unit_cols, unit_cols)), "fsdp", axis=0, tiled=True)
    inner_full, outer_turned = rest[:, : tp * unit_cols], rest[:, tp * unit_cols :]

    shape = (count, length, width)
    queries = (dot(rows, query_full, BY_ROWS) + query_bias_full).astype(LOW).reshape(shape)
    keys_all = dot(rows, key_full, BY_ROWS).astype(LOW).reshape(shape)
    values = (dot(rows, value_full, BY_ROWS) + value_bias_full).astype(LOW).reshape(shape)
    context, logsum = attend(queries, keys_all, values, ids)
    context, grad_out = meet(context, dealt(by_member(out_grad)), (2,))
    context = context.reshape(count * length, width)
    mixed = dot(context, output_turned, BY_LAST) + output_bias
    first_normed, first_scaling = normalize(rows.astype(WIDE) + mixed)
    first_rows = first_normed * first_gain + first_shift
    first_low = first_rows.astype(LOW)
    preactivation = dot(first_low, inner_full, BY_ROWS) + inner_bias_full
    cumulative = 0.5 * (1.0 + lax.erf(preactivation * 0.7071067811865476))
    activation_rows = (preactivation * cumulative).astype(LOW)
    density = jnp.exp(-0.5 * preactivation * preactivation) * 0.3989422804014327
    slope = cumulative + preactivation * density
    activation_rows, grad_out = meet(activation_rows, grad_out, (1, 3))
    branch = dot(activation_rows, outer_turned, BY_LAST)
    second_normed, second_scaling = normalize(first_rows + branch + outer_bias)
    second_rows = second_normed * second_gain + second_shift
    layer_out = by_arrival(second_rows.astype(LOW))

    grad_out = whole_rows(grad_out).astype(WIDE)
    grad_second, second_gain_grad, second_shift_grad = normalize_back(
        grad_out, second_normed, second_scaling, second_gain
    )
    outer_bias_grad = jnp.sum(grad_second, axis=0)
    grad_branch = grad_second.astype(LOW)
    outer_grad = dot(grad_branch, activation_rows, BY_FIRST).astype(LOW)
    outer_share = lax.psum_scatter(outer_grad, "fsdp", scatter_dimension=0, tiled=True)
    grad_activ = dot(grad_branch, outer_turned, BY_ROWS)
    grad_pre = (grad_activ * slope).astype(LOW)
    inner_bias_grad = jnp.sum(grad_pre.astype(WIDE), axis=0)
    layer_out = sent_back(layer_out, range(2, 3))
    inner_share, layer_out[2:3] = scatter_core(
        dot(first_low, grad_pre, BY_FIRST).astype(LOW), layer_out[2:3]
    )
    inner_share, layer_out = lax.optimization_barrier((inner_share, layer_out))
    layer_out = sent_back(layer_out, [step for step in range(1, tp) if step != 2])
    grad_first = grad_second + dot(grad_pre, inner_full, BY_LAST)
    grad_mixed, first_gain_grad, first_shift_grad = normalize_back(
        grad_first, first_normed, first_scaling, first_gain
    )
    output_bias_grad = jnp.sum(grad_mixed, axis=0)
    grad_mixed_low = grad_mixed.astype(LOW)
    output_grad = dot(grad_mixed_low, context, BY_FIRST).astype(LOW)
    grad_context = dot(grad_mixed_low, output_turned, BY_ROWS).astype(LOW).reshape(shape)
    vectors = [
        output_bias_grad,
        first_gain_grad,
        first_shift_grad,
        outer_bias_grad,
        second_gain_grad,
        second_shift_grad,
        by_rank(jnp.sum(grad_context.astype(WIDE), axis=(0, 1))),
        *jnp.split(by_rank(inner_bias_grad), inner_bias_grad.shape[0] // width),
    ]
    (inner_share, _), vectors = scatter_near(inner_share), vectors
    grad_context, inner_share, output_grad, vectors = lax.optimization_barrier(
        (grad_context, inner_share, output_grad, vectors)
    )
    vectors = lax.all_gather(jnp.stack(vectors), ("tp", "fsdp"), axis=0)
    inner_share, _ = scatter_far(inner_share)
    back = functools.partial(
        attend_back, queries, keys_all, values, grad_context, context.reshape(shape), logsum, ids
    )
    halfway = back(None, 0)
    halfway, inner_share, outer_share, layer_out = lax.optimization_barrier(
        (halfway, inner_share, outer_share, layer_out)
    )
    layer_out = own_places(layer_out)
    units = (unit_cols, unit_cols)
    unit_parts = own_columns(jnp.concatenate([inner_share, outer_share], axis=1), units)
    rows_grads, unit_parts, vectors = lax.optimization_barrier(
        (back(halfway, 1), unit_parts, vectors)
    )
    totals = jnp.sum(vectors, axis=0).reshape(-1)
    inner_share, outer_share = summed(unit_parts, units)
    query_rows_grad, key_rows_grad, value_rows_grad = (
        array.reshape(count * length, width) for array in rows_grads
    )
    head_grads = [
        dot(rows, grad, BY_FIRST).astype(LOW)
        for grad in (query_rows_grad, key_rows_grad, value_rows_grad)
    ]
    tokens_grad = (
        grad_mixed
        + dot(query_rows_grad, query_full, BY_LAST)
        + dot(key_rows_grad, key_full, BY_LAST)
        + dot(value_rows_grad, value_full, BY_LAST)
    ).astype(LOW)
    late = jnp.sum(query_rows_grad.astype(WIDE), axis=0)
    heads_share, (tokens_grad, late) = scatter_core(
        jnp.concatenate(head_grads + [output_grad], axis=1), (tokens_grad, late)
    )
    late = total_over_fsdp(late)
    tokens_grad = sent_back(by_arrival(tokens_grad))
    heads_share, tokens_grad[:3] = scatter_near(heads_share, tokens_grad[:3])
    heads_share, tokens_grad[3:] = scatter_far(heads_share, tokens_grad[3:])
    heads_share, late = lax.optimization_barrier((heads_share, late))
    high = late.astype(LOW)
    late = jnp.concatenate([high, (late - high.astype(WIDE)).astype(LOW)])
    late = jnp.pad(late, (0, heads_share.shape[1] - late.shape[0]))[None]
    heads_share = own_columns(jnp.concatenate([heads_share, late], axis=0), (head_cols,) * 4)
    heads_share = summed(heads_share, (head_cols,) * 4)
    query_bias_total = heads_share[0][shard_rows] + heads_share[1][shard_rows]
    query_share, key_share, value_share, output_share = (
        share[:shard_rows] for share in heads_share
    )
    tokens_grad = own_places(tokens_grad).astype(WIDE)
    rowwise = [totals[i * width : (i + 1) * width] for i in range(6)]
    value_bias_total = lax.dynamic_slice_in_dim(totals, 6 * width + rank * head_cols, head_cols)
    inner_bias_total = lax.dynamic_slice_in_dim(totals, 7 * width + rank * unit_cols, unit_cols)
    return (
        layer_out,
        tokens_grad,
        query_share,
        query_bias_total,
        key_share,
        value_share,
        value_bias_total,
        output_share.T,
        rowwise[0],
        rowwise[1],
        rowwise[2],
        inner_share,
        inner_bias_total,
        outer_share.T,
        rowwise[3],
        rowwise[4],
        rowwise[5],
    )


def solution(mesh):
    split = P("fsdp", "tp", None)
    across, turned = P("fsdp", "tp"), P("tp", "fsdp")
    seqs, units, copied = P("fsdp", None), P("tp"), P()
    return jax.shard_map(
        functools.partial(on_device, mesh.shape["fsdp"], mesh.shape["tp"]),
        mesh=mesh,
        in_specs=(
            split,
            seqs,
            seqs,
            across,
            units,
            across,
            across,
            units,
            turned,
            copied,
            copied,
            copied,
            across,
            units,
            turned,
            copied,
            copied,
            copied,
            split,
        ),
        out_specs=(
            split,
            split,
            across,
            units,
            across,
            across,
            units,
            turned,
            copied,
            copied,
            copied,
            across,
            units,
            turned,
            copied,
            copied,
            copied,
        ),
        check_vma=False,
    )
```

```python
import functools

import jax
import jax.numpy as jnp
from jax import lax
from jax.experimental import pallas as pl
from jax.sharding import PartitionSpec as P

HDIM = 64
EPSILON = 1e-12
MASKED = -1000000000.0
PAIR = 2 * HDIM
BLOCK = 256
LOW = jnp.bfloat16
WIDE = jnp.float32
BY_LAST = (((1,), (1,)), ((), ()))
BY_ROWS = (((1,), (0,)), ((), ()))
BY_FIRST = (((0,), (0,)), ((), ()))


def dot(left, right, dims):
    return lax.dot_general(left, right, dims, preferred_element_type=WIDE)


def halves(pair, fill=0):
    lane = lax.broadcasted_iota(jnp.int32, (1, PAIR), 1)
    other = jnp.full((), fill, pair.dtype)
    return jnp.where(lane < HDIM, pair, other), jnp.where(lane < HDIM, other, pair)


def attend_kernel(q_ref, k_ref, v_ref, row_ref, col_ref, context_ref, logsum_ref, *, scaling):
    keys_all = k_ref[0]
    turned = [half.T for half in halves(v_ref[0], 1)]
    seen = col_ref[0] == row_ref[0]
    pieces = []
    for head, queries in enumerate(halves(q_ref[0] * scaling)):
        scores = jnp.where(seen, dot(keys_all, queries, BY_LAST), MASKED)
        highest = jnp.max(scores, axis=0, keepdims=True)
        piece = dot(turned[head], jnp.exp(scores - highest).astype(LOW), BY_ROWS)
        mine, ones = (piece[:HDIM], piece[HDIM:]) if head == 0 else (piece[HDIM:], piece[:HDIM])
        sums = ones[:1]
        logsum_ref[0, 0, head : head + 1, :] = highest + jnp.log(sums)
        pieces.append(mine * (1.0 / sums))
    context_ref[0] = jnp.concatenate(pieces, axis=0).T.astype(LOW)


def attend_back_kernel(
    q_ref, k_ref, v_ref, g_ref, c_ref, logsum_ref, row_ref, col_ref, dq_ref, dk_ref, dv_ref, *, scaling
):
    keys_all = k_ref[0]
    values = v_ref[0]
    turned = [half.T for half in halves(keys_all)]
    key_ids = col_ref[0]
    length = q_ref.shape[1]
    key_grad = jnp.zeros((length, PAIR), WIDE)
    value_grad = jnp.zeros((length, PAIR), WIDE)
    for start in range(0, length, BLOCK):
        part = slice(start, start + BLOCK)
        seen = key_ids == row_ref[0, :, part]
        total = None
        queries_of = halves(q_ref[0, part, :] * scaling)
        grads_of = halves(g_ref[0, part, :])
        products = g_ref[0, part, :].astype(WIDE).T * c_ref[0, part, :].astype(WIDE).T
        for head in range(2):
            queries, grads = queries_of[head], grads_of[head]
            level = jnp.sum(products[head * HDIM : (head + 1) * HDIM], axis=0, keepdims=True)
            scores = jnp.where(seen, dot(keys_all, queries, BY_LAST), MASKED)
            probs = jnp.exp(scores - logsum_ref[0, 0, head : head + 1, part])
            grad_probs = dot(values, grads, BY_LAST)
            value_grad = value_grad + dot(probs.astype(LOW), grads, BY_ROWS)
            grad_scores = (probs * (grad_probs - level)).astype(LOW)
            key_grad = key_grad + dot(grad_scores, queries, BY_ROWS)
            piece = dot(turned[head], grad_scores, BY_ROWS)
            total = piece if total is None else total + piece
        dq_ref[0, part, :] = (total.T * HDIM ** (-0.5)).astype(LOW)
    dk_ref[0] = key_grad.astype(LOW)
    dv_ref[0] = value_grad.astype(LOW)


def attention_specs(length, first=0):
    return (
        pl.BlockSpec((1, length, PAIR), lambda s, p: (s, 0, p + first)),
        pl.BlockSpec((1, 1, length), lambda s, p: (s, 0, 0)),
        pl.BlockSpec((1, length, 1), lambda s, p: (s, 0, 0)),
        pl.BlockSpec((1, 1, 2, length), lambda s, p: (s, p + first, 0, 0)),
    )


def attend(queries, keys_all, values, ids):
    count, length, width = queries.shape
    rows, as_row, as_col, sums = attention_specs(length)
    scaling = HDIM ** (-0.5)
    return pl.pallas_call(
        functools.partial(attend_kernel, scaling=scaling),
        grid=(count, width // PAIR),
        in_specs=[rows, rows, rows, as_row, as_col],
        out_specs=[rows, sums],
        out_shape=[
            jax.ShapeDtypeStruct(queries.shape, LOW),
            jax.ShapeDtypeStruct((count, width // PAIR, 2, length), WIDE),
        ],
        cost_estimate=pl.CostEstimate(
            flops=28 * count * width * length * length,
            transcendentals=count * width * length * length // HDIM,
            bytes_accessed=8 * count * width * length,
        ),
        name="attend",
    )(queries, keys_all, values, *ids)


def attend_back(queries, keys_all, values, grad_context, context, logsum, ids, earlier, part):
    count, length, width = queries.shape
    pairs = width // PAIR
    first = pairs // 2 * part
    rows, as_row, as_col, sums = attention_specs(length, first)
    body = functools.partial(attend_back_kernel, scaling=HDIM ** (-0.5))
    operands = [queries, keys_all, values, grad_context, context, logsum, *ids]
    in_specs = [rows] * 5 + [sums, as_row, as_col]
    aliases = {}
    if earlier is not None:

        def body(*refs):
            attend_back_kernel(*refs[:8], *refs[11:], scaling=HDIM ** (-0.5))

        aliases = {8 + i: i for i in range(3)}
        operands += list(earlier)
        in_specs += [pl.BlockSpec(memory_space=pl.ANY)] * 3
    return pl.pallas_call(
        body,
        grid=(count, (pairs - first) if part else pairs // 2),
        in_specs=in_specs,
        out_specs=[rows, rows, rows],
        out_shape=[jax.ShapeDtypeStruct(queries.shape, LOW)] * 3,
        input_output_aliases=aliases,
        cost_estimate=pl.CostEstimate(
            flops=24 * count * width * length * length,
            transcendentals=count * width * length * length // HDIM // 2,
            bytes_accessed=7 * count * width * length,
        ),
        name="attend_back",
    )(*operands)


def meet(value, parts, picks):
    picked = [step for step in picks if step < len(parts)]
    value, held = lax.optimization_barrier((value, [parts[step] for step in picked]))
    parts = list(parts)
    for step, part in zip(picked, held):
        parts[step] = part
    return value, parts


def spread(block):
    members = lax.axis_size("tp")
    rank_pairs = [[(i, (i + step) % members) for i in range(members)] for step in range(1, members)]
    return [block] + [lax.ppermute(block, "tp", pairs) for pairs in rank_pairs]


def dealt(blocks):
    members, rank = lax.axis_size("tp"), lax.axis_index("tp")
    parts = []
    for step in range(members):
        block = lax.dynamic_slice_in_dim(blocks, (rank + step) % members, 1, 0)[0]
        pairs = [(i, (i + step) % members) for i in range(members)]
        parts.append(lax.ppermute(block, "tp", pairs) if step else block)
    return parts


def sent_back(parts, steps=None):
    members = lax.axis_size("tp")
    moved = list(parts)
    for step in range(1, members) if steps is None else steps:
        pairs = [(i, (i - step) % members) for i in range(members)]
        moved[step] = lax.ppermute(parts[step], "tp", pairs)
    return moved


def by_source(moved):
    members, rank = len(moved), lax.axis_index("tp")
    shape = (members,) + moved[0].shape
    above = (lax.broadcasted_iota(jnp.int32, shape, 0) - rank) % members
    result = jnp.broadcast_to(moved[0][None], shape)
    for step in range(1, members):
        result = jnp.where(above == step, moved[step][None], result)
    return result


def flip(axis, members, bit, block):
    return lax.ppermute(block, axis, [(i, i ^ bit) for i in range(members)])


def beside(bit, block, other, place):
    mine = lax.axis_index("fsdp") // bit % 2
    shape = block.shape[:place] + (2,) + block.shape[place:]
    spot = lax.broadcasted_iota(jnp.int32, shape, place)
    return jnp.where(spot == mine, jnp.expand_dims(block, place), jnp.expand_dims(other, place))


def entries(bit, array, place):
    mine = lax.axis_index("fsdp") // bit % 2
    return [
        lax.squeeze(lax.dynamic_slice_in_dim(array, spot, 1, place), (place,)) for spot in (mine, 1 - mine)
    ]


def together(*groups):
    return lax.optimization_barrier(tuple(list(group) for group in groups))


def gather_rows(members, block, before, beyond, fillers):
    if members != 8:
        return lax.all_gather(block, "fsdp", axis=0, tiled=True), before, beyond, fillers
    rows, cols = block.shape
    first, second = block[:, : cols // 2], block[:, cols // 2 :]
    near = (flip("fsdp", members, 2, first), flip("fsdp", members, 4, second))
    near, beyond, fillers = together(near, beyond, fillers)
    first, second = beside(2, first, near[0], 0), beside(4, second, near[1], 0)
    far = (flip("fsdp", members, 4, first), flip("fsdp", members, 2, second))
    far, before[:3] = together(far, before[:3])
    both = jnp.concatenate([beside(4, first, far[0], 0), beside(2, second, far[1], 1)], axis=3)
    (other,), before[3:] = together((flip("fsdp", members, 1, both),), before[3:])
    return beside(1, both, other, 2).reshape(members * rows, cols), before, beyond, fillers


def add_low(kept, moved):
    return (kept.astype(WIDE) + moved.astype(WIDE)).astype(LOW)


def scatter_core(grad, others=()):
    if lax.axis_size("fsdp") != 8:
        return lax.psum_scatter(grad, "fsdp", scatter_dimension=0, tiled=True), others
    total_rows, cols = grad.shape
    kept, theirs = entries(1, grad.reshape(2, 2, 2, total_rows // 8, cols), 2)
    (moved,), others = together((flip("fsdp", 8, 1, theirs),), others)
    return add_low(kept, moved), others


def scatter_near(grad, others=()):
    if lax.axis_size("fsdp") != 8:
        return grad, others
    half = grad.shape[-1] // 2
    first, first_out = entries(4, grad[..., :half], 0)
    second, second_out = entries(2, grad[..., half:], 1)
    moved = (flip("fsdp", 8, 4, first_out), flip("fsdp", 8, 2, second_out))
    moved, others = together(moved, others)
    return (add_low(first, moved[0]), add_low(second, moved[1])), others


def scatter_far(grad, others=()):
    if lax.axis_size("fsdp") != 8:
        return grad, others
    first, first_out = entries(2, grad[0], 0)
    second, second_out = entries(4, grad[1], 0)
    moved = (flip("fsdp", 8, 2, first_out), flip("fsdp", 8, 4, second_out))
    moved, others = together(moved, others)
    return jnp.concatenate([add_low(first, moved[0]), add_low(second, moved[1])], axis=1), others


def total_over_fsdp(vector):
    members, bit = lax.axis_size("fsdp"), 1
    while bit < members:
        vector = vector + flip("fsdp", members, bit, vector)
        bit *= 2
    return vector


def normalize(token_rows):
    centred = token_rows - jnp.mean(token_rows, axis=-1, keepdims=True)
    scaling = lax.rsqrt(jnp.mean(centred * centred, axis=-1, keepdims=True) + EPSILON)
    return centred * scaling, scaling


def normalize_back(grad_rows, normed, scaling, gain_row):
    grad_normed = grad_rows * gain_row
    adjusted = grad_normed - jnp.mean(grad_normed, axis=-1, keepdims=True)
    adjusted = adjusted - normed * jnp.mean(grad_normed * normed, axis=-1, keepdims=True)
    return scaling * adjusted, jnp.sum(grad_rows * normed, axis=0), jnp.sum(grad_rows, axis=0)


def on_device(
    fsdp,
    tp,
    tokens,
    segment_ids,
    live_mask,
    query_weight,
    query_bias,
    key_weight,
    value_weight,
    value_bias,
    output_weight,
    output_bias,
    first_gain,
    first_shift,
    inner_weight,
    inner_bias,
    outer_weight,
    outer_bias,
    second_gain,
    second_shift,
    out_grad,
):
    sequences, places, width = tokens.shape
    count = sequences // tp
    length = places * tp
    rank = lax.axis_index("tp")
    head_cols = query_weight.shape[1]
    unit_cols = inner_weight.shape[1]
    shard_rows = query_weight.shape[0]

    def whole_rows(parts):
        return jnp.concatenate(parts, axis=1).reshape(count * length, width)

    def by_member(array):
        return array.reshape(tp, count, places, width)

    def by_arrival(array):
        parts = array.reshape(count, tp, places, width)
        return [parts[:, step] for step in range(tp)]

    def own_places(parts):
        return by_source(parts).reshape(sequences, places, width)

    def columns(parts, widths):
        pieces, first = [], 0
        for cols in widths:
            pieces += [part[:shard_rows, first : first + cols] for part in parts]
            first += cols
        return jnp.concatenate(pieces, axis=1)

    def own_columns(share, widths):
        parts = []
        for step in range(tp):
            pieces, first = [], 0
            for cols in widths:
                pieces.append(share[:, first + step * cols : first + (step + 1) * cols])
                first += tp * cols
            parts.append(jnp.concatenate(pieces, axis=1))
        return sent_back(parts)

    def summed(parts, widths):
        total, first, pieces = sum(part.astype(WIDE) for part in parts), 0, []
        for cols in widths:
            pieces.append(total[:, first : first + cols])
            first += cols
        return pieces

    def by_rank(vector):
        parts = vector.reshape(tp, -1)
        parts = [lax.dynamic_slice_in_dim(parts, (rank - spot) % tp, 1, 0) for spot in range(tp)]
        return jnp.concatenate(parts, axis=0).reshape(-1)

    biases = jnp.concatenate([query_bias, value_bias, inner_bias]).reshape(-1, 4 * head_cols // 2)
    biases = jnp.pad(biases, ((0, 0), (0, 4 * head_cols - biases.shape[1])))
    heads = jnp.concatenate([query_weight, key_weight, value_weight, output_weight.T], axis=1)
    heads = spread(jnp.concatenate([heads, biases], axis=0))
    rest = jnp.concatenate([inner_weight, outer_weight.T], axis=1)
    rest, heads = meet(rest, heads, (1, 2, 3))
    rest = spread(rest)
    tokens, rest = meet(tokens, rest, (1,))
    rows = dealt(by_member(tokens))
    biases = [part[shard_rows:, : 2 * head_cols].reshape(-1).astype(WIDE) for part in heads]
    query_bias_full = jnp.concatenate([part[:head_cols] for part in biases])
    value_bias_full = jnp.concatenate([part[head_cols : 2 * head_cols] for part in biases])
    inner_bias_full = jnp.concatenate([part[2 * head_cols :] for part in biases])
    first = rank * count
    segment = lax.dynamic_slice_in_dim(segment_ids, first, count, 0)
    live = lax.dynamic_slice_in_dim(live_mask, first, count, 0)
    spots = lax.broadcasted_iota(jnp.int32, segment.shape, 1)
    ids = jnp.where(live == 1, segment, length + spots).reshape(count, tp, places)
    ids = [lax.dynamic_slice_in_dim(ids, (rank - step) % tp, 1, 1) for step in range(tp)]
    ids = jnp.concatenate(ids, axis=1).reshape(count, length)
    ids = (ids[:, None, :], ids[:, :, None])
    fillers = (
        *ids,
        *(vector.astype(WIDE) for vector in (output_bias, first_gain, first_shift)),
        *(vector.astype(WIDE) for vector in (outer_bias, second_gain, second_shift)),
        *(query_bias_full, value_bias_full, inner_bias_full),
    )
    heads, rows, rest, fillers = gather_rows(
        fsdp, columns(heads, (head_cols,) * 4), rows, rest, fillers
    )
    ids = fillers[:2]
    output_bias, first_gain, first_shift, outer_bias, second_gain, second_shift = fillers[2:8]
    query_bias_full, value_bias_full, inner_bias_full = fillers[8:]
    query_full, key_full, value_full, output_turned = (
        heads[:, i * width : (i + 1) * width] for i in range(4)
    )
    rows = whole_rows(rows)
    rows, out_grad = lax.optimization_barrier((rows, out_grad))
    rest = lax.all_gather(columns(rest, (unit_cols, unit_cols)), "fsdp", axis=0, tiled=True)
    inner_full, outer_turned = rest[:, : tp * unit_cols], rest[:, tp * unit_cols :]

    shape = (count, length, width)
    queries = (dot(rows, query_full, BY_ROWS) + query_bias_full).astype(LOW).reshape(shape)
    keys_all = dot(rows, key_full, BY_ROWS).astype(LOW).reshape(shape)
    values = (dot(rows, value_full, BY_ROWS) + value_bias_full).astype(LOW).reshape(shape)
    context, logsum = attend(queries, keys_all, values, ids)
    context, grad_out = meet(context, dealt(by_member(out_grad)), (2,))
    context = context.reshape(count * length, width)
    mixed = dot(context, output_turned, BY_LAST) + output_bias
    first_normed, first_scaling = normalize(rows.astype(WIDE) + mixed)
    first_rows = first_normed * first_gain + first_shift
    first_low = first_rows.astype(LOW)
    preactivation = dot(first_low, inner_full, BY_ROWS) + inner_bias_full
    cumulative = 0.5 * (1.0 + lax.erf(preactivation * 0.7071067811865476))
    activation_rows = (preactivation * cumulative).astype(LOW)
    density = jnp.exp(-0.5 * preactivation * preactivation) * 0.3989422804014327
    slope = cumulative + preactivation * density
    activation_rows, grad_out = meet(activation_rows, grad_out, (1, 3))
    branch = dot(activation_rows, outer_turned, BY_LAST)
    second_normed, second_scaling = normalize(first_rows + branch + outer_bias)
    second_rows = second_normed * second_gain + second_shift
    layer_out = by_arrival(second_rows.astype(LOW))

    grad_out = whole_rows(grad_out).astype(WIDE)
    grad_second, second_gain_grad, second_shift_grad = normalize_back(
        grad_out, second_normed, second_scaling, second_gain
    )
    outer_bias_grad = jnp.sum(grad_second, axis=0)
    grad_branch = grad_second.astype(LOW)
    outer_grad = dot(grad_branch, activation_rows, BY_FIRST).astype(LOW)
    outer_share = lax.psum_scatter(outer_grad, "fsdp", scatter_dimension=0, tiled=True)
    grad_activ = dot(grad_branch, outer_turned, BY_ROWS)
    grad_pre = (grad_activ * slope).astype(LOW)
    inner_bias_grad = jnp.sum(grad_pre.astype(WIDE), axis=0)
    layer_out = sent_back(layer_out, range(2, 3))
    inner_share, layer_out[2:3] = scatter_core(
        dot(first_low, grad_pre, BY_FIRST).astype(LOW), layer_out[2:3]
    )
    inner_share, layer_out = lax.optimization_barrier((inner_share, layer_out))
    layer_out = sent_back(layer_out, [step for step in range(1, tp) if step != 2])
    grad_first = grad_second + dot(grad_pre, inner_full, BY_LAST)
    grad_mixed, first_gain_grad, first_shift_grad = normalize_back(
        grad_first, first_normed, first_scaling, first_gain
    )
    output_bias_grad = jnp.sum(grad_mixed, axis=0)
    grad_mixed_low = grad_mixed.astype(LOW)
    output_grad = dot(grad_mixed_low, context, BY_FIRST).astype(LOW)
    grad_context = dot(grad_mixed_low, output_turned, BY_ROWS).astype(LOW).reshape(shape)
    vectors = [
        output_bias_grad,
        first_gain_grad,
        first_shift_grad,
        outer_bias_grad,
        second_gain_grad,
        second_shift_grad,
        *jnp.split(by_rank(inner_bias_grad), inner_bias_grad.shape[0] // width),
        jnp.zeros((width,), WIDE),
        jnp.zeros((width,), WIDE),
    ]
    vectors = lax.all_gather(
        jnp.stack(lax.optimization_barrier(vectors)), ("tp", "fsdp"), axis=0
    )
    inner_share, _ = scatter_near(inner_share)
    grad_context, inner_share, output_grad = lax.optimization_barrier(
        (grad_context, inner_share, output_grad)
    )
    inner_share, _ = scatter_far(inner_share)
    back = functools.partial(
        attend_back, queries, keys_all, values, grad_context, context.reshape(shape), logsum, ids
    )
    value_bias_grad = jnp.sum(grad_context.astype(WIDE), axis=(0, 1))
    halfway = back(None, 0)
    halfway, inner_share, outer_share, layer_out = lax.optimization_barrier(
        (halfway, inner_share, outer_share, layer_out)
    )
    layer_out = own_places(layer_out)
    units = (unit_cols, unit_cols)
    unit_parts = own_columns(jnp.concatenate([inner_share, outer_share], axis=1), units)
    rows_grads, unit_parts, vectors = lax.optimization_barrier(
        (back(halfway, 1), unit_parts, vectors)
    )
    totals = jnp.sum(vectors, axis=0).reshape(-1)[: -2 * width]
    inner_share, outer_share = summed(unit_parts, units)
    query_rows_grad, key_rows_grad, value_rows_grad = (
        array.reshape(count * length, width) for array in rows_grads
    )
    head_grads = [
        dot(rows, grad, BY_FIRST).astype(LOW)
        for grad in (query_rows_grad, key_rows_grad, value_rows_grad)
    ]
    tokens_grad = (
        grad_mixed
        + dot(query_rows_grad, query_full, BY_LAST)
        + dot(key_rows_grad, key_full, BY_LAST)
        + dot(value_rows_grad, value_full, BY_LAST)
    ).astype(LOW)
    late = [jnp.sum(query_rows_grad.astype(WIDE), axis=0), value_bias_grad]
    late = jnp.concatenate(late)
    heads_share, (tokens_grad, late) = scatter_core(
        jnp.concatenate(head_grads + [output_grad], axis=1), (tokens_grad, late)
    )
    late = total_over_fsdp(late)
    tokens_grad = sent_back(by_arrival(tokens_grad))
    heads_share, tokens_grad[:3] = scatter_near(heads_share, tokens_grad[:3])
    heads_share, tokens_grad[3:] = scatter_far(heads_share, tokens_grad[3:])
    heads_share, late = lax.optimization_barrier((heads_share, late))
    high = late.astype(LOW)
    late = jnp.stack([high, (late - high.astype(WIDE)).astype(LOW)]).reshape(2, 2, width)
    late = late.transpose(1, 0, 2).reshape(1, 4 * width)
    heads_share = own_columns(jnp.concatenate([heads_share, late], axis=0), (head_cols,) * 4)
    heads_share = summed(heads_share, (head_cols,) * 4)
    query_bias_total = heads_share[0][shard_rows] + heads_share[1][shard_rows]
    value_bias_total = heads_share[2][shard_rows] + heads_share[3][shard_rows]
    query_share, key_share, value_share, output_share = (
        share[:shard_rows] for share in heads_share
    )
    tokens_grad = own_places(tokens_grad).astype(WIDE)
    rowwise = [totals[i * width : (i + 1) * width] for i in range(6)]
    inner_bias_total = lax.dynamic_slice_in_dim(totals, 6 * width + rank * unit_cols, unit_cols)
    return (
        layer_out,
        tokens_grad,
        query_share,
        query_bias_total,
        key_share,
        value_share,
        value_bias_total,
        output_share.T,
        rowwise[0],
        rowwise[1],
        rowwise[2],
        inner_share,
        inner_bias_total,
        outer_share.T,
        rowwise[3],
        rowwise[4],
        rowwise[5],
    )


def solution(mesh):
    split = P("fsdp", "tp", None)
    across, turned = P("fsdp", "tp"), P("tp", "fsdp")
    seqs, units, copied = P("fsdp", None), P("tp"), P()
    return jax.shard_map(
        functools.partial(on_device, mesh.shape["fsdp"], mesh.shape["tp"]),
        mesh=mesh,
        in_specs=(
            split,
            seqs,
            seqs,
            across,
            units,
            across,
            across,
            units,
            turned,
            copied,
            copied,
            copied,
            across,
            units,
            turned,
            copied,
            copied,
            copied,
            split,
        ),
        out_specs=(
            split,
            split,
            across,
            units,
            across,
            across,
            units,
            turned,
            copied,
            copied,
            copied,
            across,
            units,
            turned,
            copied,
            copied,
            copied,
        ),
        check_vma=False,
    )
```

```python
import functools

import jax
import jax.numpy as jnp
from jax import lax
from jax.experimental import pallas as pl
from jax.sharding import PartitionSpec as P

HDIM = 64
EPSILON = 1e-12
MASKED = -1000000000.0
PAIR = 2 * HDIM
BLOCK = 256
LOW = jnp.bfloat16
WIDE = jnp.float32
BY_LAST = (((1,), (1,)), ((), ()))
BY_ROWS = (((1,), (0,)), ((), ()))
BY_FIRST = (((0,), (0,)), ((), ()))


def dot(left, right, dims):
    return lax.dot_general(left, right, dims, preferred_element_type=WIDE)


def halves(pair, fill=0):
    lane = lax.broadcasted_iota(jnp.int32, (1, PAIR), 1)
    other = jnp.full((), fill, pair.dtype)
    return jnp.where(lane < HDIM, pair, other), jnp.where(lane < HDIM, other, pair)


def attend_kernel(q_ref, k_ref, v_ref, row_ref, col_ref, context_ref, logsum_ref, *, scaling):
    keys_all = k_ref[0]
    turned = [half.T for half in halves(v_ref[0], 1)]
    seen = col_ref[0] == row_ref[0]
    pieces = []
    for head, queries in enumerate(halves(q_ref[0] * scaling)):
        scores = jnp.where(seen, dot(keys_all, queries, BY_LAST), MASKED)
        highest = jnp.max(scores, axis=0, keepdims=True)
        piece = dot(turned[head], jnp.exp(scores - highest).astype(LOW), BY_ROWS)
        mine, ones = (piece[:HDIM], piece[HDIM:]) if head == 0 else (piece[HDIM:], piece[:HDIM])
        sums = ones[:1]
        logsum_ref[0, 0, head : head + 1, :] = highest + jnp.log(sums)
        pieces.append(mine * (1.0 / sums))
    context_ref[0] = jnp.concatenate(pieces, axis=0).T.astype(LOW)


def attend_back_kernel(
    q_ref, k_ref, v_ref, g_ref, c_ref, logsum_ref, row_ref, col_ref, dq_ref, dk_ref, dv_ref, *, scaling
):
    keys_all = k_ref[0]
    values = v_ref[0]
    turned = [half.T for half in halves(keys_all)]
    key_ids = col_ref[0]
    length = q_ref.shape[1]
    key_grad = jnp.zeros((length, PAIR), WIDE)
    value_grad = jnp.zeros((length, PAIR), WIDE)
    for start in range(0, length, BLOCK):
        part = slice(start, start + BLOCK)
        seen = key_ids == row_ref[0, :, part]
        total = None
        queries_of = halves(q_ref[0, part, :] * scaling)
        grads_of = halves(g_ref[0, part, :])
        products = g_ref[0, part, :].astype(WIDE).T * c_ref[0, part, :].astype(WIDE).T
        for head in range(2):
            queries, grads = queries_of[head], grads_of[head]
            level = jnp.sum(products[head * HDIM : (head + 1) * HDIM], axis=0, keepdims=True)
            scores = jnp.where(seen, dot(keys_all, queries, BY_LAST), MASKED)
            probs = jnp.exp(scores - logsum_ref[0, 0, head : head + 1, part])
            grad_probs = dot(values, grads, BY_LAST)
            value_grad = value_grad + dot(probs.astype(LOW), grads, BY_ROWS)
            grad_scores = (probs * (grad_probs - level)).astype(LOW)
            key_grad = key_grad + dot(grad_scores, queries, BY_ROWS)
            piece = dot(turned[head], grad_scores, BY_ROWS)
            total = piece if total is None else total + piece
        dq_ref[0, part, :] = (total.T * HDIM ** (-0.5)).astype(LOW)
    dk_ref[0] = key_grad.astype(LOW)
    dv_ref[0] = value_grad.astype(LOW)


def attention_specs(length, first=0):
    return (
        pl.BlockSpec((1, length, PAIR), lambda s, p: (s, 0, p + first)),
        pl.BlockSpec((1, 1, length), lambda s, p: (s, 0, 0)),
        pl.BlockSpec((1, length, 1), lambda s, p: (s, 0, 0)),
        pl.BlockSpec((1, 1, 2, length), lambda s, p: (s, p + first, 0, 0)),
    )


def attend(queries, keys_all, values, ids):
    count, length, width = queries.shape
    rows, as_row, as_col, sums = attention_specs(length)
    scaling = HDIM ** (-0.5)
    return pl.pallas_call(
        functools.partial(attend_kernel, scaling=scaling),
        grid=(count, width // PAIR),
        in_specs=[rows, rows, rows, as_row, as_col],
        out_specs=[rows, sums],
        out_shape=[
            jax.ShapeDtypeStruct(queries.shape, LOW),
            jax.ShapeDtypeStruct((count, width // PAIR, 2, length), WIDE),
        ],
        cost_estimate=pl.CostEstimate(
            flops=28 * count * width * length * length,
            transcendentals=count * width * length * length // HDIM,
            bytes_accessed=8 * count * width * length,
        ),
        name="attend",
    )(queries, keys_all, values, *ids)


def attend_back(queries, keys_all, values, grad_context, context, logsum, ids, earlier, part):
    count, length, width = queries.shape
    pairs = width // PAIR
    first = pairs // 2 * part
    rows, as_row, as_col, sums = attention_specs(length, first)
    body = functools.partial(attend_back_kernel, scaling=HDIM ** (-0.5))
    operands = [queries, keys_all, values, grad_context, context, logsum, *ids]
    in_specs = [rows] * 5 + [sums, as_row, as_col]
    aliases = {}
    if earlier is not None:

        def body(*refs):
            attend_back_kernel(*refs[:8], *refs[11:], scaling=HDIM ** (-0.5))

        aliases = {8 + i: i for i in range(3)}
        operands += list(earlier)
        in_specs += [pl.BlockSpec(memory_space=pl.ANY)] * 3
    return pl.pallas_call(
        body,
        grid=(count, (pairs - first) if part else pairs // 2),
        in_specs=in_specs,
        out_specs=[rows, rows, rows],
        out_shape=[jax.ShapeDtypeStruct(queries.shape, LOW)] * 3,
        input_output_aliases=aliases,
        cost_estimate=pl.CostEstimate(
            flops=24 * count * width * length * length,
            transcendentals=count * width * length * length // HDIM // 2,
            bytes_accessed=7 * count * width * length,
        ),
        name="attend_back",
    )(*operands)


def meet(value, parts, picks):
    picked = [step for step in picks if step < len(parts)]
    value, held = lax.optimization_barrier((value, [parts[step] for step in picked]))
    parts = list(parts)
    for step, part in zip(picked, held):
        parts[step] = part
    return value, parts


def spread(block):
    members = lax.axis_size("tp")
    rank_pairs = [[(i, (i + step) % members) for i in range(members)] for step in range(1, members)]
    return [block] + [lax.ppermute(block, "tp", pairs) for pairs in rank_pairs]


def dealt(blocks):
    members, rank = lax.axis_size("tp"), lax.axis_index("tp")
    parts = []
    for step in range(members):
        block = lax.dynamic_slice_in_dim(blocks, (rank + step) % members, 1, 0)[0]
        pairs = [(i, (i + step) % members) for i in range(members)]
        parts.append(lax.ppermute(block, "tp", pairs) if step else block)
    return parts


def sent_back(parts, steps=None):
    members = lax.axis_size("tp")
    moved = list(parts)
    for step in range(1, members) if steps is None else steps:
        pairs = [(i, (i - step) % members) for i in range(members)]
        moved[step] = lax.ppermute(parts[step], "tp", pairs)
    return moved


def by_source(moved):
    members, rank = len(moved), lax.axis_index("tp")
    shape = (members,) + moved[0].shape
    above = (lax.broadcasted_iota(jnp.int32, shape, 0) - rank) % members
    result = jnp.broadcast_to(moved[0][None], shape)
    for step in range(1, members):
        result = jnp.where(above == step, moved[step][None], result)
    return result


def flip(axis, members, bit, block):
    return lax.ppermute(block, axis, [(i, i ^ bit) for i in range(members)])


def beside(bit, block, other, place):
    mine = lax.axis_index("fsdp") // bit % 2
    shape = block.shape[:place] + (2,) + block.shape[place:]
    spot = lax.broadcasted_iota(jnp.int32, shape, place)
    return jnp.where(spot == mine, jnp.expand_dims(block, place), jnp.expand_dims(other, place))


def entries(bit, array, place):
    mine = lax.axis_index("fsdp") // bit % 2
    return [
        lax.squeeze(lax.dynamic_slice_in_dim(array, spot, 1, place), (place,)) for spot in (mine, 1 - mine)
    ]


def together(*groups):
    return lax.optimization_barrier(tuple(list(group) for group in groups))


def gather_rows(members, block, before, beyond, fillers):
    if members != 8:
        return lax.all_gather(block, "fsdp", axis=0, tiled=True), before, beyond, fillers
    rows, cols = block.shape
    first, second = block[:, : cols // 2], block[:, cols // 2 :]
    near = (flip("fsdp", members, 2, first), flip("fsdp", members, 4, second))
    near, beyond, fillers = together(near, beyond, fillers)
    first, second = beside(2, first, near[0], 0), beside(4, second, near[1], 0)
    far = (flip("fsdp", members, 4, first), flip("fsdp", members, 2, second))
    far, before[:3] = together(far, before[:3])
    both = jnp.concatenate([beside(4, first, far[0], 0), beside(2, second, far[1], 1)], axis=3)
    (other,), before[3:] = together((flip("fsdp", members, 1, both),), before[3:])
    return beside(1, both, other, 2).reshape(members * rows, cols), before, beyond, fillers


def add_low(kept, moved):
    return (kept.astype(WIDE) + moved.astype(WIDE)).astype(LOW)


def scatter_core(grad, others=()):
    if lax.axis_size("fsdp") != 8:
        return lax.psum_scatter(grad, "fsdp", scatter_dimension=0, tiled=True), others
    total_rows, cols = grad.shape
    kept, theirs = entries(1, grad.reshape(2, 2, 2, total_rows // 8, cols), 2)
    (moved,), others = together((flip("fsdp", 8, 1, theirs),), others)
    return add_low(kept, moved), others


def scatter_near(grad, others=()):
    if lax.axis_size("fsdp") != 8:
        return grad, others
    half = grad.shape[-1] // 2
    first, first_out = entries(4, grad[..., :half], 0)
    second, second_out = entries(2, grad[..., half:], 1)
    moved = (flip("fsdp", 8, 4, first_out), flip("fsdp", 8, 2, second_out))
    moved, others = together(moved, others)
    return (add_low(first, moved[0]), add_low(second, moved[1])), others


def scatter_far(grad, others=()):
    if lax.axis_size("fsdp") != 8:
        return grad, others
    first, first_out = entries(2, grad[0], 0)
    second, second_out = entries(4, grad[1], 0)
    moved = (flip("fsdp", 8, 2, first_out), flip("fsdp", 8, 4, second_out))
    moved, others = together(moved, others)
    return jnp.concatenate([add_low(first, moved[0]), add_low(second, moved[1])], axis=1), others


def total_over_fsdp(vector):
    members, bit = lax.axis_size("fsdp"), 1
    while bit < members:
        vector = vector + flip("fsdp", members, bit, vector)
        bit *= 2
    return vector


def normalize(token_rows):
    centred = token_rows - jnp.mean(token_rows, axis=-1, keepdims=True)
    scaling = lax.rsqrt(jnp.mean(centred * centred, axis=-1, keepdims=True) + EPSILON)
    return centred * scaling, scaling


def normalize_back(grad_rows, normed, scaling, gain_row):
    grad_normed = grad_rows * gain_row
    adjusted = grad_normed - jnp.mean(grad_normed, axis=-1, keepdims=True)
    adjusted = adjusted - normed * jnp.mean(grad_normed * normed, axis=-1, keepdims=True)
    return scaling * adjusted, jnp.sum(grad_rows * normed, axis=0), jnp.sum(grad_rows, axis=0)


def on_device(
    fsdp,
    tp,
    tokens,
    segment_ids,
    live_mask,
    query_weight,
    query_bias,
    key_weight,
    value_weight,
    value_bias,
    output_weight,
    output_bias,
    first_gain,
    first_shift,
    inner_weight,
    inner_bias,
    outer_weight,
    outer_bias,
    second_gain,
    second_shift,
    out_grad,
):
    sequences, places, width = tokens.shape
    count = sequences // tp
    length = places * tp
    rank = lax.axis_index("tp")
    head_cols = query_weight.shape[1]
    unit_cols = inner_weight.shape[1]
    shard_rows = query_weight.shape[0]

    def whole_rows(parts):
        return jnp.concatenate(parts, axis=1).reshape(count * length, width)

    def by_member(array):
        return array.reshape(tp, count, places, width)

    def by_arrival(array):
        parts = array.reshape(count, tp, places, width)
        return [parts[:, step] for step in range(tp)]

    def own_places(parts):
        return by_source(parts).reshape(sequences, places, width)

    def columns(parts, widths):
        pieces, first = [], 0
        for cols in widths:
            pieces += [part[:shard_rows, first : first + cols] for part in parts]
            first += cols
        return jnp.concatenate(pieces, axis=1)

    def own_columns(share, widths, shared=None):
        parts = []
        for step in range(tp):
            pieces, first = [], 0
            for cols in widths:
                pieces.append(share[:, first + step * cols : first + (step + 1) * cols])
                first += tp * cols
            part = jnp.concatenate(pieces, axis=1)
            parts.append(part if shared is None else jnp.concatenate([part, shared], axis=0))
        return sent_back(parts)

    def summed(parts, widths):
        total, first, pieces = sum(part.astype(WIDE) for part in parts), 0, []
        for cols in widths:
            pieces.append(total[:, first : first + cols])
            first += cols
        return pieces

    def by_rank(vector):
        parts = vector.reshape(tp, -1)
        parts = [lax.dynamic_slice_in_dim(parts, (rank - spot) % tp, 1, 0) for spot in range(tp)]
        return jnp.concatenate(parts, axis=0).reshape(-1)

    biases = jnp.concatenate([query_bias, value_bias, inner_bias]).reshape(-1, 4 * head_cols // 2)
    biases = jnp.pad(biases, ((0, 0), (0, 4 * head_cols - biases.shape[1])))
    heads = jnp.concatenate([query_weight, key_weight, value_weight, output_weight.T], axis=1)
    heads = spread(jnp.concatenate([heads, biases], axis=0))
    rest = jnp.concatenate([inner_weight, outer_weight.T], axis=1)
    rest, heads = meet(rest, heads, (1, 2, 3))
    rest = spread(rest)
    tokens, rest = meet(tokens, rest, (1,))
    rows = dealt(by_member(tokens))
    biases = [part[shard_rows:, : 2 * head_cols].reshape(-1).astype(WIDE) for part in heads]
    query_bias_full = jnp.concatenate([part[:head_cols] for part in biases])
    value_bias_full = jnp.concatenate([part[head_cols : 2 * head_cols] for part in biases])
    inner_bias_full = jnp.concatenate([part[2 * head_cols :] for part in biases])
    first = rank * count
    segment = lax.dynamic_slice_in_dim(segment_ids, first, count, 0)
    live = lax.dynamic_slice_in_dim(live_mask, first, count, 0)
    spots = lax.broadcasted_iota(jnp.int32, segment.shape, 1)
    ids = jnp.where(live == 1, segment, length + spots).reshape(count, tp, places)
    ids = [lax.dynamic_slice_in_dim(ids, (rank - step) % tp, 1, 1) for step in range(tp)]
    ids = jnp.concatenate(ids, axis=1).reshape(count, length)
    ids = (ids[:, None, :], ids[:, :, None])
    fillers = (
        *ids,
        *(vector.astype(WIDE) for vector in (output_bias, first_gain, first_shift)),
        *(vector.astype(WIDE) for vector in (outer_bias, second_gain, second_shift)),
        *(query_bias_full, value_bias_full, inner_bias_full),
    )
    heads, rows, rest, fillers = gather_rows(
        fsdp, columns(heads, (head_cols,) * 4), rows, rest, fillers
    )
    ids = fillers[:2]
    output_bias, first_gain, first_shift, outer_bias, second_gain, second_shift = fillers[2:8]
    query_bias_full, value_bias_full, inner_bias_full = fillers[8:]
    query_full, key_full, value_full, output_turned = (
        heads[:, i * width : (i + 1) * width] for i in range(4)
    )
    rows = whole_rows(rows)
    rows, out_grad = lax.optimization_barrier((rows, out_grad))
    rest = lax.all_gather(columns(rest, (unit_cols, unit_cols)), "fsdp", axis=0, tiled=True)
    inner_full, outer_turned = rest[:, : tp * unit_cols], rest[:, tp * unit_cols :]

    shape = (count, length, width)
    queries = (dot(rows, query_full, BY_ROWS) + query_bias_full).astype(LOW).reshape(shape)
    keys_all = dot(rows, key_full, BY_ROWS).astype(LOW).reshape(shape)
    values = (dot(rows, value_full, BY_ROWS) + value_bias_full).astype(LOW).reshape(shape)
    context, logsum = attend(queries, keys_all, values, ids)
    context, grad_out = meet(context, dealt(by_member(out_grad)), (2,))
    context = context.reshape(count * length, width)
    mixed = dot(context, output_turned, BY_LAST) + output_bias
    first_normed, first_scaling = normalize(rows.astype(WIDE) + mixed)
    first_rows = first_normed * first_gain + first_shift
    first_low = first_rows.astype(LOW)
    preactivation = dot(first_low, inner_full, BY_ROWS) + inner_bias_full
    cumulative = 0.5 * (1.0 + lax.erf(preactivation * 0.7071067811865476))
    activation_rows = (preactivation * cumulative).astype(LOW)
    density = jnp.exp(-0.5 * preactivation * preactivation) * 0.3989422804014327
    slope = cumulative + preactivation * density
    activation_rows, grad_out = meet(activation_rows, grad_out, (1, 3))
    branch = dot(activation_rows, outer_turned, BY_LAST)
    second_normed, second_scaling = normalize(first_rows + branch + outer_bias)
    second_rows = second_normed * second_gain + second_shift
    layer_out = by_arrival(second_rows.astype(LOW))

    grad_out = whole_rows(grad_out).astype(WIDE)
    grad_second, second_gain_grad, second_shift_grad = normalize_back(
        grad_out, second_normed, second_scaling, second_gain
    )
    outer_bias_grad = jnp.sum(grad_second, axis=0)
    grad_branch = grad_second.astype(LOW)
    outer_grad = dot(grad_branch, activation_rows, BY_FIRST).astype(LOW)
    outer_share = lax.psum_scatter(outer_grad, "fsdp", scatter_dimension=0, tiled=True)
    grad_activ = dot(grad_branch, outer_turned, BY_ROWS)
    grad_pre = (grad_activ * slope).astype(LOW)
    inner_bias_grad = jnp.sum(grad_pre.astype(WIDE), axis=0)
    layer_out = sent_back(layer_out, range(2, 3))
    inner_share, layer_out[2:3] = scatter_core(
        dot(first_low, grad_pre, BY_FIRST).astype(LOW), layer_out[2:3]
    )
    inner_share, layer_out = lax.optimization_barrier((inner_share, layer_out))
    layer_out = sent_back(layer_out, [step for step in range(1, tp) if step != 2])
    grad_first = grad_second + dot(grad_pre, inner_full, BY_LAST)
    grad_mixed, first_gain_grad, first_shift_grad = normalize_back(
        grad_first, first_normed, first_scaling, first_gain
    )
    output_bias_grad = jnp.sum(grad_mixed, axis=0)
    grad_mixed_low = grad_mixed.astype(LOW)
    output_grad = dot(grad_mixed_low, context, BY_FIRST).astype(LOW)
    grad_context = dot(grad_mixed_low, output_turned, BY_ROWS).astype(LOW).reshape(shape)
    vectors = [
        output_bias_grad,
        first_gain_grad,
        first_shift_grad,
        outer_bias_grad,
        second_gain_grad,
        second_shift_grad,
        *jnp.split(by_rank(inner_bias_grad), inner_bias_grad.shape[0] // width),
    ]
    inner_share, _ = scatter_near(inner_share)
    grad_context, inner_share, output_grad, vectors = lax.optimization_barrier(
        (grad_context, inner_share, output_grad, vectors)
    )
    inner_share, _ = scatter_far(inner_share)
    back = functools.partial(
        attend_back, queries, keys_all, values, grad_context, context.reshape(shape), logsum, ids
    )
    value_bias_grad = jnp.sum(grad_context.astype(WIDE), axis=(0, 1))
    halfway = back(None, 0)
    halfway, inner_share, outer_share, layer_out = lax.optimization_barrier(
        (halfway, inner_share, outer_share, layer_out)
    )
    layer_out = own_places(layer_out)
    units = (unit_cols, unit_cols)
    unit_parts = own_columns(jnp.concatenate([inner_share, outer_share], axis=1), units)
    rows_grads, unit_parts = lax.optimization_barrier((back(halfway, 1), unit_parts))
    inner_share, outer_share = summed(unit_parts, units)
    query_rows_grad, key_rows_grad, value_rows_grad = (
        array.reshape(count * length, width) for array in rows_grads
    )
    head_grads = [
        dot(rows, grad, BY_FIRST).astype(LOW)
        for grad in (query_rows_grad, key_rows_grad, value_rows_grad)
    ]
    tokens_grad = (
        grad_mixed
        + dot(query_rows_grad, query_full, BY_LAST)
        + dot(key_rows_grad, key_full, BY_LAST)
        + dot(value_rows_grad, value_full, BY_LAST)
    ).astype(LOW)
    late = [jnp.sum(query_rows_grad.astype(WIDE), axis=0), value_bias_grad]
    late = jnp.stack(late + vectors)
    heads_share, (tokens_grad, late) = scatter_core(
        jnp.concatenate(head_grads + [output_grad], axis=1), (tokens_grad, late)
    )
    late = total_over_fsdp(late)
    tokens_grad = sent_back(by_arrival(tokens_grad))
    heads_share, tokens_grad[:3] = scatter_near(heads_share, tokens_grad[:3])
    heads_share, tokens_grad[3:] = scatter_far(heads_share, tokens_grad[3:])
    heads_share, late = lax.optimization_barrier((heads_share, late))
    high = late.astype(LOW)
    lower = (late - high.astype(WIDE)).astype(LOW)
    heads_parts = own_columns(
        jnp.concatenate(
            [heads_share, jnp.stack([high[0], lower[0], high[1], lower[1]]).reshape(1, -1)], axis=0
        ),
        (head_cols,) * 4,
        jnp.concatenate([high[2:], lower[2:]], axis=0),
    )
    totals = by_source([part[shard_rows + 1 :] for part in heads_parts]).astype(WIDE)
    totals = totals[:, : len(vectors)] + totals[:, len(vectors) :]
    totals = jnp.sum(totals, axis=0).reshape(-1)
    heads_share = summed([part[: shard_rows + 1] for part in heads_parts], (head_cols,) * 4)
    query_bias_total = heads_share[0][shard_rows] + heads_share[1][shard_rows]
    value_bias_total = heads_share[2][shard_rows] + heads_share[3][shard_rows]
    query_share, key_share, value_share, output_share = (
        share[:shard_rows] for share in heads_share
    )
    tokens_grad = own_places(tokens_grad).astype(WIDE)
    rowwise = [totals[i * width : (i + 1) * width] for i in range(6)]
    inner_bias_total = lax.dynamic_slice_in_dim(totals, 6 * width + rank * unit_cols, unit_cols)
    return (
        layer_out,
        tokens_grad,
        query_share,
        query_bias_total,
        key_share,
        value_share,
        value_bias_total,
        output_share.T,
        rowwise[0],
        rowwise[1],
        rowwise[2],
        inner_share,
        inner_bias_total,
        outer_share.T,
        rowwise[3],
        rowwise[4],
        rowwise[5],
    )


def solution(mesh):
    split = P("fsdp", "tp", None)
    across, turned = P("fsdp", "tp"), P("tp", "fsdp")
    seqs, units, copied = P("fsdp", None), P("tp"), P()
    return jax.shard_map(
        functools.partial(on_device, mesh.shape["fsdp"], mesh.shape["tp"]),
        mesh=mesh,
        in_specs=(
            split,
            seqs,
            seqs,
            across,
            units,
            across,
            across,
            units,
            turned,
            copied,
            copied,
            copied,
            across,
            units,
            turned,
            copied,
            copied,
            copied,
            split,
        ),
        out_specs=(
            split,
            split,
            across,
            units,
            across,
            across,
            units,
            turned,
            copied,
            copied,
            copied,
            across,
            units,
            turned,
            copied,
            copied,
            copied,
        ),
        check_vma=False,
    )
```

```python
import functools

import jax
import jax.numpy as jnp
from jax import lax
from jax.experimental import pallas as pl
from jax.sharding import PartitionSpec as P

HDIM = 64
EPSILON = 1e-12
MASKED = -1000000000.0
PAIR = 2 * HDIM
BLOCK = 256
LOW = jnp.bfloat16
WIDE = jnp.float32
BY_LAST = (((1,), (1,)), ((), ()))
BY_ROWS = (((1,), (0,)), ((), ()))
BY_FIRST = (((0,), (0,)), ((), ()))


def dot(left, right, dims):
    return lax.dot_general(left, right, dims, preferred_element_type=WIDE)


def halves(pair, fill=0):
    lane = lax.broadcasted_iota(jnp.int32, (1, PAIR), 1)
    other = jnp.full((), fill, pair.dtype)
    return jnp.where(lane < HDIM, pair, other), jnp.where(lane < HDIM, other, pair)


def attend_kernel(q_ref, k_ref, v_ref, row_ref, col_ref, context_ref, logsum_ref, *, scaling):
    keys_all = k_ref[0]
    turned = [half.T for half in halves(v_ref[0], 1)]
    seen = col_ref[0] == row_ref[0]
    pieces = []
    for head, queries in enumerate(halves(q_ref[0] * scaling)):
        scores = jnp.where(seen, dot(keys_all, queries, BY_LAST), MASKED)
        highest = jnp.max(scores, axis=0, keepdims=True)
        piece = dot(turned[head], jnp.exp(scores - highest).astype(LOW), BY_ROWS)
        mine, ones = (piece[:HDIM], piece[HDIM:]) if head == 0 else (piece[HDIM:], piece[:HDIM])
        sums = ones[:1]
        logsum_ref[0, 0, head : head + 1, :] = highest + jnp.log(sums)
        pieces.append(mine * (1.0 / sums))
    context_ref[0] = jnp.concatenate(pieces, axis=0).T.astype(LOW)


def attend_back_kernel(
    q_ref, k_ref, v_ref, g_ref, c_ref, logsum_ref, row_ref, col_ref, dq_ref, dk_ref, dv_ref, *, scaling
):
    keys_all = k_ref[0]
    values = v_ref[0]
    turned = [half.T for half in halves(keys_all)]
    key_ids = col_ref[0]
    length = q_ref.shape[1]
    key_grad = jnp.zeros((length, PAIR), WIDE)
    value_grad = jnp.zeros((length, PAIR), WIDE)
    for start in range(0, length, BLOCK):
        part = slice(start, start + BLOCK)
        seen = key_ids == row_ref[0, :, part]
        total = None
        queries_of = halves(q_ref[0, part, :] * scaling)
        grads_of = halves(g_ref[0, part, :])
        products = g_ref[0, part, :].astype(WIDE).T * c_ref[0, part, :].astype(WIDE).T
        for head in range(2):
            queries, grads = queries_of[head], grads_of[head]
            level = jnp.sum(products[head * HDIM : (head + 1) * HDIM], axis=0, keepdims=True)
            scores = jnp.where(seen, dot(keys_all, queries, BY_LAST), MASKED)
            probs = jnp.exp(scores - logsum_ref[0, 0, head : head + 1, part])
            grad_probs = dot(values, grads, BY_LAST)
            value_grad = value_grad + dot(probs.astype(LOW), grads, BY_ROWS)
            grad_scores = (probs * (grad_probs - level)).astype(LOW)
            key_grad = key_grad + dot(grad_scores, queries, BY_ROWS)
            piece = dot(turned[head], grad_scores, BY_ROWS)
            total = piece if total is None else total + piece
        dq_ref[0, part, :] = (total.T * HDIM ** (-0.5)).astype(LOW)
    dk_ref[0] = key_grad.astype(LOW)
    dv_ref[0] = value_grad.astype(LOW)


def attention_specs(length, first=0):
    return (
        pl.BlockSpec((1, length, PAIR), lambda s, p: (s, 0, p + first)),
        pl.BlockSpec((1, 1, length), lambda s, p: (s, 0, 0)),
        pl.BlockSpec((1, length, 1), lambda s, p: (s, 0, 0)),
        pl.BlockSpec((1, 1, 2, length), lambda s, p: (s, p + first, 0, 0)),
    )


def attend(queries, keys_all, values, ids):
    count, length, width = queries.shape
    rows, as_row, as_col, sums = attention_specs(length)
    scaling = HDIM ** (-0.5)
    return pl.pallas_call(
        functools.partial(attend_kernel, scaling=scaling),
        grid=(count, width // PAIR),
        in_specs=[rows, rows, rows, as_row, as_col],
        out_specs=[rows, sums],
        out_shape=[
            jax.ShapeDtypeStruct(queries.shape, LOW),
            jax.ShapeDtypeStruct((count, width // PAIR, 2, length), WIDE),
        ],
        cost_estimate=pl.CostEstimate(
            flops=28 * count * width * length * length,
            transcendentals=count * width * length * length // HDIM,
            bytes_accessed=8 * count * width * length,
        ),
        name="attend",
    )(queries, keys_all, values, *ids)


def attend_back(queries, keys_all, values, grad_context, context, logsum, ids, earlier, part):
    count, length, width = queries.shape
    pairs = width // PAIR
    first = pairs // 2 * part
    rows, as_row, as_col, sums = attention_specs(length, first)
    body = functools.partial(attend_back_kernel, scaling=HDIM ** (-0.5))
    operands = [queries, keys_all, values, grad_context, context, logsum, *ids]
    in_specs = [rows] * 5 + [sums, as_row, as_col]
    aliases = {}
    if earlier is not None:

        def body(*refs):
            attend_back_kernel(*refs[:8], *refs[11:], scaling=HDIM ** (-0.5))

        aliases = {8 + i: i for i in range(3)}
        operands += list(earlier)
        in_specs += [pl.BlockSpec(memory_space=pl.ANY)] * 3
    return pl.pallas_call(
        body,
        grid=(count, (pairs - first) if part else pairs // 2),
        in_specs=in_specs,
        out_specs=[rows, rows, rows],
        out_shape=[jax.ShapeDtypeStruct(queries.shape, LOW)] * 3,
        input_output_aliases=aliases,
        cost_estimate=pl.CostEstimate(
            flops=24 * count * width * length * length,
            transcendentals=count * width * length * length // HDIM // 2,
            bytes_accessed=7 * count * width * length,
        ),
        name="attend_back",
    )(*operands)


def meet(value, parts, picks):
    picked = [step for step in picks if step < len(parts)]
    value, held = lax.optimization_barrier((value, [parts[step] for step in picked]))
    parts = list(parts)
    for step, part in zip(picked, held):
        parts[step] = part
    return value, parts


def spread(block):
    members = lax.axis_size("tp")
    rank_pairs = [[(i, (i + step) % members) for i in range(members)] for step in range(1, members)]
    return [block] + [lax.ppermute(block, "tp", pairs) for pairs in rank_pairs]


def dealt(blocks):
    members, rank = lax.axis_size("tp"), lax.axis_index("tp")
    parts = []
    for step in range(members):
        block = lax.dynamic_slice_in_dim(blocks, (rank + step) % members, 1, 0)[0]
        pairs = [(i, (i + step) % members) for i in range(members)]
        parts.append(lax.ppermute(block, "tp", pairs) if step else block)
    return parts


def sent_back(parts, steps=None):
    members = lax.axis_size("tp")
    moved = list(parts)
    for step in range(1, members) if steps is None else steps:
        pairs = [(i, (i - step) % members) for i in range(members)]
        moved[step] = lax.ppermute(parts[step], "tp", pairs)
    return moved


def by_source(moved):
    members, rank = len(moved), lax.axis_index("tp")
    shape = (members,) + moved[0].shape
    above = (lax.broadcasted_iota(jnp.int32, shape, 0) - rank) % members
    result = jnp.broadcast_to(moved[0][None], shape)
    for step in range(1, members):
        result = jnp.where(above == step, moved[step][None], result)
    return result


def flip(axis, members, bit, block):
    return lax.ppermute(block, axis, [(i, i ^ bit) for i in range(members)])


def beside(bit, block, other, place):
    mine = lax.axis_index("fsdp") // bit % 2
    shape = block.shape[:place] + (2,) + block.shape[place:]
    spot = lax.broadcasted_iota(jnp.int32, shape, place)
    return jnp.where(spot == mine, jnp.expand_dims(block, place), jnp.expand_dims(other, place))


def entries(bit, array, place):
    mine = lax.axis_index("fsdp") // bit % 2
    return [
        lax.squeeze(lax.dynamic_slice_in_dim(array, spot, 1, place), (place,)) for spot in (mine, 1 - mine)
    ]


def together(*groups):
    return lax.optimization_barrier(tuple(list(group) for group in groups))


def gather_rows(members, block, before, beyond, fillers):
    if members != 8:
        return lax.all_gather(block, "fsdp", axis=0, tiled=True), before, beyond, fillers
    rows, cols = block.shape
    first, second = block[:, : cols // 2], block[:, cols // 2 :]
    near = (flip("fsdp", members, 2, first), flip("fsdp", members, 4, second))
    near, beyond, fillers = together(near, beyond, fillers)
    first, second = beside(2, first, near[0], 0), beside(4, second, near[1], 0)
    far = (flip("fsdp", members, 4, first), flip("fsdp", members, 2, second))
    far, before[:3] = together(far, before[:3])
    both = jnp.concatenate([beside(4, first, far[0], 0), beside(2, second, far[1], 1)], axis=3)
    (other,), before[3:] = together((flip("fsdp", members, 1, both),), before[3:])
    return beside(1, both, other, 2).reshape(members * rows, cols), before, beyond, fillers


def add_low(kept, moved):
    return (kept.astype(WIDE) + moved.astype(WIDE)).astype(LOW)


def scatter_core(grad, others=()):
    if lax.axis_size("fsdp") != 8:
        return lax.psum_scatter(grad, "fsdp", scatter_dimension=0, tiled=True), others
    total_rows, cols = grad.shape
    kept, theirs = entries(1, grad.reshape(2, 2, 2, total_rows // 8, cols), 2)
    (moved,), others = together((flip("fsdp", 8, 1, theirs),), others)
    return add_low(kept, moved), others


def scatter_near(grad, others=()):
    if lax.axis_size("fsdp") != 8:
        return grad, others
    half = grad.shape[-1] // 2
    first, first_out = entries(4, grad[..., :half], 0)
    second, second_out = entries(2, grad[..., half:], 1)
    moved = (flip("fsdp", 8, 4, first_out), flip("fsdp", 8, 2, second_out))
    moved, others = together(moved, others)
    return (add_low(first, moved[0]), add_low(second, moved[1])), others


def scatter_far(grad, others=()):
    if lax.axis_size("fsdp") != 8:
        return grad, others
    first, first_out = entries(2, grad[0], 0)
    second, second_out = entries(4, grad[1], 0)
    moved = (flip("fsdp", 8, 2, first_out), flip("fsdp", 8, 4, second_out))
    moved, others = together(moved, others)
    return jnp.concatenate([add_low(first, moved[0]), add_low(second, moved[1])], axis=1), others


def total_over_fsdp(vector):
    members, bit = lax.axis_size("fsdp"), 1
    while bit < members:
        vector = vector + flip("fsdp", members, bit, vector)
        bit *= 2
    return vector


def normalize(token_rows):
    centred = token_rows - jnp.mean(token_rows, axis=-1, keepdims=True)
    scaling = lax.rsqrt(jnp.mean(centred * centred, axis=-1, keepdims=True) + EPSILON)
    return centred * scaling, scaling


def normalize_back(grad_rows, normed, scaling, gain_row):
    grad_normed = grad_rows * gain_row
    adjusted = grad_normed - jnp.mean(grad_normed, axis=-1, keepdims=True)
    adjusted = adjusted - normed * jnp.mean(grad_normed * normed, axis=-1, keepdims=True)
    return scaling * adjusted, jnp.sum(grad_rows * normed, axis=0), jnp.sum(grad_rows, axis=0)


def on_device(
    fsdp,
    tp,
    tokens,
    segment_ids,
    live_mask,
    query_weight,
    query_bias,
    key_weight,
    value_weight,
    value_bias,
    output_weight,
    output_bias,
    first_gain,
    first_shift,
    inner_weight,
    inner_bias,
    outer_weight,
    outer_bias,
    second_gain,
    second_shift,
    out_grad,
):
    sequences, places, width = tokens.shape
    count = sequences // tp
    length = places * tp
    rank = lax.axis_index("tp")
    head_cols = query_weight.shape[1]
    unit_cols = inner_weight.shape[1]
    shard_rows = query_weight.shape[0]

    def whole_rows(parts):
        return jnp.concatenate(parts, axis=1).reshape(count * length, width)

    def by_member(array):
        return array.reshape(tp, count, places, width)

    def by_arrival(array):
        parts = array.reshape(count, tp, places, width)
        return [parts[:, step] for step in range(tp)]

    def own_places(parts):
        return by_source(parts).reshape(sequences, places, width)

    def columns(parts, widths):
        pieces, first = [], 0
        for cols in widths:
            pieces += [part[:shard_rows, first : first + cols] for part in parts]
            first += cols
        return jnp.concatenate(pieces, axis=1)

    def own_columns(share, widths, shared=None):
        parts = []
        for step in range(tp):
            pieces, first = [], 0
            for cols in widths:
                pieces.append(share[:, first + step * cols : first + (step + 1) * cols])
                first += tp * cols
            part = jnp.concatenate(pieces, axis=1)
            parts.append(part if shared is None else jnp.concatenate([part, shared], axis=0))
        return sent_back(parts)

    def summed(parts, widths):
        total, first, pieces = sum(part.astype(WIDE) for part in parts), 0, []
        for cols in widths:
            pieces.append(total[:, first : first + cols])
            first += cols
        return pieces

    def by_rank(vector):
        parts = vector.reshape(tp, -1)
        parts = [lax.dynamic_slice_in_dim(parts, (rank - spot) % tp, 1, 0) for spot in range(tp)]
        return jnp.concatenate(parts, axis=0).reshape(-1)

    biases = jnp.concatenate([query_bias, value_bias, inner_bias]).reshape(-1, 4 * head_cols // 2)
    biases = jnp.pad(biases, ((0, 0), (0, 4 * head_cols - biases.shape[1])))
    heads = jnp.concatenate([query_weight, key_weight, value_weight, output_weight.T], axis=1)
    heads = spread(jnp.concatenate([heads, biases], axis=0))
    rest = jnp.concatenate([inner_weight, outer_weight.T], axis=1)
    rest, heads = meet(rest, heads, (1, 2, 3))
    rest = spread(rest)
    tokens, rest = meet(tokens, rest, (1,))
    rows = dealt(by_member(tokens))
    biases = [part[shard_rows:, : 2 * head_cols].reshape(-1).astype(WIDE) for part in heads]
    query_bias_full = jnp.concatenate([part[:head_cols] for part in biases])
    value_bias_full = jnp.concatenate([part[head_cols : 2 * head_cols] for part in biases])
    inner_bias_full = jnp.concatenate([part[2 * head_cols :] for part in biases])
    first = rank * count
    segment = lax.dynamic_slice_in_dim(segment_ids, first, count, 0)
    live = lax.dynamic_slice_in_dim(live_mask, first, count, 0)
    spots = lax.broadcasted_iota(jnp.int32, segment.shape, 1)
    ids = jnp.where(live == 1, segment, length + spots).reshape(count, tp, places)
    ids = [lax.dynamic_slice_in_dim(ids, (rank - step) % tp, 1, 1) for step in range(tp)]
    ids = jnp.concatenate(ids, axis=1).reshape(count, length)
    ids = (ids[:, None, :], ids[:, :, None])
    fillers = (
        *ids,
        *(vector.astype(WIDE) for vector in (output_bias, first_gain, first_shift)),
        *(vector.astype(WIDE) for vector in (outer_bias, second_gain, second_shift)),
        *(query_bias_full, value_bias_full, inner_bias_full),
    )
    heads, rows, rest, fillers = gather_rows(
        fsdp, columns(heads, (head_cols,) * 4), rows, rest, fillers
    )
    ids = fillers[:2]
    output_bias, first_gain, first_shift, outer_bias, second_gain, second_shift = fillers[2:8]
    query_bias_full, value_bias_full, inner_bias_full = fillers[8:]
    query_full, key_full, value_full, output_turned = (
        heads[:, i * width : (i + 1) * width] for i in range(4)
    )
    rows = whole_rows(rows)
    rows, out_grad = lax.optimization_barrier((rows, out_grad))
    rest = lax.all_gather(columns(rest, (unit_cols, unit_cols)), "fsdp", axis=0, tiled=True)
    inner_full, outer_turned = rest[:, : tp * unit_cols], rest[:, tp * unit_cols :]

    shape = (count, length, width)
    queries = (dot(rows, query_full, BY_ROWS) + query_bias_full).astype(LOW).reshape(shape)
    keys_all = dot(rows, key_full, BY_ROWS).astype(LOW).reshape(shape)
    values = (dot(rows, value_full, BY_ROWS) + value_bias_full).astype(LOW).reshape(shape)
    context, logsum = attend(queries, keys_all, values, ids)
    context, grad_out = meet(context, dealt(by_member(out_grad)), (2,))
    context = context.reshape(count * length, width)
    mixed = dot(context, output_turned, BY_LAST) + output_bias
    first_normed, first_scaling = normalize(rows.astype(WIDE) + mixed)
    first_rows = first_normed * first_gain + first_shift
    first_low = first_rows.astype(LOW)
    preactivation = dot(first_low, inner_full, BY_ROWS) + inner_bias_full
    cumulative = 0.5 * (1.0 + lax.erf(preactivation * 0.7071067811865476))
    activation_rows = (preactivation * cumulative).astype(LOW)
    density = jnp.exp(-0.5 * preactivation * preactivation) * 0.3989422804014327
    slope = cumulative + preactivation * density
    activation_rows, grad_out = meet(activation_rows, grad_out, (1, 3))
    branch = dot(activation_rows, outer_turned, BY_LAST)
    second_normed, second_scaling = normalize(first_rows + branch + outer_bias)
    second_rows = second_normed * second_gain + second_shift
    layer_out = by_arrival(second_rows.astype(LOW))

    grad_out = whole_rows(grad_out).astype(WIDE)
    grad_second, second_gain_grad, second_shift_grad = normalize_back(
        grad_out, second_normed, second_scaling, second_gain
    )
    outer_bias_grad = jnp.sum(grad_second, axis=0)
    grad_branch = grad_second.astype(LOW)
    outer_grad = dot(grad_branch, activation_rows, BY_FIRST).astype(LOW)
    outer_share = lax.psum_scatter(outer_grad, "fsdp", scatter_dimension=0, tiled=True)
    grad_activ = dot(grad_branch, outer_turned, BY_ROWS)
    grad_pre = (grad_activ * slope).astype(LOW)
    inner_bias_grad = jnp.sum(grad_pre.astype(WIDE), axis=0)
    layer_out = sent_back(layer_out, range(2, 3))
    inner_share, layer_out[2:3] = scatter_core(
        dot(first_low, grad_pre, BY_FIRST).astype(LOW), layer_out[2:3]
    )
    inner_share, layer_out = lax.optimization_barrier((inner_share, layer_out))
    layer_out = sent_back(layer_out, [step for step in range(1, tp) if step != 2])
    grad_first = grad_second + dot(grad_pre, inner_full, BY_LAST)
    grad_mixed, first_gain_grad, first_shift_grad = normalize_back(
        grad_first, first_normed, first_scaling, first_gain
    )
    output_bias_grad = jnp.sum(grad_mixed, axis=0)
    grad_mixed_low = grad_mixed.astype(LOW)
    output_grad = dot(grad_mixed_low, context, BY_FIRST).astype(LOW)
    grad_context = dot(grad_mixed_low, output_turned, BY_ROWS).astype(LOW).reshape(shape)
    vectors = [
        output_bias_grad,
        first_gain_grad,
        first_shift_grad,
        outer_bias_grad,
        second_gain_grad,
        second_shift_grad,
        *jnp.split(by_rank(inner_bias_grad), inner_bias_grad.shape[0] // width),
    ]
    inner_share, _ = scatter_near(inner_share)
    grad_context, inner_share, output_grad, vectors = lax.optimization_barrier(
        (grad_context, inner_share, output_grad, vectors)
    )
    inner_share, _ = scatter_far(inner_share)
    back = functools.partial(
        attend_back, queries, keys_all, values, grad_context, context.reshape(shape), logsum, ids
    )
    value_bias_grad = jnp.sum(grad_context.astype(WIDE), axis=(0, 1))
    halfway = back(None, 0)
    halfway, inner_share, outer_share, layer_out = lax.optimization_barrier(
        (halfway, inner_share, outer_share, layer_out)
    )
    layer_out = own_places(layer_out)
    units = (unit_cols, unit_cols)
    unit_parts = own_columns(jnp.concatenate([inner_share, outer_share], axis=1), units)
    rows_grads, unit_parts = lax.optimization_barrier((back(halfway, 1), unit_parts))
    inner_share, outer_share = summed(unit_parts, units)
    query_rows_grad, key_rows_grad, value_rows_grad = (
        array.reshape(count * length, width) for array in rows_grads
    )
    head_grads = [
        dot(rows, grad, BY_FIRST).astype(LOW)
        for grad in (query_rows_grad, key_rows_grad, value_rows_grad)
    ]
    tokens_grad = (
        grad_mixed
        + dot(query_rows_grad, query_full, BY_LAST)
        + dot(key_rows_grad, key_full, BY_LAST)
        + dot(value_rows_grad, value_full, BY_LAST)
    ).astype(LOW)
    late = [jnp.sum(query_rows_grad.astype(WIDE), axis=0), value_bias_grad]
    late = jnp.stack(late + vectors)
    heads_share, (tokens_grad, late) = scatter_core(
        jnp.concatenate(head_grads + [output_grad], axis=1), (tokens_grad, late)
    )
    late = total_over_fsdp(late)
    tokens_grad = sent_back(by_arrival(tokens_grad), range(2, 3))
    heads_share, tokens_grad[2:3] = scatter_near(heads_share, tokens_grad[2:3])
    heads_share, tokens_grad = lax.optimization_barrier((heads_share, tokens_grad))
    tokens_grad = sent_back(tokens_grad, [step for step in range(1, tp) if step != 2])
    heads_share, tokens_grad = scatter_far(heads_share, tokens_grad)
    heads_share, late = lax.optimization_barrier((heads_share, late))
    high = late.astype(LOW)
    lower = (late - high.astype(WIDE)).astype(LOW)
    heads_parts = own_columns(
        jnp.concatenate(
            [heads_share, jnp.stack([high[0], lower[0], high[1], lower[1]]).reshape(1, -1)], axis=0
        ),
        (head_cols,) * 4,
        jnp.concatenate([high[2:], lower[2:]], axis=0),
    )
    totals = by_source([part[shard_rows + 1 :] for part in heads_parts]).astype(WIDE)
    totals = totals[:, : len(vectors)] + totals[:, len(vectors) :]
    totals = jnp.sum(totals, axis=0).reshape(-1)
    heads_share = summed([part[: shard_rows + 1] for part in heads_parts], (head_cols,) * 4)
    query_bias_total = heads_share[0][shard_rows] + heads_share[1][shard_rows]
    value_bias_total = heads_share[2][shard_rows] + heads_share[3][shard_rows]
    query_share, key_share, value_share, output_share = (
        share[:shard_rows] for share in heads_share
    )
    tokens_grad = own_places(tokens_grad).astype(WIDE)
    rowwise = [totals[i * width : (i + 1) * width] for i in range(6)]
    inner_bias_total = lax.dynamic_slice_in_dim(totals, 6 * width + rank * unit_cols, unit_cols)
    return (
        layer_out,
        tokens_grad,
        query_share,
        query_bias_total,
        key_share,
        value_share,
        value_bias_total,
        output_share.T,
        rowwise[0],
        rowwise[1],
        rowwise[2],
        inner_share,
        inner_bias_total,
        outer_share.T,
        rowwise[3],
        rowwise[4],
        rowwise[5],
    )


def solution(mesh):
    split = P("fsdp", "tp", None)
    across, turned = P("fsdp", "tp"), P("tp", "fsdp")
    seqs, units, copied = P("fsdp", None), P("tp"), P()
    return jax.shard_map(
        functools.partial(on_device, mesh.shape["fsdp"], mesh.shape["tp"]),
        mesh=mesh,
        in_specs=(
            split,
            seqs,
            seqs,
            across,
            units,
            across,
            across,
            units,
            turned,
            copied,
            copied,
            copied,
            across,
            units,
            turned,
            copied,
            copied,
            copied,
            split,
        ),
        out_specs=(
            split,
            split,
            across,
            units,
            across,
            across,
            units,
            turned,
            copied,
            copied,
            copied,
            across,
            units,
            turned,
            copied,
            copied,
            copied,
        ),
        check_vma=False,
    )
```
